32 devices in a mesh: ctx: 4 (over x, core), fsdp: 8 (over z, y).
Axes of the slice: x: 2, y: 2, z: 4, core: 2. Of those that a mesh axis runs over, the one named last changes fastest.
Arguments:
- inputs: bfloat16 [2, 8, 2048, 768], P(None, 'fsdp', 'ctx'), may hold values from -6 to 6
- segments: int32 [2, 8, 2048], P(None, 'fsdp'), may hold values from 0 to 31, never falling along the last dimension, each value on 1 to 1024 neighbouring positions
- block_reach: int32 [2, 8], P(None, 'fsdp'), may hold values from 1 to 16
- query_weight: bfloat16 [768, 768], P(('ctx', 'fsdp')), may hold values from -0.21875 to 0.21875
- query_bias: bfloat16 [768], P(('ctx', 'fsdp')), may hold values from -3 to 3
- key_weight: bfloat16 [768, 768], P(('ctx', 'fsdp')), may hold values from -0.21875 to 0.21875
- value_weight: bfloat16 [768, 768], P(('ctx', 'fsdp')), may hold values from -0.21875 to 0.21875
- value_bias: bfloat16 [768], P(('ctx', 'fsdp')), may hold values from -3 to 3
- output_weight: bfloat16 [768, 768], P(('ctx', 'fsdp')), may hold values from -0.875 to 0.875
- output_bias: bfloat16 [768], P(('ctx', 'fsdp')), may hold values from -3 to 3
- first_gain: bfloat16 [768], P(('ctx', 'fsdp')), may hold values from 0.099609375 to 1.8984375
- first_shift: bfloat16 [768], P(('ctx', 'fsdp')), may hold values from -3 to 3
- expand_weight: bfloat16 [768, 3072], P(('ctx', 'fsdp')), may hold values from -0.21875 to 0.21875
- expand_bias: bfloat16 [3072], P(('ctx', 'fsdp')), may hold values from -3 to 3
- contract_weight: bfloat16 [3072, 768], P(('ctx', 'fsdp')), may hold values from -0.109375 to 0.109375
- contract_bias: bfloat16 [768], P(('ctx', 'fsdp')), may hold values from -3 to 3
- second_gain: bfloat16 [768], P(('ctx', 'fsdp')), may hold values from 0.099609375 to 1.8984375
- second_shift: bfloat16 [768], P(('ctx', 'fsdp')), may hold values from -3 to 3
- output_grad: bfloat16 [2, 8, 2048, 768], P(None, 'fsdp', 'ctx'), may hold values from -6 to 6
Outputs:
- layer_output: bfloat16 [2, 8, 2048, 768], P(None, 'fsdp', 'ctx')
- input_grad: float32 [2, 8, 2048, 768], P(None, 'fsdp', 'ctx')
- query_weight_grad: float32 [768, 768], P(('ctx', 'fsdp'))
- query_bias_grad: float32 [768], P(('ctx', 'fsdp'))
- key_weight_grad: float32 [768, 768], P(('ctx', 'fsdp'))
- value_weight_grad: float32 [768, 768], P(('ctx', 'fsdp'))
- value_bias_grad: float32 [768], P(('ctx', 'fsdp'))
- output_weight_grad: float32 [768, 768], P(('ctx', 'fsdp'))
- output_bias_grad: float32 [768], P(('ctx', 'fsdp'))
- first_gain_grad: float32 [768], P(('ctx', 'fsdp'))
- first_shift_grad: float32 [768], P(('ctx', 'fsdp'))
- expand_weight_grad: float32 [768, 3072], P(('ctx', 'fsdp'))
- expand_bias_grad: float32 [3072], P(('ctx', 'fsdp'))
- contract_weight_grad: float32 [3072, 768], P(('ctx', 'fsdp'))
- contract_bias_grad: float32 [768], P(('ctx', 'fsdp'))
- second_gain_grad: float32 [768], P(('ctx', 'fsdp'))
- second_shift_grad: float32 [768], P(('ctx', 'fsdp'))
The draws below stay inside these ranges and needn't reach their ends.
Inputs may be any that keep to these rules, and one draw needn't show every extreme that they name: `segments`: each sequence's tokens form consecutive documents whose numbers never fall, the longest of 1024 tokens.
All inputs are finite; a program needn't handle non-finite values.
Results may differ from the reference program's by a relative error of at most 0.014.
The reference program's roundings to bfloat16 on the way count: a program that leaves them out, or rounds other values in their place, can miss the bound.
Values may be sent and summed in bfloat16 or wider, within the bound.
A program may use at most 384 MiB of HBM per device.

```python
import math
import jax
import jax.numpy as jnp
import numpy as np
from jax import lax

D = 768
HEADS = 12
HEAD_DIM = 64
FF = 3072
MICRO = 2
KEY_BLOCK = 128
SEQ_LEN = 2048
SEQS = 8


def place_ends(values, own_key, smallest, top_value):
    index_at = [jax.random.randint(jax.random.fold_in(own_key, axis), (), 0, length) for axis, length in enumerate(values.shape)]
    widest = values.shape.index(max(values.shape))
    beside = index_at[:widest] + [(index_at[widest] + 1) % values.shape[widest]] + index_at[widest + 1:]
    return values.at[tuple(index_at)].set(smallest).at[tuple(beside)].set(top_value)


def with_spikes(values, own_key, source, target, blocks, factor):
    def block_of(dim):
        return (jnp.arange(values.shape[dim]) // (values.shape[dim] // blocks)).reshape((-1,) + (1,) * (values.ndim - 1 - dim))

    first = jax.random.permutation(own_key, blocks)[block_of(target)]
    far = (block_of(target) + blocks // 2) % blocks
    return jnp.where((block_of(source) == first) | (block_of(source) == far), factor * values, values)


def block_scale(own_key, shape, cuts, low, high):
    loudness = 1.0
    for dim, blocks in cuts:
        steps = jax.random.uniform(jax.random.fold_in(jax.random.fold_in(own_key, 6), dim), (blocks,), jnp.float32, low / len(cuts), high / len(cuts))
        loudness = loudness * jnp.repeat(jnp.exp(steps), shape[dim] // blocks).reshape((-1,) + (1,) * (len(shape) - 1 - dim))
    return loudness


def split_up(count, total, limit, skew):
    loads = [(1 << 20) // math.isqrt(standing ** skew) + 1 for standing in range(2, count + 1)]
    rest, given = total - limit - (count - 1), [1] * (count - 1)
    while rest > 0:
        candidates = [i for i in range(count - 1) if given[i] < limit]
        mass, remaining = sum([loads[i] for i in candidates]), rest
        for i in candidates:
            addition = min(limit - given[i], max(1, remaining * loads[i] // mass), rest)
            given[i] = given[i] + addition
            rest = rest - addition
    return np.array([limit] + given)


def uneven(key, count, total, most, skew):
    if count == 2:
        one = jax.random.randint(key, (), max(1, total - most), min(most, total - 1) + 1)
        return jnp.stack([one, total - one])
    tallies = jnp.asarray(split_up(count, total, most, skew), jnp.int32)
    pairs = (count - 1) // 2
    giver, sink = tallies[1:1 + 2 * pairs:2], tallies[2:2 + 2 * pairs:2]
    slack = jnp.minimum(giver - 1, most - sink)
    moved = jax.random.randint(jax.random.fold_in(key, 1), (pairs,), 0, 1 << 20) % (slack + 1)
    tallies = tallies.at[1:1 + 2 * pairs:2].set(giver - moved).at[2:2 + 2 * pairs:2].set(sink + moved)
    return tallies[jax.random.permutation(jax.random.fold_in(key, 2), count)]


def normal_values(rng, shape, scale, limit, pieces=(), held_as=jnp.bfloat16):
    drawn = scale * jax.random.normal(rng, shape, jnp.float32)
    if pieces:
        drawn = drawn * block_scale(rng, shape, pieces, -0.22, 0.18)
    return jnp.clip(drawn, -limit, limit).astype(held_as)


def noise_with(own_key, shape, spread, most, pieces, heavy, kind=jnp.bfloat16):
    array = spread * jax.random.normal(own_key, shape, jnp.float32)
    if pieces:
        array = array * block_scale(own_key, shape, pieces, -0.22, 0.18)
    return jnp.clip(with_spikes(array, jax.random.fold_in(own_key, 3), *heavy), -most, most).astype(kind)


def setup_inputs(seed: int = 0) -> dict:
    splits = jax.random.split(jax.random.key(seed), 20)
    inputs = noise_with(splits[0], (MICRO, SEQS, SEQ_LEN, D), 1.0, 6.0, ((1, 8), (2, 4)), (1, 3, 8, 2.0))
    segments = jax.vmap(lambda own: jnp.searchsorted(jnp.cumsum(uneven(own, max(4, SEQ_LEN // 64), SEQ_LEN, SEQ_LEN // 2, 2)), jnp.arange(SEQ_LEN), side="right"))(jax.random.split(splits[1], MICRO * SEQS)).reshape((MICRO, SEQS, SEQ_LEN)).astype(jnp.int32)
    block_reach = place_ends(jax.random.randint(splits[2], (MICRO, SEQS), 1, SEQ_LEN // KEY_BLOCK + 1), jax.random.fold_in(splits[2], 1), 1, (SEQ_LEN // KEY_BLOCK + 1) - 1).astype(jnp.int32)
    query_weight = normal_values(splits[3], (D, D), D ** -0.5, 0.21875, ((0, 32),))
    query_bias = normal_values(splits[4], (D,), 0.5, 3.0, ((0, 32),))
    key_weight = normal_values(splits[5], (D, D), D ** -0.5, 0.21875, ((0, 32),))
    value_weight = normal_values(splits[6], (D, D), D ** -0.5, 0.21875, ((0, 32),))
    value_bias = normal_values(splits[7], (D,), 0.5, 3.0, ((0, 32),))
    output_weight = normal_values(splits[8], (D, D), (D // 16) ** -0.5, 0.875, ((0, 32),))
    output_bias = normal_values(splits[9], (D,), 0.5, 3.0, ((0, 32),))
    first_gain = jnp.clip(1.0 + 0.18 * jax.random.normal(splits[10], (D,), jnp.float32), 0.099609375, 1.8984375).astype(jnp.bfloat16)
    first_shift = normal_values(splits[11], (D,), 0.5, 3.0, ((0, 32),))
    expand_weight = normal_values(splits[12], (D, FF), D ** -0.5, 0.21875, ((0, 32),))
    expand_bias = normal_values(splits[13], (FF,), 0.5, 3.0, ((0, 32),))
    contract_weight = normal_values(splits[14], (FF, D), FF ** -0.5, 0.109375, ((0, 32),))
    contract_bias = normal_values(splits[15], (D,), 0.5, 3.0, ((0, 32),))
    second_gain = jnp.clip(1.0 + 0.18 * jax.random.normal(splits[16], (D,), jnp.float32), 0.099609375, 1.8984375).astype(jnp.bfloat16)
    second_shift = normal_values(splits[17], (D,), 0.5, 3.0, ((0, 32),))
    output_grad = noise_with(splits[18], (MICRO, SEQS, SEQ_LEN, D), 1.0, 6.0, ((1, 8), (2, 4)), (1, 3, 8, 2.0))
    return {"inputs": inputs, "segments": segments, "block_reach": block_reach, "query_weight": query_weight, "query_bias": query_bias, "key_weight": key_weight, "value_weight": value_weight, "value_bias": value_bias, "output_weight": output_weight, "output_bias": output_bias, "first_gain": first_gain, "first_shift": first_shift, "expand_weight": expand_weight, "expand_bias": expand_bias, "contract_weight": contract_weight, "contract_bias": contract_bias, "second_gain": second_gain, "second_shift": second_shift, "output_grad": output_grad}


@jax.custom_vjp
def low(v):
    return lax.optimization_barrier(v.astype(jnp.bfloat16)).astype(jnp.float32)

@jax.custom_vjp
def low_back(v):
    return v

def low_keep(v):
    return (low(v), None)

def low_pass(kept, grad):
    return (grad,)

def back_keep(v):
    return (v, None)

def back_low(kept, grad):
    return (low(grad),)
low.defvjp(low_keep, low_pass)
low_back.defvjp(back_keep, back_low)

def layer_norm(summed, gain, shift):
    row_mean = lax.optimization_barrier(jnp.mean(summed, axis=-1, keepdims=True))
    centered = summed - row_mean
    variance = lax.optimization_barrier(jnp.mean(centered * centered, axis=-1, keepdims=True))
    return centered * lax.rsqrt(variance + 1e-05) * gain + shift

def product(left, right):
    return jnp.dot(left, right, precision=lax.Precision.HIGHEST)

def forward_seq(tokens, params, seg_row, reach):
    query_weight, query_bias, key_weight, value_weight, value_bias, output_weight, output_bias, first_gain, first_shift, expand_weight, expand_bias, contract_weight, contract_bias, second_gain, second_shift = params
    length = tokens.shape[0]
    queries = low(low_back(product(tokens, query_weight) + query_bias))
    key_rows = low(low_back(product(tokens, key_weight)))
    value_rows = low(low_back(product(tokens, value_weight) + value_bias))
    query_heads = queries.reshape(length, HEADS, HEAD_DIM)
    key_heads = key_rows.reshape(length, HEADS, HEAD_DIM)
    value_heads = value_rows.reshape(length, HEADS, HEAD_DIM)
    scores = jnp.einsum('qhd,khd->hqk', query_heads, key_heads, precision=lax.Precision.HIGHEST) * (1.0 / HEAD_DIM ** 0.5)
    scores = low_back(scores)
    position = jnp.arange(length, dtype=jnp.int32)
    blocks = position // KEY_BLOCK
    key_mask = (seg_row[:, None] == seg_row[None, :]) & (jnp.abs(blocks[:, None] - blocks[None, :]) < reach)
    scores = jnp.where(key_mask[None], scores, -1e+30)
    peak = lax.optimization_barrier(jnp.max(scores, axis=-1, keepdims=True))
    shifted = jnp.exp(scores - peak)
    soft = shifted / lax.optimization_barrier(jnp.sum(shifted, axis=-1, keepdims=True))
    probs = low(soft)
    attended = jnp.einsum('hqk,khd->qhd', probs, value_heads, precision=lax.Precision.HIGHEST).reshape(length, HEADS * HEAD_DIM)
    attended = low(low_back(attended))
    branch = low_back(product(attended, output_weight) + output_bias)
    hidden = layer_norm(tokens + branch, first_gain, first_shift)
    pre = low_back(product(low(hidden), expand_weight) + expand_bias)
    act = low(jax.nn.gelu(pre, approximate=False))
    ffn_branch = low_back(product(act, contract_weight) + contract_bias)
    return layer_norm(hidden + ffn_branch, second_gain, second_shift)

def reference(inputs, segments, block_reach, query_weight, query_bias, key_weight, value_weight, value_bias, output_weight, output_bias, first_gain, first_shift, expand_weight, expand_bias, contract_weight, contract_bias, second_gain, second_shift, output_grad):
    params = tuple((weight.astype(jnp.float32) for weight in (query_weight, query_bias, key_weight, value_weight, value_bias, output_weight, output_bias, first_gain, first_shift, expand_weight, expand_bias, contract_weight, contract_bias, second_gain, second_shift)))
    sequences = inputs.reshape(MICRO * SEQS, SEQ_LEN, D).astype(jnp.float32)
    seg_rows = segments.reshape(MICRO * SEQS, SEQ_LEN).astype(jnp.int32)
    reaches = block_reach.reshape(MICRO * SEQS).astype(jnp.int32)
    cotangents = output_grad.reshape(MICRO * SEQS, SEQ_LEN, D).astype(jnp.float32)
    zeros = tuple((jnp.zeros_like(weight) for weight in params))

    def one_sequence(summed, item):
        tokens, seg_row, reach, cotangent = item
        result, pull = jax.vjp(lambda a, b: forward_seq(a, b, seg_row, reach), tokens, params)
        token_grad, param_grads = pull(cotangent)
        summed = tuple((left + right for left, right in zip(summed, param_grads)))
        return (summed, (result.astype(jnp.bfloat16), token_grad))
    grads, (results, token_grads) = lax.scan(one_sequence, zeros, (sequences, seg_rows, reaches, cotangents))
    return (results.reshape(MICRO, SEQS, SEQ_LEN, D), token_grads.reshape(MICRO, SEQS, SEQ_LEN, D), grads[0], grads[1], grads[2], grads[3], grads[4], grads[5], grads[6], grads[7], grads[8], grads[9], grads[10], grads[11], grads[12], grads[13], grads[14])
```

```python
import functools, math
import jax, jax.numpy as jnp
from jax import lax
from jax.experimental import pallas as pl
from jax.experimental.pallas import tpu as pltpu
from jax.sharding import PartitionSpec as P

HD = 64
KEY_BLOCK = 128
TILE = 256
SEG_COUNT = 32
FAR = 1e30

def mask_rows(seg_row, reach, length, extra):
    blocks = length // KEY_BLOCK
    row = lax.broadcasted_iota(jnp.int32, (HD, length), 0)
    seg = jnp.broadcast_to(seg_row, (HD, length))
    block = lax.broadcasted_iota(jnp.int32, (HD, length), 1) // KEY_BLOCK
    is_seg = row < SEG_COUNT
    is_block = (row >= SEG_COUNT) & (row < SEG_COUNT + blocks)
    key_at = row - SEG_COUNT
    far = is_block & (jnp.abs(key_at - block) >= reach)
    q_side = jnp.where((is_seg & (seg == row)) | far, -FAR, 0.0)
    k_side = jnp.where((is_seg & (seg != row)) | (is_block & (key_at == block)), 1.0, 0.0)
    return q_side, k_side

def fwd_kernel(heads, lo_ref, hi_ref, reach_ref, seg_ref, qkv_ref, att_ref, lse_ref, kaug, qaug, vtr):
    m = pl.program_id(0)
    length = qkv_ref.shape[1]
    width = heads * HD
    q_side, k_side = mask_rows(seg_ref[0], reach_ref[m], length, 0)
    q_side = q_side.astype(jnp.bfloat16)
    k_side = jnp.transpose(k_side).astype(jnp.bfloat16)
    for h in range(heads):
        q = qkv_ref[0, :, h * HD:(h + 1) * HD]
        k = qkv_ref[0, :, width + h * HD:width + (h + 1) * HD]
        v = qkv_ref[0, :, 2 * width + h * HD:2 * width + (h + 1) * HD]
        qaug[h, 0:HD, :] = jnp.transpose(q.astype(jnp.float32) * (1.0 / math.sqrt(HD))).astype(jnp.bfloat16)
        qaug[h, HD:2 * HD, :] = q_side
        kaug[h, :, 0:HD] = k
        kaug[h, :, HD:2 * HD] = k_side
        vtr[h] = jnp.transpose(v)

    def q_step(i, _):
        qs = pl.ds(pl.multiple_of(i * TILE, TILE), TILE)
        def k_step(j, carry):
            ks = pl.ds(pl.multiple_of(j * TILE, TILE), TILE)
            out = []
            for h in range(heads):
                peak, total, acc = carry[h]
                s = jnp.dot(kaug[h, ks, :], qaug[h, :, qs], preferred_element_type=jnp.float32)
                new = jnp.maximum(peak, jnp.max(s, axis=0, keepdims=True))
                p = jnp.exp(s - new)
                fade = jnp.exp(peak - new)
                total = total * fade + jnp.sum(p, axis=0, keepdims=True)
                acc = acc * fade + jnp.dot(vtr[h, :, ks], p.astype(jnp.bfloat16), preferred_element_type=jnp.float32)
                out.append((new, total, acc))
            return tuple(out)
        start = tuple((jnp.full((1, TILE), -3e38, jnp.float32), jnp.zeros((1, TILE), jnp.float32), jnp.zeros((HD, TILE), jnp.float32)) for _ in range(heads))
        done = lax.fori_loop(lo_ref[m, i], hi_ref[m, i], k_step, start)
        for h in range(heads):
            peak, total, acc = done[h]
            att_ref[0, qs, h * HD:(h + 1) * HD] = jnp.transpose(acc / total).astype(jnp.bfloat16)
            lse_ref[0, h:h + 1, qs] = peak + jnp.log(total)
        return 0
    lax.fori_loop(0, length // TILE, q_step, 0)

def bounds(segments, reach):
    first = segments[:, ::TILE]
    last = segments[:, TILE - 1::TILE]
    n = first.shape[1]
    at = jnp.arange(n)
    per = TILE // KEY_BLOCK
    gap = per * jnp.abs(at[:, None] - at[None, :]) - (per - 1)
    near = gap[None] < reach[:, None, None]
    before = (at[None, :] < at[:, None])[None] & near & (first[:, :, None] == last[:, None, :])
    after = (at[None, :] > at[:, None])[None] & near & (last[:, :, None] == first[:, None, :])
    lo = at[None] - jnp.sum(before, axis=2, dtype=jnp.int32)
    hi = at[None] + 1 + jnp.sum(after, axis=2, dtype=jnp.int32)
    return lo.astype(jnp.int32), hi.astype(jnp.int32)

def attend(qkv, segments, lo, hi, reach, heads):
    micro, length, cols = qkv.shape
    width = heads * HD
    return pl.pallas_call(
        functools.partial(fwd_kernel, heads),
        out_shape=(jax.ShapeDtypeStruct((micro, length, width), jnp.bfloat16), jax.ShapeDtypeStruct((micro, 8, length), jnp.float32)),
        grid_spec=pltpu.PrefetchScalarGridSpec(
            num_scalar_prefetch=3, grid=(micro,),
            in_specs=[pl.BlockSpec((1, 1, length), lambda m, *_: (m, 0, 0)), pl.BlockSpec((1, length, cols), lambda m, *_: (m, 0, 0))],
            out_specs=[pl.BlockSpec((1, length, width), lambda m, *_: (m, 0, 0)), pl.BlockSpec((1, 8, length), lambda m, *_: (m, 0, 0))],
            scratch_shapes=[pltpu.VMEM((heads, length, 2 * HD), jnp.bfloat16), pltpu.VMEM((heads, 2 * HD, length), jnp.bfloat16), pltpu.VMEM((heads, HD, length), jnp.bfloat16)]),
        compiler_params=pltpu.CompilerParams(dimension_semantics=("arbitrary",), vmem_limit_bytes=60 << 20),
        name="attend",
    )(lo, hi, reach, segments[:, None, :], qkv)

def bwd_kernel(heads, lo_ref, hi_ref, reach_ref, seg_ref, qkv_ref, att_ref, datt_ref, lse_ref, dqkv_ref,
               kaug, qaug, v_nat, dotr, do_z, q_z, ktr, delta, dqt, dkv):
    m = pl.program_id(0)
    length = qkv_ref.shape[1]
    width = heads * HD
    scale = 1.0 / math.sqrt(HD)
    q_side, k_side = mask_rows(seg_ref[0], reach_ref[m], length, 0)
    q_side = q_side.astype(jnp.bfloat16)
    k_side = jnp.transpose(k_side).astype(jnp.bfloat16)
    for h in range(heads):
        q = (qkv_ref[0, :, h * HD:(h + 1) * HD].astype(jnp.float32) * scale)
        k = qkv_ref[0, :, width + h * HD:width + (h + 1) * HD]
        v = qkv_ref[0, :, 2 * width + h * HD:2 * width + (h + 1) * HD]
        do = datt_ref[0, :, h * HD:(h + 1) * HD]
        o = att_ref[0, :, h * HD:(h + 1) * HD]
        qaug[h, 0:HD, :] = jnp.transpose(q).astype(jnp.bfloat16)
        qaug[h, HD:2 * HD, :] = q_side
        kaug[h, :, 0:HD] = k
        kaug[h, :, HD:2 * HD] = k_side
        ktr[h] = jnp.transpose(k)
        v_nat[h] = v
        do_t = jnp.transpose(do.astype(jnp.float32))
        dotr[h] = do_t.astype(jnp.bfloat16)
        delta[h] = jnp.sum(do_t * jnp.transpose(o.astype(jnp.float32)), axis=0, keepdims=True)
        zero = jnp.zeros((length, HD), jnp.bfloat16)
        do_z[h, :, 0:HD] = do
        do_z[h, :, HD:2 * HD] = zero
        q_z[h, :, 0:HD] = zero
        q_z[h, :, HD:2 * HD] = q.astype(jnp.bfloat16)
    dqt[...] = jnp.zeros_like(dqt)

    def k_step(j, _):
        ks = pl.ds(pl.multiple_of(j * TILE, TILE), TILE)
        dkv[...] = jnp.zeros_like(dkv)
        def q_step(i, _):
            qs = pl.ds(pl.multiple_of(i * TILE, TILE), TILE)
            for h in range(heads):
                s = jnp.dot(kaug[h, ks, :], qaug[h, :, qs], preferred_element_type=jnp.float32)
                p = jnp.exp(s - lse_ref[0, h:h + 1, qs])
                dp = jnp.dot(v_nat[h, ks, :], dotr[h, :, qs], preferred_element_type=jnp.float32)
                ds = (p * (dp - delta[h, :, qs])).astype(jnp.bfloat16)
                dkv[h] += jnp.dot(p.astype(jnp.bfloat16), do_z[h, qs, :], preferred_element_type=jnp.float32) + jnp.dot(ds, q_z[h, qs, :], preferred_element_type=jnp.float32)
                dqt[h, :, qs] += jnp.dot(ktr[h, :, ks], ds, preferred_element_type=jnp.float32)
            return 0
        lax.fori_loop(lo_ref[m, j], hi_ref[m, j], q_step, 0)
        for h in range(heads):
            both = dkv[h]
            dqkv_ref[0, ks, 2 * width + h * HD:2 * width + (h + 1) * HD] = both[:, 0:HD].astype(jnp.bfloat16)
            dqkv_ref[0, ks, width + h * HD:width + (h + 1) * HD] = both[:, HD:2 * HD].astype(jnp.bfloat16)
        return 0
    lax.fori_loop(0, length // TILE, k_step, 0)
    for h in range(heads):
        dqkv_ref[0, :, h * HD:(h + 1) * HD] = jnp.transpose(dqt[h] * scale).astype(jnp.bfloat16)

def attend_back(qkv, att, datt, lse, segments, lo, hi, reach, heads):
    micro, length, cols = qkv.shape
    width = heads * HD
    big = lambda n: pl.BlockSpec((1, length, n), lambda m, *_: (m, 0, 0))
    return pl.pallas_call(
        functools.partial(bwd_kernel, heads),
        out_shape=jax.ShapeDtypeStruct((micro, length, cols), jnp.bfloat16),
        grid_spec=pltpu.PrefetchScalarGridSpec(
            num_scalar_prefetch=3, grid=(micro,),
            in_specs=[pl.BlockSpec((1, 1, length), lambda m, *_: (m, 0, 0)), big(cols), big(width), big(width), pl.BlockSpec((1, 8, length), lambda m, *_: (m, 0, 0))],
            out_specs=big(cols),
            scratch_shapes=[
                pltpu.VMEM((heads, length, 2 * HD), jnp.bfloat16),
                pltpu.VMEM((heads, 2 * HD, length), jnp.bfloat16),
                pltpu.VMEM((heads, length, HD), jnp.bfloat16),
                pltpu.VMEM((heads, HD, length), jnp.bfloat16),
                pltpu.VMEM((heads, length, 2 * HD), jnp.bfloat16),
                pltpu.VMEM((heads, length, 2 * HD), jnp.bfloat16),
                pltpu.VMEM((heads, HD, length), jnp.bfloat16),
                pltpu.VMEM((heads, 1, length), jnp.float32),
                pltpu.VMEM((heads, HD, length), jnp.float32),
                pltpu.VMEM((heads, TILE, 2 * HD), jnp.float32)]),
        compiler_params=pltpu.CompilerParams(dimension_semantics=("arbitrary",), vmem_limit_bytes=60 << 20),
        name="attend_back",
    )(lo, hi, reach, segments[:, None, :], qkv, att, datt, lse)


def layer_norm(summed, gain, shift):
    row_mean = jnp.mean(summed, axis=-1, keepdims=True)
    centered = summed - row_mean
    variance = jnp.mean(centered * centered, axis=-1, keepdims=True)
    recip = lax.rsqrt(variance + 1e-05)
    normed = centered * recip
    return (normed * gain + shift, normed, recip)


def norm_back(upstream, normed, recip, gain):
    scaled = upstream * gain
    first_mean = jnp.mean(scaled, axis=-1, keepdims=True)
    second_mean = jnp.mean(scaled * normed, axis=-1, keepdims=True)
    d_summed = recip * (scaled - first_mean - normed * second_mean)
    return (d_summed, jnp.sum(upstream * normed, axis=0), jnp.sum(upstream, axis=0))


def dot(left, right):
    return jnp.dot(left, right, preferred_element_type=jnp.float32)


def weight_term(left, right):
    return jnp.einsum("ta,tb->ab", left, right, preferred_element_type=jnp.float32)


def back_term(grad_low, weight):
    return jnp.einsum("tb,ab->ta", grad_low, weight, preferred_element_type=jnp.float32)


def column_sum(grad_low):
    return jnp.sum(grad_low.astype(jnp.float32), axis=0)


def exchange(pieces):
    count = lax.axis_size("ctx")
    me = lax.axis_index("ctx")
    got = lax.dynamic_update_index_in_dim(
        jnp.zeros_like(pieces), lax.dynamic_index_in_dim(pieces, me, 0, keepdims=False), me, 0
    )
    for step in range(1, count):
        piece = lax.dynamic_index_in_dim(pieces, (me + step) % count, 0, keepdims=False)
        piece = lax.ppermute(piece, "ctx", [(a, (a + step) % count) for a in range(count)])
        got = lax.dynamic_update_index_in_dim(got, piece, (me - step) % count, 0)
    return got


def body(
    inputs, segments, block_reach,
    query_weight, query_bias, key_weight, value_weight, value_bias, output_weight, output_bias,
    first_gain, first_shift, expand_weight, expand_bias, contract_weight, contract_bias,
    second_gain, second_shift, output_grad,
):
    every = ("ctx", "fsdp")
    ctx = lax.axis_size("ctx")
    me = lax.axis_index("ctx")
    micro, _, rows, width = inputs.shape
    length = rows * ctx
    cols = width // ctx
    heads = cols // HD
    f32, bf16 = jnp.float32, jnp.bfloat16

    small = jnp.concatenate([query_bias, value_bias, output_bias, first_gain, first_shift, contract_bias, second_gain, second_shift, expand_bias])
    share = query_bias.shape[0]
    small_all = lax.all_gather(small[None], every, axis=0, tiled=True)
    vector = lambda n: small_all[:, n * share : (n + 1) * share].reshape(-1).astype(f32)
    b_query, b_value, b_output, g_first, s_first, b_contract, g_second, s_second = [vector(n) for n in range(8)]
    b_expand = small_all[:, 8 * share :].reshape(-1).astype(f32)
    w_qkv = lax.all_gather(jnp.concatenate([query_weight, key_weight, value_weight], axis=1), every, axis=0, tiled=True)
    tokens_all = lax.all_gather(inputs[:, 0], "ctx", axis=1, tiled=True)
    w_output = lax.all_gather(output_weight, every, axis=0, tiled=True)
    w_expand = lax.all_gather(expand_weight, every, axis=0, tiled=True)
    w_contract = lax.all_gather(contract_weight, every, axis=0, tiled=True)

    mine = lambda matrix, n: lax.dynamic_slice_in_dim(matrix, n * width + me * cols, cols, 1)
    w_mine = jnp.concatenate([mine(w_qkv, n) for n in range(3)], axis=1)
    own = lambda vec: lax.dynamic_slice_in_dim(vec, me * cols, cols, 0)
    b_mine = jnp.concatenate([own(b_query), jnp.zeros((cols,), f32), own(b_value)])
    seg = segments[:, 0]
    reach = block_reach[:, 0]
    lo, hi = bounds(seg, reach)

    flat_all = tokens_all.reshape(micro * length, width)
    qkv = (dot(flat_all, w_mine) + b_mine).astype(bf16).reshape(micro, length, 3 * cols)
    att_mine, lse = attend(qkv, seg, lo, hi, reach, heads)
    pieces = att_mine.reshape(micro, ctx, rows, cols)
    attended = [exchange(pieces[m]).transpose(1, 0, 2).reshape(rows, width) for m in range(micro)]
    attended = jnp.concatenate(attended, axis=0)

    tokens = inputs[:, 0].reshape(micro * rows, width)
    branch = dot(attended, w_output) + b_output
    hidden, normed_first, recip_first = layer_norm(tokens.astype(f32) + branch, g_first, s_first)
    hidden_low = hidden.astype(bf16)
    pre = dot(hidden_low, w_expand) + b_expand
    phi = 0.5 * (1.0 + lax.erf(pre * (1.0 / math.sqrt(2.0))))
    act_low = (pre * phi).astype(bf16)
    slope = phi + pre * (jnp.exp(-0.5 * pre * pre) * (1.0 / math.sqrt(2.0 * math.pi)))
    second_sum = hidden + dot(act_low, w_contract) + b_contract
    result, normed_second, recip_second = layer_norm(second_sum, g_second, s_second)
    layer_output = result.astype(bf16)
    upstream = output_grad[:, 0].reshape(micro * rows, width).astype(f32)
    d_res2, grad_g2, grad_s2 = norm_back(upstream, normed_second, recip_second, g_second)
    d_ffn = d_res2.astype(bf16)
    grad_w2 = weight_term(act_low, d_ffn)
    grad_b2 = column_sum(d_ffn)
    d_pre = (back_term(d_ffn, w_contract) * slope).astype(bf16)
    grad_w1 = weight_term(hidden_low, d_pre)
    grad_b1 = column_sum(d_pre)
    d_hidden = d_res2 + back_term(d_pre, w_expand)
    d_res1, grad_g1, grad_s1 = norm_back(d_hidden, normed_first, recip_first, g_first)
    d_branch = d_res1.astype(bf16)
    grad_wo = weight_term(attended, d_branch)
    grad_bo = column_sum(d_branch)
    d_attended = back_term(d_branch, w_output).astype(bf16)

    out_pieces = d_attended.reshape(micro, rows, ctx, cols)
    datt_mine = jnp.stack([exchange(out_pieces[m].transpose(1, 0, 2)).reshape(length, cols) for m in range(micro)])
    d_qkv = attend_back(qkv, att_mine, datt_mine, lse, seg, lo, hi, reach, heads)
    flat_d = d_qkv.reshape(micro * length, 3 * cols)
    grad_qkv = weight_term(flat_all, flat_d)
    grad_b = column_sum(flat_d)
    part = back_term(flat_d, w_mine).astype(bf16).reshape(micro, length, width)
    summed = lax.psum_scatter(part, "ctx", scatter_dimension=1, tiled=True).reshape(micro * rows, width)
    token_grad = d_res1 + summed.astype(f32)

    fold = lambda grad: lax.psum_scatter(grad.astype(bf16), every, scatter_dimension=0, tiled=True).astype(f32)
    spread = lambda n, total: lax.dynamic_update_slice_in_dim(
        jnp.zeros((width, width), total.dtype), total[:, n * cols : (n + 1) * cols], me * cols, 1)
    gq, gk, gv = [fold(spread(n, grad_qkv)) for n in range(3)]
    place = lambda vec: lax.dynamic_update_slice_in_dim(jnp.zeros((width,), f32), vec, me * cols, 0)
    vectors = [place(grad_b[:cols]), place(grad_b[2 * cols :]), grad_bo, grad_g1, grad_s1, grad_b2, grad_g2, grad_s2, grad_b1]
    stacked = jnp.concatenate([v.reshape(-1, share if n < 8 else 4 * share) for n, v in enumerate(vectors)], axis=1)
    summed_small = lax.psum_scatter(stacked, every, scatter_dimension=0, tiled=True)[0]
    piece = lambda n: summed_small[n * share : (n + 1) * share]
    gbq, gbv, gbo, gg1, gs1, gb2, gg2, gs2 = [piece(n) for n in range(8)]
    gb1 = summed_small[8 * share :]
    four = (micro, 1, rows, width)
    return (
        layer_output.reshape(four), token_grad.reshape(four), gq, gbq, gk, gv, gbv, fold(grad_wo), gbo, gg1, gs1,
        fold(grad_w1), gb1, fold(grad_w2), gb2, gg2, gs2,
    )


def solution(mesh):
    rows = P(("ctx", "fsdp"), None)
    flat = P(("ctx", "fsdp"))
    tokens = P(None, "fsdp", "ctx", None)
    params = (rows, flat, rows, rows, flat, rows, flat, flat, flat, rows, flat, rows, flat, flat, flat)
    return jax.shard_map(
        body,
        mesh=mesh,
        in_specs=(tokens, P(None, "fsdp", None), P(None, "fsdp")) + params + (tokens,),
        out_specs=(tokens, tokens) + params,
        check_vma=False,
    )
```

```python
import functools
import math

import jax
import jax.numpy as jnp
from jax import lax
from jax.experimental import pallas as pl
from jax.experimental.pallas import tpu as pltpu
from jax.sharding import PartitionSpec as P

HD = 64
KEY_BLOCK = 128
TILE = 256
SEG_COUNT = 32
FAR = 1e30

def mask_rows(seg_row, reach, length, extra):
    blocks = length // KEY_BLOCK
    row = lax.broadcasted_iota(jnp.int32, (HD, length), 0)
    seg = jnp.broadcast_to(seg_row, (HD, length))
    block = lax.broadcasted_iota(jnp.int32, (HD, length), 1) // KEY_BLOCK
    is_seg = row < SEG_COUNT
    is_block = (row >= SEG_COUNT) & (row < SEG_COUNT + blocks)
    key_at = row - SEG_COUNT
    far = is_block & (jnp.abs(key_at - block) >= reach)
    q_side = jnp.where((is_seg & (seg == row)) | far, -FAR, 0.0)
    k_side = jnp.where((is_seg & (seg != row)) | (is_block & (key_at == block)), 1.0, 0.0)
    return q_side, k_side

def fwd_kernel(heads, lo_ref, hi_ref, reach_ref, seg_ref, qkv_ref, att_ref, lse_ref, kaug, qaug, vtr):
    m = pl.program_id(0)
    length = qkv_ref.shape[1]
    width = heads * HD
    q_side, k_side = mask_rows(seg_ref[0], reach_ref[m], length, 0)
    q_side = q_side.astype(jnp.bfloat16)
    k_side = jnp.transpose(k_side).astype(jnp.bfloat16)
    for h in range(heads):
        q = qkv_ref[0, :, h * HD:(h + 1) * HD]
        k = qkv_ref[0, :, width + h * HD:width + (h + 1) * HD]
        v = qkv_ref[0, :, 2 * width + h * HD:2 * width + (h + 1) * HD]
        qaug[h, 0:HD, :] = jnp.transpose(q.astype(jnp.float32) * (1.0 / math.sqrt(HD))).astype(jnp.bfloat16)
        qaug[h, HD:2 * HD, :] = q_side
        kaug[h, :, 0:HD] = k
        kaug[h, :, HD:2 * HD] = k_side
        vtr[h] = jnp.transpose(v)

    def q_step(i, _):
        qs = pl.ds(pl.multiple_of(i * TILE, TILE), TILE)
        def k_step(j, carry):
            ks = pl.ds(pl.multiple_of(j * TILE, TILE), TILE)
            out = []
            for h in range(heads):
                peak, total, acc = carry[h]
                s = jnp.dot(kaug[h, ks, :], qaug[h, :, qs], preferred_element_type=jnp.float32)
                new = jnp.maximum(peak, jnp.max(s, axis=0, keepdims=True))
                p = jnp.exp(s - new)
                fade = jnp.exp(peak - new)
                total = total * fade + jnp.sum(p, axis=0, keepdims=True)
                acc = acc * fade + jnp.dot(vtr[h, :, ks], p.astype(jnp.bfloat16), preferred_element_type=jnp.float32)
                out.append((new, total, acc))
            return tuple(out)
        start = tuple((jnp.full((1, TILE), -3e38, jnp.float32), jnp.zeros((1, TILE), jnp.float32), jnp.zeros((HD, TILE), jnp.float32)) for _ in range(heads))
        done = lax.fori_loop(lo_ref[m, i], hi_ref[m, i], k_step, start)
        for h in range(heads):
            peak, total, acc = done[h]
            att_ref[0, qs, h * HD:(h + 1) * HD] = jnp.transpose(acc / total).astype(jnp.bfloat16)
            lse_ref[0, h:h + 1, qs] = peak + jnp.log(total)
        return 0
    lax.fori_loop(0, length // TILE, q_step, 0)

def bounds(segments, reach):
    first = segments[:, ::TILE]
    last = segments[:, TILE - 1::TILE]
    n = first.shape[1]
    at = jnp.arange(n)
    per = TILE // KEY_BLOCK
    gap = per * jnp.abs(at[:, None] - at[None, :]) - (per - 1)
    near = gap[None] < reach[:, None, None]
    before = (at[None, :] < at[:, None])[None] & near & (first[:, :, None] == last[:, None, :])
    after = (at[None, :] > at[:, None])[None] & near & (last[:, :, None] == first[:, None, :])
    lo = at[None] - jnp.sum(before, axis=2, dtype=jnp.int32)
    hi = at[None] + 1 + jnp.sum(after, axis=2, dtype=jnp.int32)
    return lo.astype(jnp.int32), hi.astype(jnp.int32)

def attend(qkv, segments, lo, hi, reach, heads):
    micro, length, cols = qkv.shape
    width = heads * HD
    return pl.pallas_call(
        functools.partial(fwd_kernel, heads),
        out_shape=(jax.ShapeDtypeStruct((micro, length, width), jnp.bfloat16), jax.ShapeDtypeStruct((micro, 8, length), jnp.float32)),
        grid_spec=pltpu.PrefetchScalarGridSpec(
            num_scalar_prefetch=3, grid=(micro,),
            in_specs=[pl.BlockSpec((1, 1, length), lambda m, *_: (m, 0, 0)), pl.BlockSpec((1, length, cols), lambda m, *_: (m, 0, 0))],
            out_specs=[pl.BlockSpec((1, length, width), lambda m, *_: (m, 0, 0)), pl.BlockSpec((1, 8, length), lambda m, *_: (m, 0, 0))],
            scratch_shapes=[pltpu.VMEM((heads, length, 2 * HD), jnp.bfloat16), pltpu.VMEM((heads, 2 * HD, length), jnp.bfloat16), pltpu.VMEM((heads, HD, length), jnp.bfloat16)]),
        compiler_params=pltpu.CompilerParams(dimension_semantics=("arbitrary",), vmem_limit_bytes=60 << 20),
        name="attend",
    )(lo, hi, reach, segments[:, None, :], qkv)

def bwd_kernel(heads, lo_ref, hi_ref, reach_ref, seg_ref, qkv_ref, att_ref, datt_ref, lse_ref, dqkv_ref,
               kaug, qaug, v_nat, dotr, do_z, q_z, ktr, delta, dqt, dkv):
    m = pl.program_id(0)
    length = qkv_ref.shape[1]
    width = heads * HD
    scale = 1.0 / math.sqrt(HD)
    q_side, k_side = mask_rows(seg_ref[0], reach_ref[m], length, 0)
    q_side = q_side.astype(jnp.bfloat16)
    k_side = jnp.transpose(k_side).astype(jnp.bfloat16)
    for h in range(heads):
        q = (qkv_ref[0, :, h * HD:(h + 1) * HD].astype(jnp.float32) * scale)
        k = qkv_ref[0, :, width + h * HD:width + (h + 1) * HD]
        v = qkv_ref[0, :, 2 * width + h * HD:2 * width + (h + 1) * HD]
        do = datt_ref[0, :, h * HD:(h + 1) * HD]
        o = att_ref[0, :, h * HD:(h + 1) * HD]
        qaug[h, 0:HD, :] = jnp.transpose(q).astype(jnp.bfloat16)
        qaug[h, HD:2 * HD, :] = q_side
        kaug[h, :, 0:HD] = k
        kaug[h, :, HD:2 * HD] = k_side
        ktr[h] = jnp.transpose(k)
        v_nat[h] = v
        do_t = jnp.transpose(do.astype(jnp.float32))
        dotr[h] = do_t.astype(jnp.bfloat16)
        delta[h] = jnp.sum(do_t * jnp.transpose(o.astype(jnp.float32)), axis=0, keepdims=True)
        zero = jnp.zeros((length, HD), jnp.bfloat16)
        do_z[h, :, 0:HD] = do
        do_z[h, :, HD:2 * HD] = zero
        q_z[h, :, 0:HD] = zero
        q_z[h, :, HD:2 * HD] = q.astype(jnp.bfloat16)
    dqt[...] = jnp.zeros_like(dqt)

    def k_step(j, _):
        ks = pl.ds(pl.multiple_of(j * TILE, TILE), TILE)
        dkv[...] = jnp.zeros_like(dkv)
        def q_step(i, _):
            qs = pl.ds(pl.multiple_of(i * TILE, TILE), TILE)
            for h in range(heads):
                s = jnp.dot(kaug[h, ks, :], qaug[h, :, qs], preferred_element_type=jnp.float32)
                p = jnp.exp(s - lse_ref[0, h:h + 1, qs])
                dp = jnp.dot(v_nat[h, ks, :], dotr[h, :, qs], preferred_element_type=jnp.float32)
                ds = (p * (dp - delta[h, :, qs])).astype(jnp.bfloat16)
                dkv[h] += jnp.dot(p.astype(jnp.bfloat16), do_z[h, qs, :], preferred_element_type=jnp.float32) + jnp.dot(ds, q_z[h, qs, :], preferred_element_type=jnp.float32)
                dqt[h, :, qs] += jnp.dot(ktr[h, :, ks], ds, preferred_element_type=jnp.float32)
            return 0
        lax.fori_loop(lo_ref[m, j], hi_ref[m, j], q_step, 0)
        for h in range(heads):
            both = dkv[h]
            dqkv_ref[0, ks, 2 * width + h * HD:2 * width + (h + 1) * HD] = both[:, 0:HD].astype(jnp.bfloat16)
            dqkv_ref[0, ks, width + h * HD:width + (h + 1) * HD] = both[:, HD:2 * HD].astype(jnp.bfloat16)
        return 0
    lax.fori_loop(0, length // TILE, k_step, 0)
    for h in range(heads):
        dqkv_ref[0, :, h * HD:(h + 1) * HD] = jnp.transpose(dqt[h] * scale).astype(jnp.bfloat16)

def attend_back(qkv, att, datt, lse, segments, lo, hi, reach, heads):
    micro, length, cols = qkv.shape
    width = heads * HD
    big = lambda n: pl.BlockSpec((1, length, n), lambda m, *_: (m, 0, 0))
    return pl.pallas_call(
        functools.partial(bwd_kernel, heads),
        out_shape=jax.ShapeDtypeStruct((micro, length, cols), jnp.bfloat16),
        grid_spec=pltpu.PrefetchScalarGridSpec(
            num_scalar_prefetch=3, grid=(micro,),
            in_specs=[pl.BlockSpec((1, 1, length), lambda m, *_: (m, 0, 0)), big(cols), big(width), big(width), pl.BlockSpec((1, 8, length), lambda m, *_: (m, 0, 0))],
            out_specs=big(cols),
            scratch_shapes=[
                pltpu.VMEM((heads, length, 2 * HD), jnp.bfloat16),
                pltpu.VMEM((heads, 2 * HD, length), jnp.bfloat16),
                pltpu.VMEM((heads, length, HD), jnp.bfloat16),
                pltpu.VMEM((heads, HD, length), jnp.bfloat16),
                pltpu.VMEM((heads, length, 2 * HD), jnp.bfloat16),
                pltpu.VMEM((heads, length, 2 * HD), jnp.bfloat16),
                pltpu.VMEM((heads, HD, length), jnp.bfloat16),
                pltpu.VMEM((heads, 1, length), jnp.float32),
                pltpu.VMEM((heads, HD, length), jnp.float32),
                pltpu.VMEM((heads, TILE, 2 * HD), jnp.float32)]),
        compiler_params=pltpu.CompilerParams(dimension_semantics=("arbitrary",), vmem_limit_bytes=60 << 20),
        name="attend_back",
    )(lo, hi, reach, segments[:, None, :], qkv, att, datt, lse)


MESH = pl.DeviceIdType.MESH


def greet(peers):
    barrier = pltpu.get_barrier_semaphore()
    for peer in peers:
        pl.semaphore_signal(barrier, inc=1, device_id=peer, device_id_type=MESH)
    pl.semaphore_wait(barrier, len(peers))


def add_low(left, right):
    return (left.astype(jnp.float32) + right.astype(jnp.float32)).astype(jnp.bfloat16)


class Sends:
    def __init__(self, send_sem, recv_sem):
        self.send_sem, self.recv_sem, self.used, self.open = send_sem, recv_sem, 0, []

    def start(self, src, dst, peer):
        n = self.used
        self.used += 1
        copy = pltpu.make_async_remote_copy(
            src_ref=src, dst_ref=dst, send_sem=self.send_sem.at[n], recv_sem=self.recv_sem.at[n],
            device_id=peer, device_id_type=MESH)
        copy.start()
        self.open.append(copy)
        return copy

    def finish(self):
        for copy in self.open:
            copy.wait_send()


def fold_kernel(pieces, arrays, zs, *refs):
    parts = len(pieces)
    grads, heads_in, tokens_in = refs[:arrays], refs[arrays], refs[arrays + 1]
    outs, heads_out, tokens_out = refs[arrays + 2 : 2 * arrays + 2], refs[2 * arrays + 2], refs[2 * arrays + 3]
    at = 2 * arrays + 4
    own, got_c, got_y, got_x, got_z = [], [], [], [], []
    for n in range(parts):
        a, b, c, d, e = refs[at : at + 5]
        own.append(a), got_c.append(b), got_y.append(c), got_x.append(d), got_z.append(e)
        at += 5
    h_own, h_y, h_z, h_c = refs[at : at + 4]
    t_own, t_c, t_x = refs[at + 4 : at + 7]
    send_sem, recv_sem, load_sem = refs[at + 7 : at + 10]

    c, f = lax.axis_index("ctx"), lax.axis_index("fsdp")
    x, core, z, y = c // 2, c % 2, f // 2, f % 2
    partner = {"ctx": x * 2 + (1 - core), "fsdp": f}
    beside = {"ctx": (1 - x) * 2 + core, "fsdp": f}
    above = {"ctx": c, "fsdp": z * 2 + (1 - y)}
    far = [{"ctx": c, "fsdp": lax.rem(z + s, zs) * 2 + y} for s in range(1, zs)]
    across = [{"ctx": lax.rem(c + s, 4), "fsdp": f} for s in range(1, 4)]
    sends = Sends(send_sem, recv_sem)

    loads = []
    def load(src, dst):
        copy = pltpu.make_async_copy(src, dst, load_sem.at[len(loads)])
        copy.start()
        loads.append(copy)
        return copy

    greet([above] + far + across)

    load_t = load(tokens_in.at[:, :, core], t_own)
    copy_t = sends.start(tokens_in.at[:, :, 1 - core], t_c, partner)
    load_g, copy_c = [], []
    for n in range(parts):
        array, first, count = pieces[n]
        lanes = pl.ds(first, count)
        load_g.append(load(grads[array].at[:, core, :, :, :, lanes], own[n]))
        copy_c.append(sends.start(grads[array].at[:, 1 - core, :, :, :, lanes], got_c[n], partner))
    load_h = load(heads_in.at[:, :, y], h_own)
    copy_h = sends.start(heads_in.at[:, :, 1 - y], h_y, above)

    micro, chunks = t_own.shape[0], t_own.shape[2] // 64
    load_t.wait(), copy_t.wait_recv()
    def sum_t(there):
        def step(i, _):
            m, rows = i // chunks, pl.ds(pl.multiple_of(lax.rem(i, chunks) * 64, 64), 64)
            t_c[m, there, rows, :] = add_low(t_own[m, there, rows, :], t_c[m, there, rows, :])
            return 0
        lax.fori_loop(0, micro * chunks, step, 0)
    sum_t(1 - x)
    copy_tx = sends.start(t_c.at[:, 1 - x], t_x, beside)

    copy_y = []
    for n in range(parts):
        load_g[n].wait(), copy_c[n].wait_recv()
        def sum_c(keep, n=n):
            def step(i, _):
                a, b = i // zs, lax.rem(i, zs)
                own[n][a, b, keep] = add_low(own[n][a, b, keep], got_c[n][a, b, keep])
                return 0
            lax.fori_loop(0, 2 * zs, step, 0)
        sum_c(1 - y)
        copy_y.append(sends.start(own[n].at[:, :, 1 - y], got_y[n], above))
        sum_c(y)
    load_h.wait(), copy_h.wait_recv()
    def sum_h(i, _):
        a, b = i // zs, lax.rem(i, zs)
        h_y[a, b] = add_low(h_own[a, b], h_y[a, b])
        return 0
    lax.fori_loop(0, 4 * zs, sum_h, 0)
    copy_hz = [sends.start(h_y.at[:, lax.rem(z + s, zs)], h_z.at[s - 1], far[s - 1]) for s in range(1, zs)]
    copy_x = []
    for n in range(parts):
        copy_y[n].wait_recv()
        def sum_y(there, n=n):
            def step(b, _):
                got_y[n][there, b] = add_low(own[n][there, b, y], got_y[n][there, b])
                return 0
            lax.fori_loop(0, zs, step, 0)
        sum_y(1 - x)
        copy_x.append(sends.start(got_y[n].at[1 - x], got_x[n], beside))
        sum_y(x)
    sum_t(x)
    for copy in copy_hz:
        copy.wait_recv()
    for a in range(4):
        total = h_y[a, z].astype(jnp.float32)
        for s in range(1, zs):
            total = total + h_z[s - 1, a].astype(jnp.float32)
        h_own[a, 0] = total.astype(jnp.bfloat16)
    copy_hc = [sends.start(h_own.at[lax.rem(c + s, 4), 0], h_c.at[s - 1], across[s - 1]) for s in range(1, 4)]
    copy_z = []
    for n in range(parts):
        copy_x[n].wait_recv()
        def sum_x(b, _, n=n):
            got_x[n][b] = add_low(got_y[n][x, b], got_x[n][b])
            return 0
        lax.fori_loop(0, zs, sum_x, 0)
        copy_z.append([sends.start(got_x[n].at[lax.rem(z + s, zs)], got_z[n].at[s - 1], far[s - 1]) for s in range(1, zs)])
    copy_tx.wait_recv()
    def last_t(i, _):
        m, rows = i // chunks, pl.ds(pl.multiple_of(lax.rem(i, chunks) * 64, 64), 64)
        tokens_out[m, rows, :] = t_c[m, x, rows, :].astype(jnp.float32) + t_x[m, rows, :].astype(jnp.float32)
        return 0
    lax.fori_loop(0, micro * chunks, last_t, 0)
    heads_out[c] = h_own[c, 0].astype(jnp.float32)
    for s in range(1, 4):
        copy_hc[s - 1].wait_recv()
        heads_out[lax.rem(c + 4 - s, 4)] = h_c[s - 1].astype(jnp.float32)
    for n in range(parts):
        for copy in copy_z[n]:
            copy.wait_recv()
        total = got_x[n][z].astype(jnp.float32)
        for s in range(1, zs):
            total = total + got_z[n][s - 1].astype(jnp.float32)
        array, first, count = pieces[n]
        outs[array][:, first : first + count] = total
    sends.finish()


def fold(grads, cuts, by_head, tokens):
    ctx, fsdp = lax.axis_size("ctx"), lax.axis_size("fsdp")
    zs = fsdp // 2
    assert ctx == 4 and fsdp % 2 == 0
    f32, bf16 = jnp.float32, jnp.bfloat16
    hr, hw = by_head.shape[1:]
    micro, _, tr, tw = tokens.shape
    scratch, out, pieces = [], [], []
    for n, (g, cut) in enumerate(zip(grads, cuts)):
        r, w = g.shape[1:]
        out.append(jax.ShapeDtypeStruct((r, w), f32))
        for i in range(cut):
            v = w // cut
            pieces.append((n, i * v, v))
            scratch += [pltpu.VMEM((2, zs, 2, r, v), bf16), pltpu.VMEM((2, zs, 2, r, v), bf16), pltpu.VMEM((2, zs, r, v), bf16),
                        pltpu.VMEM((zs, r, v), bf16), pltpu.VMEM((zs - 1, r, v), bf16)]
    parts = len(pieces)
    scratch += [pltpu.VMEM((4, zs, hr, hw), bf16), pltpu.VMEM((4, zs, hr, hw), bf16), pltpu.VMEM((zs - 1, 4, hr, hw), bf16), pltpu.VMEM((3, hr, hw), bf16)]
    scratch += [pltpu.VMEM((micro, 2, tr, tw), bf16), pltpu.VMEM((micro, 2, tr, tw), bf16), pltpu.VMEM((micro, tr, tw), bf16)]
    copies = parts * (3 + zs - 1) + 2 + 1 + (zs - 1) + 3
    scratch += [pltpu.SemaphoreType.DMA((copies,)), pltpu.SemaphoreType.DMA((copies,)), pltpu.SemaphoreType.DMA((parts + 2,))]
    out += [jax.ShapeDtypeStruct((4, hr, hw), f32), jax.ShapeDtypeStruct((micro, tr, tw), f32)]
    return pl.pallas_call(
        functools.partial(fold_kernel, tuple(pieces), len(grads), zs),
        out_shape=tuple(out),
        in_specs=[pl.BlockSpec(memory_space=pl.ANY)] * (len(grads) + 2),
        out_specs=[pl.BlockSpec(memory_space=pltpu.VMEM)] * (len(grads) + 2),
        scratch_shapes=scratch,
        compiler_params=pltpu.CompilerParams(collective_id=1, has_side_effects=True, vmem_limit_bytes=63 << 20),
        name="fold",
    )(*[g.reshape((2, 2, zs, 2) + g.shape[1:]) for g in grads], by_head.reshape(4, zs, 2, hr, hw), tokens.reshape(micro, 2, 2, tr, tw))


def collect_kernel(zs, mine, tokens, mine_out, tokens_out, held_mine, held, send_sem, recv_sem, load_sem):
    c, f = lax.axis_index("ctx"), lax.axis_index("fsdp")
    x, core, z, y = c // 2, c % 2, f // 2, f % 2
    partner = {"ctx": x * 2 + (1 - core), "fsdp": f}
    beside = {"ctx": (1 - x) * 2 + core, "fsdp": f}
    above = {"ctx": c, "fsdp": z * 2 + (1 - y)}
    far = [{"ctx": c, "fsdp": lax.rem(z + s, zs) * 2 + y} for s in range(1, zs)]
    across = [{"ctx": lax.rem(c + s, 4), "fsdp": f} for s in range(1, 4)]
    greet([above] + far + across)
    sends = Sends(send_sem, recv_sem)
    micro = tokens.shape[0]
    loads = [pltpu.make_async_copy(mine.at[c], held_mine, load_sem.at[0]), pltpu.make_async_copy(tokens, held, load_sem.at[1])]
    for copy in loads:
        copy.start()
    first = [sends.start(mine.at[lax.rem(c + s, 4)], mine_out.at[c, z, y], across[s - 1]) for s in range(1, 4)]
    over_x = [sends.start(tokens.at[m], tokens_out.at[m, c], beside) for m in range(micro)]
    over_core = [sends.start(tokens.at[m], tokens_out.at[m, c], partner) for m in range(micro)]
    loads[0].wait()
    stores = [pltpu.make_async_copy(held_mine, mine_out.at[c, z, y], load_sem.at[2])]
    stores[0].start()
    loads[1].wait()
    for m in range(micro):
        stores.append(pltpu.make_async_copy(held.at[m], tokens_out.at[m, c], load_sem.at[3 + m]))
        stores[-1].start()
    for copy in first:
        copy.wait_recv()
    stores[0].wait()
    over_y = sends.start(mine_out.at[:, z, y], mine_out.at[:, z, y], above)
    own_far = [sends.start(mine_out.at[:, z, y], mine_out.at[:, z, y], peer) for peer in far]
    over_y.wait_recv()
    y_far = [sends.start(mine_out.at[:, z, 1 - y], mine_out.at[:, z, 1 - y], peer) for peer in far]
    other = (1 - x) * 2 + core
    relay = []
    for m in range(micro):
        over_x[m].wait_recv()
        relay.append(sends.start(tokens_out.at[m, other], tokens_out.at[m, other], partner))
    for copy in own_far + y_far + over_core + relay:
        copy.wait_recv()
    for copy in stores[1:]:
        copy.wait()
    sends.finish()


def collect(mine, tokens):
    ctx, fsdp = lax.axis_size("ctx"), lax.axis_size("fsdp")
    zs = fsdp // 2
    assert ctx == 4 and fsdp % 2 == 0
    micro = tokens.shape[0]
    copies = 3 + 1 + 2 * (zs - 1) + 3 * micro
    anywhere = pl.BlockSpec(memory_space=pl.ANY)
    return pl.pallas_call(
        functools.partial(collect_kernel, zs),
        out_shape=(jax.ShapeDtypeStruct((4, zs, 2) + mine.shape[1:], mine.dtype), jax.ShapeDtypeStruct((micro, 4) + tokens.shape[1:], tokens.dtype)),
        in_specs=[anywhere] * 2, out_specs=[anywhere] * 2,
        scratch_shapes=[pltpu.VMEM(mine.shape[1:], mine.dtype), pltpu.VMEM(tokens.shape, tokens.dtype), pltpu.SemaphoreType.DMA((copies,)), pltpu.SemaphoreType.DMA((copies,)), pltpu.SemaphoreType.DMA((3 + micro,))],
        compiler_params=pltpu.CompilerParams(collective_id=0, has_side_effects=True),
        name="collect",
    )(mine, tokens)


def layer_norm(summed, gain, shift):
    row_mean = jnp.mean(summed, axis=-1, keepdims=True)
    centered = summed - row_mean
    variance = jnp.mean(centered * centered, axis=-1, keepdims=True)
    recip = lax.rsqrt(variance + 1e-05)
    normed = centered * recip
    return (normed * gain + shift, normed, recip)


def norm_back(upstream, normed, recip, gain):
    scaled = upstream * gain
    first_mean = jnp.mean(scaled, axis=-1, keepdims=True)
    second_mean = jnp.mean(scaled * normed, axis=-1, keepdims=True)
    d_summed = recip * (scaled - first_mean - normed * second_mean)
    return (d_summed, jnp.sum(upstream * normed, axis=0), jnp.sum(upstream, axis=0))


def dot(left, right):
    return jnp.dot(left, right, preferred_element_type=jnp.float32)


def weight_term(left, right):
    return jnp.einsum("ta,tb->ab", left, right, preferred_element_type=jnp.float32)


def back_term(grad_low, weight):
    return jnp.einsum("tb,ab->ta", grad_low, weight, preferred_element_type=jnp.float32)


def column_sum(grad_low):
    return jnp.sum(grad_low.astype(jnp.float32), axis=0)


def exchange(pieces):
    count = lax.axis_size("ctx")
    me = lax.axis_index("ctx")
    got = lax.dynamic_update_index_in_dim(
        jnp.zeros_like(pieces), lax.dynamic_index_in_dim(pieces, me, 0, keepdims=False), me, 0
    )
    for step in range(1, count):
        piece = lax.dynamic_index_in_dim(pieces, (me + step) % count, 0, keepdims=False)
        piece = lax.ppermute(piece, "ctx", [(a, (a + step) % count) for a in range(count)])
        got = lax.dynamic_update_index_in_dim(got, piece, (me - step) % count, 0)
    return got


def body(
    inputs, segments, block_reach,
    query_weight, query_bias, key_weight, value_weight, value_bias, output_weight, output_bias,
    first_gain, first_shift, expand_weight, expand_bias, contract_weight, contract_bias,
    second_gain, second_shift, output_grad,
):
    every = ("ctx", "fsdp")
    ctx = lax.axis_size("ctx")
    me = lax.axis_index("ctx")
    micro, _, rows, width = inputs.shape
    length = rows * ctx
    cols = width // ctx
    heads = cols // HD
    f32, bf16 = jnp.float32, jnp.bfloat16

    share = query_bias.shape[0]
    ext = -(-(share + 1) // 8) * 8
    small = jnp.concatenate([query_bias, value_bias, output_bias, first_gain, first_shift, contract_bias, second_gain, second_shift, expand_bias])
    split = jnp.stack([query_weight, key_weight, value_weight], axis=1).reshape(share, 3, ctx, cols)
    mine = jnp.concatenate([
        split.transpose(2, 0, 1, 3).reshape(ctx, share, 3 * cols),
        jnp.broadcast_to(jnp.pad(small, (0, 3 * cols - small.shape[0])), (ctx, 1, 3 * cols)),
        jnp.zeros((ctx, ext - share - 1, 3 * cols), bf16)], axis=1)
    mine_all, tokens_all = collect(mine, inputs[:, 0])
    mine_all = mine_all.reshape(-1, ext, 3 * cols)
    devices = mine_all.shape[0]
    w_mine = mine_all[:, :share].reshape(width, 3 * cols)
    small_all = mine_all[:, share, : 12 * share].astype(f32)
    vector = lambda n: small_all[:, n * share : (n + 1) * share].reshape(-1)
    b_query, b_value, b_output, g_first, s_first, b_contract, g_second, s_second = [vector(n) for n in range(8)]
    b_expand = small_all[:, 8 * share :].reshape(-1)

    wide = expand_weight.shape[1] // width
    packed = jnp.concatenate([output_weight, contract_weight, expand_weight.reshape(share, wide, width).transpose(1, 0, 2).reshape(-1, width)], axis=0)
    packed = lax.all_gather(packed, every, axis=0, tiled=True).reshape(devices, -1, width)
    w_output = packed[:, :share].reshape(-1, width)
    w_contract = packed[:, share : share + share * wide].reshape(-1, width)
    w_expand = packed[:, share + share * wide :].reshape(devices, wide, share, width).transpose(0, 2, 1, 3).reshape(width, -1)

    own = lambda vec: lax.dynamic_slice_in_dim(vec, me * cols, cols, 0)
    b_mine = jnp.concatenate([own(b_query), jnp.zeros((cols,), f32), own(b_value)])
    seg = segments[:, 0]
    reach = block_reach[:, 0]
    lo, hi = bounds(seg, reach)

    flat_all = tokens_all.reshape(micro * length, width)
    qkv = (dot(flat_all, w_mine) + b_mine).astype(bf16).reshape(micro, length, 3 * cols)
    att_mine, lse = attend(qkv, seg, lo, hi, reach, heads)
    pieces = att_mine.reshape(micro, ctx, rows, cols)
    attended = [exchange(pieces[m]).transpose(1, 0, 2).reshape(rows, width) for m in range(micro)]
    attended = jnp.concatenate(attended, axis=0)

    tokens = inputs[:, 0].reshape(micro * rows, width)
    branch = dot(attended, w_output) + b_output
    hidden, normed_first, recip_first = layer_norm(tokens.astype(f32) + branch, g_first, s_first)
    hidden_low = hidden.astype(bf16)
    pre = dot(hidden_low, w_expand) + b_expand
    phi = 0.5 * (1.0 + lax.erf(pre * (1.0 / math.sqrt(2.0))))
    act_low = (pre * phi).astype(bf16)
    slope = phi + pre * (jnp.exp(-0.5 * pre * pre) * (1.0 / math.sqrt(2.0 * math.pi)))
    second_sum = hidden + dot(act_low, w_contract) + b_contract
    result, normed_second, recip_second = layer_norm(second_sum, g_second, s_second)
    layer_output = result.astype(bf16)
    upstream = output_grad[:, 0].reshape(micro * rows, width).astype(f32)
    d_res2, grad_g2, grad_s2 = norm_back(upstream, normed_second, recip_second, g_second)
    d_ffn = d_res2.astype(bf16)
    grad_w2 = weight_term(act_low, d_ffn)
    grad_b2 = column_sum(d_ffn)
    d_pre = (back_term(d_ffn, w_contract) * slope).astype(bf16)
    grad_w1 = weight_term(hidden_low, d_pre)
    grad_b1 = column_sum(d_pre)
    d_hidden = d_res2 + back_term(d_pre, w_expand)
    d_res1, grad_g1, grad_s1 = norm_back(d_hidden, normed_first, recip_first, g_first)
    d_branch = d_res1.astype(bf16)
    grad_wo = weight_term(attended, d_branch)
    grad_bo = column_sum(d_branch)
    d_attended = back_term(d_branch, w_output).astype(bf16)

    out_pieces = d_attended.reshape(micro, rows, ctx, cols)
    datt_mine = jnp.stack([exchange(out_pieces[m].transpose(1, 0, 2)).reshape(length, cols) for m in range(micro)])
    d_qkv = attend_back(qkv, att_mine, datt_mine, lse, seg, lo, hi, reach, heads)
    flat_d = d_qkv.reshape(micro * length, 3 * cols)
    grad_qkv = weight_term(flat_all, flat_d)
    grad_b = column_sum(flat_d)
    part = back_term(flat_d, w_mine).astype(bf16).reshape(micro, ctx, rows, width)

    place = lambda vec: lax.dynamic_update_slice_in_dim(jnp.zeros((width,), f32), vec, me * cols, 0)
    vectors = [place(grad_b[:cols]), place(grad_b[2 * cols :]), grad_bo, grad_g1, grad_s1, grad_b2, grad_g2, grad_s2, grad_b1]
    stacked = jnp.concatenate([v.reshape(devices, -1) for v in vectors], axis=1)
    stacked = jnp.pad(stacked, ((0, 0), (0, width - stacked.shape[1]))).astype(bf16)
    with_small = jnp.concatenate([
        grad_wo.astype(bf16).reshape(devices, share, width), stacked[:, None], jnp.zeros((devices, ext - share - 1, width), bf16)], axis=1)
    gw2 = lax.psum_scatter(grad_w2.astype(bf16), every, scatter_dimension=0, tiled=True).astype(f32)
    gw1, both, by_head, summed = fold(
        [grad_w1.astype(bf16).reshape(devices, share, -1), with_small], [2, 1],
        grad_qkv.astype(bf16).reshape(devices, share, 3 * cols), part)
    token_grad = d_res1 + summed.reshape(micro * rows, width)
    gq, gk, gv = [by_head[:, :, n * cols : (n + 1) * cols].transpose(1, 0, 2).reshape(share, width) for n in range(3)]
    piece = lambda n: both[share, n * share : (n + 1) * share]
    gbq, gbv, gbo, gg1, gs1, gb2, gg2, gs2 = [piece(n) for n in range(8)]
    gb1 = both[share, 8 * share : 12 * share]
    four = (micro, 1, rows, width)
    return (
        layer_output.reshape(four), token_grad.reshape(four), gq, gbq, gk, gv, gbv, both[:share], gbo, gg1, gs1,
        gw1, gb1, gw2, gb2, gg2, gs2,
    )


def solution(mesh):
    rows = P(("ctx", "fsdp"), None)
    flat = P(("ctx", "fsdp"))
    tokens = P(None, "fsdp", "ctx", None)
    params = (rows, flat, rows, rows, flat, rows, flat, flat, flat, rows, flat, rows, flat, flat, flat)
    return jax.shard_map(
        body,
        mesh=mesh,
        in_specs=(tokens, P(None, "fsdp", None), P(None, "fsdp")) + params + (tokens,),
        out_specs=(tokens, tokens) + params,
        check_vma=False,
    )
```

```python
import functools
import math

import jax
import jax.numpy as jnp
from jax import lax
from jax.experimental import pallas as pl
from jax.experimental.pallas import tpu as pltpu
from jax.sharding import PartitionSpec as P

HD = 64
KEY_BLOCK = 128
TILE = 256
SEG_COUNT = 32
FAR = 1e30

def mask_rows(seg_row, reach, first_block):
    n = seg_row.shape[1]
    row = lax.broadcasted_iota(jnp.int32, (HD, n), 0)
    seg = jnp.broadcast_to(seg_row, (HD, n))
    block = lax.broadcasted_iota(jnp.int32, (HD, n), 1) // KEY_BLOCK + first_block
    is_seg = row < SEG_COUNT
    key_at = row - SEG_COUNT
    far = jnp.logical_not(is_seg) & (jnp.abs(key_at - block) >= reach)
    q_side = jnp.where((is_seg & (seg == row)) | far, -FAR, 0.0)
    k_side = jnp.where((is_seg & (seg != row)) | (key_at == block), 1.0, 0.0)
    return q_side.astype(jnp.bfloat16), k_side.astype(jnp.bfloat16)


def token_block(me, s, count, rows):
    return pl.ds(pl.multiple_of(lax.rem(me + s, count) * rows, rows), rows)


def fwd_kernel(heads, count, lo_ref, hi_ref, at_ref, seg_ref, qkv_ref, *refs):
    att_refs, lse_ref, (kaug, qaug, vtr, att) = refs[:count], refs[count], refs[count + 1 :]
    reach, me = at_ref[0], at_ref[1]
    length = qkv_ref.shape[1]
    rows, width = length // count, heads * HD

    def prepare(s, _):
        here = pl.ds(pl.multiple_of(s * rows, rows), rows)
        there = token_block(me, s, count, rows)
        q_side, k_side = mask_rows(seg_ref[:, there], reach, lax.rem(me + s, count) * (rows // KEY_BLOCK))
        for h in range(heads):
            q = qkv_ref[h * HD : (h + 1) * HD, here]
            k = qkv_ref[width + h * HD : width + (h + 1) * HD, here]
            qaug[h, 0:HD, there] = (q.astype(jnp.float32) * (1.0 / math.sqrt(HD))).astype(jnp.bfloat16)
            qaug[h, HD : 2 * HD, there] = q_side
            kaug[h, there, :] = jnp.transpose(jnp.concatenate([k, k_side], axis=0))
            vtr[h, :, there] = qkv_ref[2 * width + h * HD : 2 * width + (h + 1) * HD, here]
        return 0
    lax.fori_loop(0, count, prepare, 0)

    def q_step(i, _):
        qs = pl.ds(pl.multiple_of(i * TILE, TILE), TILE)
        def k_step(j, carry):
            ks = pl.ds(pl.multiple_of(j * TILE, TILE), TILE)
            out = []
            for h in range(heads):
                peak, total, acc = carry[h]
                s = jnp.dot(kaug[h, ks, :], qaug[h, :, qs], preferred_element_type=jnp.float32)
                new = jnp.maximum(peak, jnp.max(s, axis=0, keepdims=True))
                p = jnp.exp(s - new)
                fade = jnp.exp(peak - new)
                total = total * fade + jnp.sum(p, axis=0, keepdims=True)
                acc = acc * fade + jnp.dot(vtr[h, :, ks], p.astype(jnp.bfloat16), preferred_element_type=jnp.float32)
                out.append((new, total, acc))
            return tuple(out)
        start = tuple((jnp.full((1, TILE), -3e38, jnp.float32), jnp.zeros((1, TILE), jnp.float32), jnp.zeros((HD, TILE), jnp.float32)) for _ in range(heads))
        done = lax.fori_loop(lo_ref[i], hi_ref[i], k_step, start)
        for h in range(heads):
            peak, total, acc = done[h]
            att[h * HD : (h + 1) * HD, qs] = (acc / total).astype(jnp.bfloat16)
            lse_ref[h : h + 1, qs] = peak + jnp.log(total)
        return 0
    lax.fori_loop(0, length // TILE, q_step, 0)
    for s in range(count):
        att_refs[s][...] = att[:, token_block(me, s, count, rows)]


def attend(qkv, seg, lo, hi, at, heads, count):
    cols, length = qkv.shape
    width, rows = heads * HD, length // count
    whole = lambda shape: pl.BlockSpec(shape, lambda n, *_: (0, 0))
    return pl.pallas_call(
        functools.partial(fwd_kernel, heads, count),
        out_shape=[jax.ShapeDtypeStruct((width, rows), jnp.bfloat16)] * count + [jax.ShapeDtypeStruct((8, length), jnp.float32)],
        grid_spec=pltpu.PrefetchScalarGridSpec(
            num_scalar_prefetch=3, grid=(1,),
            in_specs=[whole((1, length)), whole((cols, length))],
            out_specs=[whole((width, rows))] * count + [whole((8, length))],
            scratch_shapes=[pltpu.VMEM((heads, length, 2 * HD), jnp.bfloat16), pltpu.VMEM((heads, 2 * HD, length), jnp.bfloat16),
                            pltpu.VMEM((heads, HD, length), jnp.bfloat16), pltpu.VMEM((width, length), jnp.bfloat16)]),
        compiler_params=pltpu.CompilerParams(dimension_semantics=("arbitrary",), vmem_limit_bytes=40 << 20),
        cost_estimate=pl.CostEstimate(flops=30_000_000_000, bytes_accessed=4_000_000, transcendentals=0),
        name="attend",
    )(lo, hi, at, seg, qkv)


def bwd_kernel(heads, count, lo_ref, hi_ref, at_ref, seg_ref, qkv_ref, lse_ref, *refs):
    att_refs, datt_refs, dqkv_ref = refs[:count], refs[count : 2 * count], refs[2 * count]
    kaug, qaug, v_nat, dotr, do_z, q_z, ktr, delta, dqt, dkv = refs[2 * count + 1 :]
    reach, me = at_ref[0], at_ref[1]
    length = qkv_ref.shape[1]
    rows, width = length // count, heads * HD
    scale = 1.0 / math.sqrt(HD)
    for s in range(count):
        there = token_block(me, s, count, rows)
        for h in range(heads):
            do, o = datt_refs[s][h * HD : (h + 1) * HD, :], att_refs[s][h * HD : (h + 1) * HD, :]
            dotr[h, :, there] = do
            delta[h, :, there] = jnp.sum(do.astype(jnp.float32) * o.astype(jnp.float32), axis=0, keepdims=True)
    dqt[...] = jnp.zeros_like(dqt)

    def prepare(s, _):
        here = pl.ds(pl.multiple_of(s * rows, rows), rows)
        there = token_block(me, s, count, rows)
        q_side, k_side = mask_rows(seg_ref[:, there], reach, lax.rem(me + s, count) * (rows // KEY_BLOCK))
        zero = jnp.zeros((HD, rows), jnp.bfloat16)
        for h in range(heads):
            q = (qkv_ref[h * HD : (h + 1) * HD, here].astype(jnp.float32) * scale).astype(jnp.bfloat16)
            k = qkv_ref[width + h * HD : width + (h + 1) * HD, here]
            v = qkv_ref[2 * width + h * HD : 2 * width + (h + 1) * HD, here]
            qaug[h, 0:HD, there] = q
            qaug[h, HD : 2 * HD, there] = q_side
            kaug[h, there, :] = jnp.transpose(jnp.concatenate([k, k_side], axis=0))
            ktr[h, :, there] = k
            v_nat[h, there, :] = jnp.transpose(v)
            do_z[h, there, :] = jnp.transpose(jnp.concatenate([dotr[h, :, there], zero], axis=0))
            q_z[h, there, :] = jnp.transpose(jnp.concatenate([zero, q], axis=0))
        return 0
    lax.fori_loop(0, count, prepare, 0)

    def k_step(j, _):
        ks = pl.ds(pl.multiple_of(j * TILE, TILE), TILE)
        dkv[...] = jnp.zeros_like(dkv)
        def q_step(i, _):
            qs = pl.ds(pl.multiple_of(i * TILE, TILE), TILE)
            for h in range(heads):
                s = jnp.dot(kaug[h, ks, :], qaug[h, :, qs], preferred_element_type=jnp.float32)
                p = jnp.exp(s - lse_ref[h : h + 1, qs])
                dp = jnp.dot(v_nat[h, ks, :], dotr[h, :, qs], preferred_element_type=jnp.float32)
                ds = (p * (dp - delta[h, :, qs])).astype(jnp.bfloat16)
                dkv[h] += jnp.dot(p.astype(jnp.bfloat16), do_z[h, qs, :], preferred_element_type=jnp.float32) + jnp.dot(ds, q_z[h, qs, :], preferred_element_type=jnp.float32)
                dqt[h, :, qs] += jnp.dot(ktr[h, :, ks], ds, preferred_element_type=jnp.float32)
            return 0
        lax.fori_loop(lo_ref[j], hi_ref[j], q_step, 0)
        slot = lax.rem(j // (rows // TILE) + count - me, count)
        out = pl.ds(pl.multiple_of(slot * rows + lax.rem(j, rows // TILE) * TILE, TILE), TILE)
        for h in range(heads):
            both = dkv[h]
            dqkv_ref[out, 2 * width + h * HD : 2 * width + (h + 1) * HD] = both[:, 0:HD].astype(jnp.bfloat16)
            dqkv_ref[out, width + h * HD : width + (h + 1) * HD] = both[:, HD : 2 * HD].astype(jnp.bfloat16)
        return 0
    lax.fori_loop(0, length // TILE, k_step, 0)

    def finish(s, _):
        here = pl.ds(pl.multiple_of(s * rows, rows), rows)
        there = token_block(me, s, count, rows)
        for h in range(heads):
            dqkv_ref[here, h * HD : (h + 1) * HD] = jnp.transpose(dqt[h, :, there] * scale).astype(jnp.bfloat16)
        return 0
    lax.fori_loop(0, count, finish, 0)


def attend_back(qkv, att, datt, lse, seg, lo, hi, at, heads, count):
    cols, length = qkv.shape
    width, rows = heads * HD, length // count
    whole = lambda shape: pl.BlockSpec(shape, lambda n, *_: (0, 0))
    return pl.pallas_call(
        functools.partial(bwd_kernel, heads, count),
        out_shape=jax.ShapeDtypeStruct((length, cols), jnp.bfloat16),
        grid_spec=pltpu.PrefetchScalarGridSpec(
            num_scalar_prefetch=3, grid=(1,),
            in_specs=[whole((1, length)), whole((cols, length)), whole((8, length))] + [whole((width, rows))] * (2 * count),
            out_specs=whole((length, cols)),
            scratch_shapes=[
                pltpu.VMEM((heads, length, 2 * HD), jnp.bfloat16),
                pltpu.VMEM((heads, 2 * HD, length), jnp.bfloat16),
                pltpu.VMEM((heads, length, HD), jnp.bfloat16),
                pltpu.VMEM((heads, HD, length), jnp.bfloat16),
                pltpu.VMEM((heads, length, 2 * HD), jnp.bfloat16),
                pltpu.VMEM((heads, length, 2 * HD), jnp.bfloat16),
                pltpu.VMEM((heads, HD, length), jnp.bfloat16),
                pltpu.VMEM((heads, 1, length), jnp.float32),
                pltpu.VMEM((heads, HD, length), jnp.float32),
                pltpu.VMEM((heads, TILE, 2 * HD), jnp.float32)]),
        compiler_params=pltpu.CompilerParams(dimension_semantics=("arbitrary",), vmem_limit_bytes=48 << 20),
        cost_estimate=pl.CostEstimate(flops=30_000_000_000, bytes_accessed=6_000_000, transcendentals=0),
        name="attend_back",
    )(lo, hi, at, seg, qkv, lse, *att, *datt)


def bounds(segments, reach):
    first = segments[:, ::TILE]
    last = segments[:, TILE - 1::TILE]
    n = first.shape[1]
    at = jnp.arange(n)
    per = TILE // KEY_BLOCK
    gap = per * jnp.abs(at[:, None] - at[None, :]) - (per - 1)
    near = gap[None] < reach[:, None, None]
    before = (at[None, :] < at[:, None])[None] & near & (first[:, :, None] == last[:, None, :])
    after = (at[None, :] > at[:, None])[None] & near & (last[:, :, None] == first[:, None, :])
    lo = at[None] - jnp.sum(before, axis=2, dtype=jnp.int32)
    hi = at[None] + 1 + jnp.sum(after, axis=2, dtype=jnp.int32)
    return lo.astype(jnp.int32), hi.astype(jnp.int32)


MESH = pl.DeviceIdType.MESH


def greet(peers):
    barrier = pltpu.get_barrier_semaphore()
    for peer in peers:
        pl.semaphore_signal(barrier, inc=1, device_id=peer, device_id_type=MESH)
    pl.semaphore_wait(barrier, len(peers))


def add_low(left, right):
    return (left.astype(jnp.float32) + right.astype(jnp.float32)).astype(jnp.bfloat16)


class Sends:
    def __init__(self, send_sem, recv_sem):
        self.send_sem, self.recv_sem, self.used, self.open = send_sem, recv_sem, 0, []

    def start(self, src, dst, peer):
        n = self.used
        self.used += 1
        copy = pltpu.make_async_remote_copy(
            src_ref=src, dst_ref=dst, send_sem=self.send_sem.at[n], recv_sem=self.recv_sem.at[n],
            device_id=peer, device_id_type=MESH)
        copy.start()
        self.open.append(copy)
        return copy

    def finish(self):
        for copy in self.open:
            copy.wait_send()


def fold_kernel(zs, heads_in, tokens_in, heads_out, tokens_out, h_own, h_y, h_z, h_c, t_own, t_c, t_x, send_sem, recv_sem, load_sem):
    c, f = lax.axis_index("ctx"), lax.axis_index("fsdp")
    x, core, z, y = c // 2, c % 2, f // 2, f % 2
    partner = {"ctx": x * 2 + (1 - core), "fsdp": f}
    beside = {"ctx": (1 - x) * 2 + core, "fsdp": f}
    above = {"ctx": c, "fsdp": z * 2 + (1 - y)}
    far = [{"ctx": c, "fsdp": lax.rem(z + s, zs) * 2 + y} for s in range(1, zs)]
    across = [{"ctx": lax.rem(c + s, 4), "fsdp": f} for s in range(1, 4)]
    sends = Sends(send_sem, recv_sem)
    greet([above] + far + across)

    near = 1 + 2 * core
    other = 3 - 2 * core
    loads = [pltpu.make_async_copy(tokens_in.at[2], t_own.at[1], load_sem.at[0]),
             pltpu.make_async_copy(heads_in.at[:, :, y], h_own, load_sem.at[1]),
             pltpu.make_async_copy(tokens_in.at[0], t_own.at[0], load_sem.at[2])]
    copy_there = sends.start(tokens_in.at[other], t_c.at[1], partner)
    loads[0].start()
    copy_h = sends.start(heads_in.at[:, :, 1 - y], h_y, above)
    loads[1].start()
    copy_here = sends.start(tokens_in.at[near], t_c.at[0], partner)
    loads[2].start()

    chunks = t_own.shape[1] // 64
    def sum_t(place):
        def step(i, _):
            rows = pl.ds(pl.multiple_of(i * 64, 64), 64)
            t_c[place, rows, :] = add_low(t_own[place, rows, :], t_c[place, rows, :])
            return 0
        lax.fori_loop(0, chunks, step, 0)
    loads[0].wait(), copy_there.wait_recv()
    sum_t(1)
    copy_tx = sends.start(t_c.at[1], t_x, beside)

    loads[1].wait(), copy_h.wait_recv()
    def sum_h(i, _):
        a, b = i // zs, lax.rem(i, zs)
        h_y[a, b] = add_low(h_own[a, b], h_y[a, b])
        return 0
    lax.fori_loop(0, 4 * zs, sum_h, 0)
    copy_hz = [sends.start(h_y.at[:, lax.rem(z + s, zs)], h_z.at[s - 1], far[s - 1]) for s in range(1, zs)]
    loads[2].wait(), copy_here.wait_recv()
    sum_t(0)
    for copy in copy_hz:
        copy.wait_recv()
    def total_h(a, _):
        total = h_y[a, z].astype(jnp.float32)
        for s in range(1, zs):
            total = total + h_z[s - 1, a].astype(jnp.float32)
        h_own[a, 0] = total.astype(jnp.bfloat16)
        return 0
    lax.fori_loop(0, 4, total_h, 0)
    copy_hc = [sends.start(h_own.at[lax.rem(c + s, 4), 0], h_c.at[s - 1], across[s - 1]) for s in range(1, 4)]
    copy_tx.wait_recv()
    def last_t(i, _):
        rows = pl.ds(pl.multiple_of(i * 64, 64), 64)
        tokens_out[rows, :] = t_c[0, rows, :].astype(jnp.float32) + t_x[rows, :].astype(jnp.float32)
        return 0
    lax.fori_loop(0, chunks, last_t, 0)
    heads_out[c] = h_own[c, 0].astype(jnp.float32)
    for s in range(1, 4):
        copy_hc[s - 1].wait_recv()
        heads_out[lax.rem(c + 4 - s, 4)] = h_c[s - 1].astype(jnp.float32)
    sends.finish()


def fold(by_head, tokens):
    ctx, fsdp = lax.axis_size("ctx"), lax.axis_size("fsdp")
    zs = fsdp // 2
    assert ctx == 4 and fsdp % 2 == 0
    f32, bf16 = jnp.float32, jnp.bfloat16
    hr, hw = by_head.shape[1:]
    _, tr, tw = tokens.shape
    copies = 4 + (zs - 1) + 3
    anywhere, vmem = pl.BlockSpec(memory_space=pl.ANY), pl.BlockSpec(memory_space=pltpu.VMEM)
    return pl.pallas_call(
        functools.partial(fold_kernel, zs),
        out_shape=(jax.ShapeDtypeStruct((4, hr, hw), f32), jax.ShapeDtypeStruct((tr, tw), f32)),
        in_specs=[anywhere] * 2, out_specs=[vmem] * 2,
        scratch_shapes=[
            pltpu.VMEM((4, zs, hr, hw), bf16), pltpu.VMEM((4, zs, hr, hw), bf16), pltpu.VMEM((zs - 1, 4, hr, hw), bf16), pltpu.VMEM((3, hr, hw), bf16),
            pltpu.VMEM((2, tr, tw), bf16), pltpu.VMEM((2, tr, tw), bf16), pltpu.VMEM((tr, tw), bf16),
            pltpu.SemaphoreType.DMA((copies,)), pltpu.SemaphoreType.DMA((copies,)), pltpu.SemaphoreType.DMA((3,))],
        compiler_params=pltpu.CompilerParams(collective_id=1, has_side_effects=True, vmem_limit_bytes=63 << 20),
        name="fold",
    )(by_head.reshape(4, zs, 2, hr, hw), tokens)


def collect_kernel(zs, mine, tokens, mine_out, tokens_out, held_mine, held, send_sem, recv_sem, load_sem):
    c, f = lax.axis_index("ctx"), lax.axis_index("fsdp")
    x, core, z, y = c // 2, c % 2, f // 2, f % 2
    partner = {"ctx": x * 2 + (1 - core), "fsdp": f}
    beside = {"ctx": (1 - x) * 2 + core, "fsdp": f}
    above = {"ctx": c, "fsdp": z * 2 + (1 - y)}
    far = [{"ctx": c, "fsdp": lax.rem(z + s, zs) * 2 + y} for s in range(1, zs)]
    across = [{"ctx": lax.rem(c + s, 4), "fsdp": f} for s in range(1, 4)]
    greet([above] + far + across)
    sends = Sends(send_sem, recv_sem)
    loads = [pltpu.make_async_copy(mine.at[c], held_mine, load_sem.at[0]), pltpu.make_async_copy(tokens, held, load_sem.at[1])]
    for copy in loads:
        copy.start()
    first = [sends.start(mine.at[lax.rem(c + s, 4)], mine_out.at[c, z, y], across[s - 1]) for s in range(1, 4)]
    over_x = sends.start(tokens, tokens_out.at[2], beside)
    over_core = sends.start(tokens, tokens_out.at[3 - 2 * core], partner)
    loads[0].wait()
    stores = [pltpu.make_async_copy(held_mine, mine_out.at[c, z, y], load_sem.at[2])]
    stores[0].start()
    loads[1].wait()
    stores.append(pltpu.make_async_copy(held, tokens_out.at[0], load_sem.at[3]))
    stores[1].start()
    for copy in first:
        copy.wait_recv()
    stores[0].wait()
    over_y = sends.start(mine_out.at[:, z, y], mine_out.at[:, z, y], above)
    own_far = [sends.start(mine_out.at[:, z, y], mine_out.at[:, z, y], peer) for peer in far]
    over_y.wait_recv()
    y_far = [sends.start(mine_out.at[:, z, 1 - y], mine_out.at[:, z, 1 - y], peer) for peer in far]
    over_x.wait_recv()
    relay = sends.start(tokens_out.at[2], tokens_out.at[1 + 2 * core], partner)
    for copy in own_far + y_far + [over_core, relay]:
        copy.wait_recv()
    stores[1].wait()
    sends.finish()


def collect(mine, tokens):
    ctx, fsdp = lax.axis_size("ctx"), lax.axis_size("fsdp")
    zs = fsdp // 2
    assert ctx == 4 and fsdp % 2 == 0
    copies = 3 + 1 + 2 * (zs - 1) + 3
    anywhere = pl.BlockSpec(memory_space=pl.ANY)
    return pl.pallas_call(
        functools.partial(collect_kernel, zs),
        out_shape=(jax.ShapeDtypeStruct((4, zs, 2) + mine.shape[1:], mine.dtype), jax.ShapeDtypeStruct((4,) + tokens.shape, tokens.dtype)),
        in_specs=[anywhere] * 2, out_specs=[anywhere] * 2,
        scratch_shapes=[pltpu.VMEM(mine.shape[1:], mine.dtype), pltpu.VMEM(tokens.shape, tokens.dtype), pltpu.SemaphoreType.DMA((copies,)), pltpu.SemaphoreType.DMA((copies,)), pltpu.SemaphoreType.DMA((4,))],
        compiler_params=pltpu.CompilerParams(collective_id=0, has_side_effects=True),
        name="collect",
    )(mine, tokens)


def layer_norm(summed, gain, shift):
    row_mean = jnp.mean(summed, axis=-1, keepdims=True)
    centered = summed - row_mean
    variance = jnp.mean(centered * centered, axis=-1, keepdims=True)
    recip = lax.rsqrt(variance + 1e-05)
    normed = centered * recip
    return (normed * gain + shift, normed, recip)


def norm_back(upstream, normed, recip, gain):
    scaled = upstream * gain
    first_mean = jnp.mean(scaled, axis=-1, keepdims=True)
    second_mean = jnp.mean(scaled * normed, axis=-1, keepdims=True)
    d_summed = recip * (scaled - first_mean - normed * second_mean)
    return (d_summed, jnp.sum(upstream * normed, axis=0), jnp.sum(upstream, axis=0))


def dot(left, right):
    return jnp.dot(left, right, preferred_element_type=jnp.float32)


def weight_term(left, right):
    return jnp.einsum("ta,tb->ab", left, right, preferred_element_type=jnp.float32)


def back_term(grad_low, weight):
    return jnp.einsum("tb,ab->ta", grad_low, weight, preferred_element_type=jnp.float32)


def column_sum(grad_low):
    return jnp.sum(grad_low.astype(jnp.float32), axis=0)


def shift(piece, step):
    count = lax.axis_size("ctx")
    return lax.ppermute(piece, "ctx", [(a, (a + step) % count) for a in range(count)])


def body(
    inputs, segments, block_reach,
    query_weight, query_bias, key_weight, value_weight, value_bias, output_weight, output_bias,
    first_gain, first_shift, expand_weight, expand_bias, contract_weight, contract_bias,
    second_gain, second_shift, output_grad,
):
    every = ("ctx", "fsdp")
    ctx = lax.axis_size("ctx")
    me = lax.axis_index("ctx")
    micro, _, rows, width = inputs.shape
    length = rows * ctx
    cols = width // ctx
    heads = cols // HD
    f32, bf16 = jnp.float32, jnp.bfloat16

    share = query_bias.shape[0]
    lines = 8 + expand_bias.shape[0] // share
    ext = -(-(share + lines) // 8) * 8
    small = jnp.concatenate([v.reshape(-1, share) for v in (
        query_bias, value_bias, output_bias, first_gain, first_shift, contract_bias, second_gain, second_shift, expand_bias)], axis=0)
    small = jnp.pad(small, ((0, ext - share - lines), (0, 3 * cols - share)))
    split = jnp.concatenate([
        jnp.stack([w[:, n * cols : (n + 1) * cols] for n in range(ctx)]) for w in (query_weight, key_weight, value_weight)], axis=2)
    mine = jnp.concatenate([split, jnp.broadcast_to(small, (ctx,) + small.shape)], axis=1)

    wide = expand_weight.shape[1] // width
    packed = jnp.concatenate([output_weight, contract_weight] + [expand_weight[:, n * width : (n + 1) * width] for n in range(wide)], axis=0)
    packed = lax.all_gather(packed, every, axis=0, tiled=True)

    mine_all, tokens_first = collect(mine, inputs[0, 0])
    mine_all = mine_all.reshape(-1, ext, 3 * cols)
    devices = mine_all.shape[0]
    later, mine_all = lax.optimization_barrier((inputs[1:, 0], mine_all))
    tokens_all = [tokens_first.reshape(length, width)]
    for m in range(1, micro):
        tokens_all.append(jnp.concatenate([later[m - 1]] + [shift(later[m - 1], -s) for s in range(1, ctx)], axis=0))
    w_mine = mine_all[:, :share].reshape(width, 3 * cols)
    small_all = mine_all[:, share : share + lines, :share].astype(f32)
    vector = lambda n: small_all[:, n].reshape(-1)
    b_query, b_value, b_output, g_first, s_first, b_contract, g_second, s_second = [vector(n) for n in range(8)]
    b_expand = small_all[:, 8:].reshape(-1)

    packed = packed.reshape(devices, -1, width)
    back = [lax.rem(me + ctx - s, ctx) for s in range(ctx)]
    by_owner = packed[:, :share].reshape(ctx, cols, width)
    w_output = jnp.concatenate([lax.dynamic_index_in_dim(by_owner, back[s], 0, keepdims=False) for s in range(ctx)], axis=0)
    w_contract = packed[:, share : share + share * wide].reshape(-1, width)
    w_expand = packed[:, share + share * wide :].reshape(devices, wide, share, width).transpose(0, 2, 1, 3).reshape(width, -1)

    own = lambda vec: lax.dynamic_slice_in_dim(vec, me * cols, cols, 0)
    b_mine = jnp.concatenate([own(b_query), jnp.zeros((cols,), f32), own(b_value)])
    seg = segments[:, 0]
    reach = block_reach[:, 0]
    lo, hi = bounds(seg, reach)
    at = [jnp.stack([reach[m], me]) for m in range(micro)]

    qkv, att, lse, attended = [], [], [], []
    for m in range(micro):
        flat = tokens_all[m]
        if m:
            flat, _ = lax.optimization_barrier((flat, lse[-1]))
        projected = jnp.einsum("wc,tw->ct", w_mine, flat, preferred_element_type=f32)
        qkv.append((projected + b_mine[:, None]).astype(bf16))
        *pieces, logs = attend(qkv[m], seg[m : m + 1], lo[m], hi[m], at[m], heads, ctx)
        att.append(pieces), lse.append(logs)
        attended.append(jnp.concatenate([pieces[0]] + [shift(pieces[s], s) for s in range(1, ctx)], axis=0))
    attended = jnp.concatenate(attended, axis=1)

    tokens = inputs[:, 0].reshape(micro * rows, width)
    branch = jnp.einsum("ct,cn->tn", attended, w_output, preferred_element_type=f32) + b_output
    hidden, normed_first, recip_first = layer_norm(tokens.astype(f32) + branch, g_first, s_first)
    hidden_low = hidden.astype(bf16)
    pre = dot(hidden_low, w_expand) + b_expand
    phi = 0.5 * (1.0 + lax.erf(pre * (1.0 / math.sqrt(2.0))))
    act_low = (pre * phi).astype(bf16)
    slope = phi + pre * (jnp.exp(-0.5 * pre * pre) * (1.0 / math.sqrt(2.0 * math.pi)))
    second_sum = hidden + dot(act_low, w_contract) + b_contract
    result, normed_second, recip_second = layer_norm(second_sum, g_second, s_second)
    layer_output = result.astype(bf16)
    upstream = output_grad[:, 0].reshape(micro * rows, width).astype(f32)
    d_res2, grad_g2, grad_s2 = norm_back(upstream, normed_second, recip_second, g_second)
    d_ffn = d_res2.astype(bf16)
    grad_b2 = column_sum(d_ffn)
    d_pre = (back_term(d_ffn, w_contract) * slope).astype(bf16)
    grad_b1 = column_sum(d_pre)
    d_hidden = d_res2 + back_term(d_pre, w_expand)
    d_res1, grad_g1, grad_s1 = norm_back(d_hidden, normed_first, recip_first, g_first)
    d_branch = d_res1.astype(bf16)
    grad_bo = column_sum(d_branch)
    d_attended = [
        jnp.einsum("cn,tn->ct", w_output, d_branch[m * rows : (m + 1) * rows], preferred_element_type=f32).astype(bf16).reshape(ctx, cols, rows)
        for m in range(micro)]

    *d_attended, d_ffn, d_pre, d_branch = lax.optimization_barrier((*d_attended, d_ffn, d_pre, d_branch))
    d_att = [[d_attended[m][0]] + [shift(d_attended[m][s], -s) for s in range(1, ctx)] for m in range(micro)]
    grad_w2 = weight_term(act_low, d_ffn).astype(bf16).reshape(devices, -1, width)
    grad_w1 = [weight_term(hidden_low, d_pre[:, n * width : (n + 1) * width]).astype(bf16).reshape(devices, share, width) for n in range(wide)]
    grad_wo = dot(attended, d_branch).astype(bf16).reshape(ctx, cols, width)
    grad_wo = jnp.concatenate([lax.dynamic_index_in_dim(grad_wo, back[b], 0, keepdims=False) for b in range(ctx)], axis=0).reshape(devices, share, width)
    grads = jnp.concatenate([grad_wo, grad_w2] + grad_w1, axis=1).reshape(-1, width)
    grads = lax.psum_scatter(grads, every, scatter_dimension=0, tiled=True)

    token_grad, grad_qkv, grad_b = [], 0.0, 0.0
    part = None
    for m in range(micro):
        given = d_att[m]
        if m:
            *given, part = lax.optimization_barrier((*given, part))
            parts = [part[0]] + [shift(part[s], s) for s in range(1, ctx)]
            token_grad.append(sum((p.astype(f32) for p in parts), d_res1[(m - 1) * rows : m * rows]))
        d_qkv = attend_back(qkv[m], att[m], given, lse[m], seg[m : m + 1], lo[m], hi[m], at[m], heads, ctx)
        part = back_term(d_qkv, w_mine).astype(bf16).reshape(ctx, rows, width)
        grad_qkv = grad_qkv + weight_term(tokens_all[m], d_qkv)
        grad_b = grad_b + column_sum(d_qkv)

    place = lambda vec: lax.dynamic_update_slice_in_dim(jnp.zeros((width,), f32), vec, me * cols, 0)
    vectors = [place(grad_b[:cols]), place(grad_b[2 * cols :]), grad_bo, grad_g1, grad_s1, grad_b2, grad_g2, grad_s2]
    stacked = jnp.concatenate([v.reshape(devices, 1, share) for v in vectors] + [grad_b1.reshape(devices, -1, share)], axis=1)
    stacked = jnp.pad(stacked, ((0, 0), (0, ext - share - lines), (0, 3 * cols - share))).astype(bf16)
    by_head = jnp.concatenate([grad_qkv.astype(bf16).reshape(devices, share, 3 * cols), stacked], axis=1)
    by_head, summed = fold(by_head, part)
    token_grad.append(d_res1[(micro - 1) * rows :] + summed)
    gq, gk, gv = [by_head[:, :share, n * cols : (n + 1) * cols].transpose(1, 0, 2).reshape(share, width) for n in range(3)]
    both = jnp.sum(by_head[:, share : share + lines, :share], axis=0)
    gbq, gbv, gbo, gg1, gs1, gb2, gg2, gs2 = [both[n] for n in range(8)]
    gb1 = both[8:].reshape(-1)
    grads = grads.astype(f32)
    gwo, gw2 = grads[:share], grads[share : share + share * wide]
    gw1 = jnp.concatenate([grads[share * (1 + wide + n) : share * (2 + wide + n)] for n in range(wide)], axis=1)
    four = (micro, 1, rows, width)
    return (
        layer_output.reshape(four), jnp.stack(token_grad).reshape(four), gq, gbq, gk, gv, gbv, gwo, gbo, gg1, gs1,
        gw1, gb1, gw2, gb2, gg2, gs2,
    )


def solution(mesh):
    rows = P(("ctx", "fsdp"), None)
    flat = P(("ctx", "fsdp"))
    tokens = P(None, "fsdp", "ctx", None)
    params = (rows, flat, rows, rows, flat, rows, flat, flat, flat, rows, flat, rows, flat, flat, flat)
    return jax.shard_map(
        body,
        mesh=mesh,
        in_specs=(tokens, P(None, "fsdp", None), P(None, "fsdp")) + params + (tokens,),
        out_specs=(tokens, tokens) + params,
        check_vma=False,
    )
```

```python
import functools
import math

import jax
import jax.numpy as jnp
from jax import lax
from jax.experimental import pallas as pl
from jax.experimental.pallas import tpu as pltpu
from jax.sharding import PartitionSpec as P

HD = 64
KEY_BLOCK = 128
TILE = 256
SEG_COUNT = 32
FAR = 1e30

def mask_rows(seg_row, reach, first_block):
    n = seg_row.shape[1]
    row = lax.broadcasted_iota(jnp.int32, (HD, n), 0)
    seg = jnp.broadcast_to(seg_row, (HD, n))
    block = lax.broadcasted_iota(jnp.int32, (HD, n), 1) // KEY_BLOCK + first_block
    is_seg = row < SEG_COUNT
    key_at = row - SEG_COUNT
    far = jnp.logical_not(is_seg) & (jnp.abs(key_at - block) >= reach)
    q_side = jnp.where((is_seg & (seg == row)) | far, -FAR, 0.0)
    k_side = jnp.where((is_seg & (seg != row)) | (key_at == block), 1.0, 0.0)
    return q_side.astype(jnp.bfloat16), k_side.astype(jnp.bfloat16)


def token_block(me, s, count, rows):
    return pl.ds(pl.multiple_of(lax.rem(me + s, count) * rows, rows), rows)


def fwd_kernel(heads, count, lo_ref, hi_ref, at_ref, seg_ref, qkv_ref, *refs):
    att_refs, lse_ref, (kaug, qaug, vtr, att, held_s, held_p) = refs[:count], refs[count], refs[count + 1 :]
    reach, me = at_ref[0], at_ref[1]
    length = qkv_ref.shape[1]
    rows, width = length // count, heads * HD

    def prepare(s, _):
        here = pl.ds(pl.multiple_of(s * rows, rows), rows)
        there = token_block(me, s, count, rows)
        q_side, k_side = mask_rows(seg_ref[:, there], reach, lax.rem(me + s, count) * (rows // KEY_BLOCK))
        for h in range(heads):
            q = qkv_ref[h * HD : (h + 1) * HD, here]
            k = qkv_ref[width + h * HD : width + (h + 1) * HD, here]
            qaug[h, 0:HD, there] = (q.astype(jnp.float32) * (1.0 / math.sqrt(HD))).astype(jnp.bfloat16)
            qaug[h, HD : 2 * HD, there] = q_side
            kaug[h, there, :] = jnp.transpose(jnp.concatenate([k, k_side], axis=0))
            vtr[h, :, there] = qkv_ref[2 * width + h * HD : 2 * width + (h + 1) * HD, here]
        return 0
    lax.fori_loop(0, count, prepare, 0)

    def tile(n):
        return pl.ds(pl.multiple_of(n * TILE, TILE), TILE)

    tiles = length // TILE
    for h in range(heads):
        held_s[h] = jnp.dot(kaug[h, tile(lo_ref[0]), :], qaug[h, :, tile(0)], preferred_element_type=jnp.float32)

    def q_step(i, _):
        qs = tile(i)
        first, end = lo_ref[i], hi_ref[i]
        later = jnp.minimum(i + 1, tiles - 1)

        def k_step(j, carry):
            ks, last = tile(j), j + 1 == end
            after, after_q = tile(jnp.where(last, lo_ref[later], j + 1)), tile(jnp.where(last, later, i))
            out, kept = [], None
            def values(h, peak, total, fade, acc, p):
                out.append((peak, total, fade, acc * fade + jnp.dot(vtr[h, :, ks], p, preferred_element_type=jnp.float32)))
            for h in range(heads):
                peak, total, _, acc = carry[h]
                s = held_s[h]
                new = jnp.maximum(peak, jnp.max(s, axis=0, keepdims=True))
                p = jnp.exp(s - new)
                fade = jnp.exp(peak - new)
                total = total * fade + jnp.sum(p, axis=0, keepdims=True)
                held_s[h] = jnp.dot(kaug[h, after, :], qaug[h, :, after_q], preferred_element_type=jnp.float32)
                if h:
                    values(*kept)
                kept = (h, new, total, fade, acc, p.astype(jnp.bfloat16))
            values(*kept)
            return tuple(out)
        row = lambda value: jnp.full((1, TILE), value, jnp.float32)
        start = tuple((row(-3e38), row(0.0), row(0.0), jnp.zeros((HD, TILE), jnp.float32)) for _ in range(heads))
        done = lax.fori_loop(first, end, k_step, start)
        for h in range(heads):
            peak, total, fade, acc = done[h]
            att[h * HD : (h + 1) * HD, qs] = (acc / total).astype(jnp.bfloat16)
            lse_ref[h : h + 1, qs] = peak + jnp.log(total)
        return 0
    lax.fori_loop(0, tiles, q_step, 0)
    for s in range(count):
        att_refs[s][...] = att[:, token_block(me, s, count, rows)]


def attend(qkv, seg, lo, hi, at, heads, count):
    cols, length = qkv.shape
    width, rows = heads * HD, length // count
    whole = lambda shape: pl.BlockSpec(shape, lambda n, *_: (0, 0))
    return pl.pallas_call(
        functools.partial(fwd_kernel, heads, count),
        out_shape=[jax.ShapeDtypeStruct((width, rows), jnp.bfloat16)] * count + [jax.ShapeDtypeStruct((8, length), jnp.float32)],
        grid_spec=pltpu.PrefetchScalarGridSpec(
            num_scalar_prefetch=3, grid=(1,),
            in_specs=[whole((1, length)), whole((cols, length))],
            out_specs=[whole((width, rows))] * count + [whole((8, length))],
            scratch_shapes=[pltpu.VMEM((heads, length, 2 * HD), jnp.bfloat16), pltpu.VMEM((heads, 2 * HD, length), jnp.bfloat16),
                            pltpu.VMEM((heads, HD, length), jnp.bfloat16), pltpu.VMEM((width, length), jnp.bfloat16),
                            pltpu.VMEM((heads, TILE, TILE), jnp.float32), pltpu.VMEM((heads, TILE, TILE), jnp.bfloat16)]),
        compiler_params=pltpu.CompilerParams(dimension_semantics=("arbitrary",), vmem_limit_bytes=40 << 20),
        cost_estimate=pl.CostEstimate(flops=30_000_000_000, bytes_accessed=4_000_000, transcendentals=0),
        name="attend",
    )(lo, hi, at, seg, qkv)


def bwd_kernel(heads, count, lo_ref, hi_ref, at_ref, seg_ref, qkv_ref, lse_ref, *refs):
    att_refs, datt_refs, dqkv_ref = refs[:count], refs[count : 2 * count], refs[2 * count]
    kaug, qaug, v_nat, dotr, ktr, delta, dqt, dkt, dvt, held_s = refs[2 * count + 1 :]
    reach, me = at_ref[0], at_ref[1]
    length = qkv_ref.shape[1]
    rows, width = length // count, heads * HD
    tiles = length // TILE
    scale = 1.0 / math.sqrt(HD)
    f32, bf16 = jnp.float32, jnp.bfloat16
    for s in range(count):
        there = token_block(me, s, count, rows)
        for h in range(heads):
            do, o = datt_refs[s][h * HD : (h + 1) * HD, :], att_refs[s][h * HD : (h + 1) * HD, :]
            dotr[h, :, there] = do
            delta[h, :, there] = jnp.sum(do.astype(f32) * o.astype(f32), axis=0, keepdims=True)

    def prepare(s, _):
        here = pl.ds(pl.multiple_of(s * rows, rows), rows)
        there = token_block(me, s, count, rows)
        q_side, k_side = mask_rows(seg_ref[:, there], reach, lax.rem(me + s, count) * (rows // KEY_BLOCK))
        for h in range(heads):
            q = qkv_ref[h * HD : (h + 1) * HD, here]
            k = qkv_ref[width + h * HD : width + (h + 1) * HD, here]
            qaug[h, 0:HD, there] = (q.astype(f32) * scale).astype(bf16)
            qaug[h, HD : 2 * HD, there] = q_side
            kaug[h, there, :] = jnp.transpose(jnp.concatenate([k, k_side], axis=0))
            ktr[h, :, there] = k
            v_nat[h, there, :] = jnp.transpose(qkv_ref[2 * width + h * HD : 2 * width + (h + 1) * HD, here])
            dqt[h, :, there] = jnp.zeros((HD, rows), f32)
        return 0
    lax.fori_loop(0, count, prepare, 0)

    def tile(n):
        return pl.ds(pl.multiple_of(n * TILE, TILE), TILE)

    def over_queries(left, right):
        return lax.dot_general(left, right, (((1,), (1,)), ((), ())), preferred_element_type=f32)

    for h in range(heads):
        held_s[h] = jnp.dot(kaug[h, tile(0), :], qaug[h, :, tile(lo_ref[0])], preferred_element_type=f32)

    def k_step(j, _):
        ks = tile(j)
        first, end = lo_ref[j], hi_ref[j]
        later = jnp.minimum(j + 1, tiles - 1)
        dkt[...] = jnp.zeros_like(dkt)
        dvt[...] = jnp.zeros_like(dvt)

        def q_step(i, _):
            qs, last = tile(i), i + 1 == end
            after, after_k = tile(jnp.where(last, lo_ref[later], i + 1)), tile(jnp.where(last, later, j))
            def terms(h, p, ds):
                dvt[h] += over_queries(dotr[h, :, qs], p)
                dkt[h] += over_queries(qaug[h, 0:HD, qs], ds)
                dqt[h, :, qs] += jnp.dot(ktr[h, :, ks], ds, preferred_element_type=f32)

            def to_probs(h):
                return jnp.dot(v_nat[h, ks, :], dotr[h, :, qs], preferred_element_type=f32)
            dp, kept = to_probs(0), None
            for h in range(heads):
                ahead = to_probs(h + 1) if h + 1 < heads else None
                p = jnp.exp(held_s[h] - lse_ref[h : h + 1, qs])
                ds = (p * (dp - delta[h, :, qs])).astype(bf16)
                held_s[h] = jnp.dot(kaug[h, after_k, :], qaug[h, :, after], preferred_element_type=f32)
                if h:
                    terms(h - 1, *kept)
                kept, dp = (p.astype(bf16), ds), ahead
            terms(heads - 1, *kept)
            return 0
        lax.fori_loop(first, end, q_step, 0)
        slot = lax.rem(j // (rows // TILE) + count - me, count)
        out = pl.ds(pl.multiple_of(slot * rows + lax.rem(j, rows // TILE) * TILE, TILE), TILE)
        for h in range(heads):
            dqkv_ref[width + h * HD : width + (h + 1) * HD, out] = dkt[h].astype(bf16)
            dqkv_ref[2 * width + h * HD : 2 * width + (h + 1) * HD, out] = dvt[h].astype(bf16)
        return 0
    lax.fori_loop(0, tiles, k_step, 0)

    def finish(s, _):
        here = pl.ds(pl.multiple_of(s * rows, rows), rows)
        there = token_block(me, s, count, rows)
        for h in range(heads):
            dqkv_ref[h * HD : (h + 1) * HD, here] = (dqt[h, :, there] * scale).astype(bf16)
        return 0
    lax.fori_loop(0, count, finish, 0)


def attend_back(qkv, att, datt, lse, seg, lo, hi, at, heads, count):
    cols, length = qkv.shape
    width, rows = heads * HD, length // count
    whole = lambda shape: pl.BlockSpec(shape, lambda n, *_: (0, 0))
    return pl.pallas_call(
        functools.partial(bwd_kernel, heads, count),
        out_shape=jax.ShapeDtypeStruct((cols, length), jnp.bfloat16),
        grid_spec=pltpu.PrefetchScalarGridSpec(
            num_scalar_prefetch=3, grid=(1,),
            in_specs=[whole((1, length)), whole((cols, length)), whole((8, length))] + [whole((width, rows))] * (2 * count),
            out_specs=whole((cols, length)),
            scratch_shapes=[
                pltpu.VMEM((heads, length, 2 * HD), jnp.bfloat16),
                pltpu.VMEM((heads, 2 * HD, length), jnp.bfloat16),
                pltpu.VMEM((heads, length, HD), jnp.bfloat16),
                pltpu.VMEM((heads, HD, length), jnp.bfloat16),
                pltpu.VMEM((heads, HD, length), jnp.bfloat16),
                pltpu.VMEM((heads, 1, length), jnp.float32),
                pltpu.VMEM((heads, HD, length), jnp.float32),
                pltpu.VMEM((heads, HD, TILE), jnp.float32),
                pltpu.VMEM((heads, HD, TILE), jnp.float32),
                pltpu.VMEM((heads, TILE, TILE), jnp.float32)]),
        compiler_params=pltpu.CompilerParams(dimension_semantics=("arbitrary",), vmem_limit_bytes=48 << 20),
        cost_estimate=pl.CostEstimate(flops=30_000_000_000, bytes_accessed=6_000_000, transcendentals=0),
        name="attend_back",
    )(lo, hi, at, seg, qkv, lse, *att, *datt)


def bounds(segments, reach):
    first = segments[:, ::TILE]
    last = segments[:, TILE - 1::TILE]
    n = first.shape[1]
    at = jnp.arange(n)
    per = TILE // KEY_BLOCK
    gap = per * jnp.abs(at[:, None] - at[None, :]) - (per - 1)
    near = gap[None] < reach[:, None, None]
    before = (at[None, :] < at[:, None])[None] & near & (first[:, :, None] == last[:, None, :])
    after = (at[None, :] > at[:, None])[None] & near & (last[:, :, None] == first[:, None, :])
    lo = at[None] - jnp.sum(before, axis=2, dtype=jnp.int32)
    hi = at[None] + 1 + jnp.sum(after, axis=2, dtype=jnp.int32)
    return lo.astype(jnp.int32), hi.astype(jnp.int32)


MESH = pl.DeviceIdType.MESH


def greet(peers):
    barrier = pltpu.get_barrier_semaphore()
    for peer in peers:
        pl.semaphore_signal(barrier, inc=1, device_id=peer, device_id_type=MESH)
    pl.semaphore_wait(barrier, len(peers))


def add_low(left, right):
    return (left.astype(jnp.float32) + right.astype(jnp.float32)).astype(jnp.bfloat16)


class Sends:
    def __init__(self, send_sem, recv_sem):
        self.send_sem, self.recv_sem, self.used, self.open = send_sem, recv_sem, 0, []

    def start(self, src, dst, peer):
        n = self.used
        self.used += 1
        copy = pltpu.make_async_remote_copy(
            src_ref=src, dst_ref=dst, send_sem=self.send_sem.at[n], recv_sem=self.recv_sem.at[n],
            device_id=peer, device_id_type=MESH)
        copy.start()
        self.open.append(copy)
        return copy

    def finish(self):
        for copy in self.open:
            copy.wait_send()


def fold_kernel(zs, heads_in, tokens_in, heads_out, tokens_out, h_own, h_y, h_z, h_c, t_own, t_c, t_x, send_sem, recv_sem, load_sem):
    c, f = lax.axis_index("ctx"), lax.axis_index("fsdp")
    x, core, z, y = c // 2, c % 2, f // 2, f % 2
    partner = {"ctx": x * 2 + (1 - core), "fsdp": f}
    beside = {"ctx": (1 - x) * 2 + core, "fsdp": f}
    above = {"ctx": c, "fsdp": z * 2 + (1 - y)}
    far = [{"ctx": c, "fsdp": lax.rem(z + s, zs) * 2 + y} for s in range(1, zs)]
    across = [{"ctx": lax.rem(c + s, 4), "fsdp": f} for s in range(1, 4)]
    sends = Sends(send_sem, recv_sem)
    greet([above] + far + across)

    near = 1 + 2 * core
    other = 3 - 2 * core
    loads = [pltpu.make_async_copy(tokens_in.at[2], t_own.at[1], load_sem.at[0]),
             pltpu.make_async_copy(heads_in.at[:, :, y], h_own, load_sem.at[1]),
             pltpu.make_async_copy(tokens_in.at[0], t_own.at[0], load_sem.at[2])]
    copy_there = sends.start(tokens_in.at[other], t_c.at[1], partner)
    loads[0].start()
    copy_h = sends.start(heads_in.at[:, :, 1 - y], h_y, above)
    loads[1].start()
    copy_here = sends.start(tokens_in.at[near], t_c.at[0], partner)
    loads[2].start()

    chunks = t_own.shape[1] // 64
    def sum_t(place):
        def step(i, _):
            rows = pl.ds(pl.multiple_of(i * 64, 64), 64)
            t_c[place, rows, :] = add_low(t_own[place, rows, :], t_c[place, rows, :])
            return 0
        lax.fori_loop(0, chunks, step, 0)
    loads[0].wait(), copy_there.wait_recv()
    sum_t(1)
    copy_tx = sends.start(t_c.at[1], t_x, beside)

    loads[1].wait(), copy_h.wait_recv()
    def sum_h(i, _):
        a, b = i // zs, lax.rem(i, zs)
        h_y[a, b] = add_low(h_own[a, b], h_y[a, b])
        return 0
    lax.fori_loop(0, 4 * zs, sum_h, 0)
    copy_hz = [sends.start(h_y.at[:, lax.rem(z + s, zs)], h_z.at[s - 1], far[s - 1]) for s in range(1, zs)]
    loads[2].wait(), copy_here.wait_recv()
    sum_t(0)
    for copy in copy_hz:
        copy.wait_recv()
    def total_h(a, _):
        total = h_y[a, z].astype(jnp.float32)
        for s in range(1, zs):
            total = total + h_z[s - 1, a].astype(jnp.float32)
        h_own[a, 0] = total.astype(jnp.bfloat16)
        return 0
    lax.fori_loop(0, 4, total_h, 0)
    copy_hc = [sends.start(h_own.at[lax.rem(c + s, 4), 0], h_c.at[s - 1], across[s - 1]) for s in range(1, 4)]
    copy_tx.wait_recv()
    def last_t(i, _):
        rows = pl.ds(pl.multiple_of(i * 64, 64), 64)
        tokens_out[rows, :] = t_c[0, rows, :].astype(jnp.float32) + t_x[rows, :].astype(jnp.float32)
        return 0
    lax.fori_loop(0, chunks, last_t, 0)
    heads_out[c] = h_own[c, 0].astype(jnp.float32)
    for s in range(1, 4):
        copy_hc[s - 1].wait_recv()
        heads_out[lax.rem(c + 4 - s, 4)] = h_c[s - 1].astype(jnp.float32)
    sends.finish()


def fold(by_head, tokens):
    ctx, fsdp = lax.axis_size("ctx"), lax.axis_size("fsdp")
    zs = fsdp // 2
    assert ctx == 4 and fsdp % 2 == 0
    f32, bf16 = jnp.float32, jnp.bfloat16
    hr, hw = by_head.shape[1:]
    _, tr, tw = tokens.shape
    copies = 4 + (zs - 1) + 3
    anywhere, vmem = pl.BlockSpec(memory_space=pl.ANY), pl.BlockSpec(memory_space=pltpu.VMEM)
    return pl.pallas_call(
        functools.partial(fold_kernel, zs),
        out_shape=(jax.ShapeDtypeStruct((4, hr, hw), f32), jax.ShapeDtypeStruct((tr, tw), f32)),
        in_specs=[anywhere] * 2, out_specs=[vmem] * 2,
        scratch_shapes=[
            pltpu.VMEM((4, zs, hr, hw), bf16), pltpu.VMEM((4, zs, hr, hw), bf16), pltpu.VMEM((zs - 1, 4, hr, hw), bf16), pltpu.VMEM((3, hr, hw), bf16),
            pltpu.VMEM((2, tr, tw), bf16), pltpu.VMEM((2, tr, tw), bf16), pltpu.VMEM((tr, tw), bf16),
            pltpu.SemaphoreType.DMA((copies,)), pltpu.SemaphoreType.DMA((copies,)), pltpu.SemaphoreType.DMA((3,))],
        compiler_params=pltpu.CompilerParams(collective_id=1, has_side_effects=True, vmem_limit_bytes=63 << 20),
        name="fold",
    )(by_head.reshape(4, zs, 2, hr, hw), tokens)


def collect_kernel(zs, mine, tokens, mine_out, tokens_out, held_mine, held, send_sem, recv_sem, load_sem):
    c, f = lax.axis_index("ctx"), lax.axis_index("fsdp")
    x, core, z, y = c // 2, c % 2, f // 2, f % 2
    partner = {"ctx": x * 2 + (1 - core), "fsdp": f}
    beside = {"ctx": (1 - x) * 2 + core, "fsdp": f}
    above = {"ctx": c, "fsdp": z * 2 + (1 - y)}
    far = [{"ctx": c, "fsdp": lax.rem(z + s, zs) * 2 + y} for s in range(1, zs)]
    across = [{"ctx": lax.rem(c + s, 4), "fsdp": f} for s in range(1, 4)]
    greet([above] + far + across)
    sends = Sends(send_sem, recv_sem)
    loads = [pltpu.make_async_copy(mine.at[c], held_mine, load_sem.at[0]), pltpu.make_async_copy(tokens, held, load_sem.at[1])]
    for copy in loads:
        copy.start()
    first = [sends.start(mine.at[lax.rem(c + s, 4)], mine_out.at[c, z, y], across[s - 1]) for s in range(1, 4)]
    over_x = sends.start(tokens, tokens_out.at[2], beside)
    over_core = sends.start(tokens, tokens_out.at[3 - 2 * core], partner)
    loads[0].wait()
    stores = [pltpu.make_async_copy(held_mine, mine_out.at[c, z, y], load_sem.at[2])]
    stores[0].start()
    loads[1].wait()
    stores.append(pltpu.make_async_copy(held, tokens_out.at[0], load_sem.at[3]))
    stores[1].start()
    for copy in first:
        copy.wait_recv()
    stores[0].wait()
    over_y = sends.start(mine_out.at[:, z, y], mine_out.at[:, z, y], above)
    own_far = [sends.start(mine_out.at[:, z, y], mine_out.at[:, z, y], peer) for peer in far]
    over_x.wait_recv()
    relay = sends.start(tokens_out.at[2], tokens_out.at[1 + 2 * core], partner)
    up_down = []
    for s in range(1, zs):
        own_far[s - 1].wait_recv()
        there = lax.rem(z + zs - s, zs)
        up_down.append(sends.start(mine_out.at[:, there, y], mine_out.at[:, there, y], above))
    for copy in [over_y, over_core, relay] + up_down:
        copy.wait_recv()
    stores[1].wait()
    sends.finish()


def collect(mine, tokens):
    ctx, fsdp = lax.axis_size("ctx"), lax.axis_size("fsdp")
    zs = fsdp // 2
    assert ctx == 4 and fsdp % 2 == 0
    copies = 3 + 1 + 2 * (zs - 1) + 3
    anywhere = pl.BlockSpec(memory_space=pl.ANY)
    return pl.pallas_call(
        functools.partial(collect_kernel, zs),
        out_shape=(jax.ShapeDtypeStruct((4, zs, 2) + mine.shape[1:], mine.dtype), jax.ShapeDtypeStruct((4,) + tokens.shape, tokens.dtype)),
        in_specs=[anywhere] * 2, out_specs=[anywhere] * 2,
        scratch_shapes=[pltpu.VMEM(mine.shape[1:], mine.dtype), pltpu.VMEM(tokens.shape, tokens.dtype), pltpu.SemaphoreType.DMA((copies,)), pltpu.SemaphoreType.DMA((copies,)), pltpu.SemaphoreType.DMA((4,))],
        compiler_params=pltpu.CompilerParams(collective_id=0, has_side_effects=True),
        name="collect",
    )(mine, tokens)


def layer_norm(summed, gain, shift):
    row_mean = jnp.mean(summed, axis=-1, keepdims=True)
    centered = summed - row_mean
    variance = jnp.mean(centered * centered, axis=-1, keepdims=True)
    recip = lax.rsqrt(variance + 1e-05)
    normed = centered * recip
    return (normed * gain + shift, normed, recip)


def norm_back(upstream, normed, recip, gain):
    scaled = upstream * gain
    first_mean = jnp.mean(scaled, axis=-1, keepdims=True)
    second_mean = jnp.mean(scaled * normed, axis=-1, keepdims=True)
    d_summed = recip * (scaled - first_mean - normed * second_mean)
    return (d_summed, jnp.sum(upstream * normed, axis=0), jnp.sum(upstream, axis=0))


def dot(left, right):
    return jnp.dot(left, right, preferred_element_type=jnp.float32)


def weight_term(left, right):
    return jnp.einsum("ta,tb->ab", left, right, preferred_element_type=jnp.float32)


def back_term(grad_low, weight):
    return jnp.einsum("tb,ab->ta", grad_low, weight, preferred_element_type=jnp.float32)


def column_sum(grad_low):
    return jnp.sum(grad_low.astype(jnp.float32), axis=0)


def shift(piece, step):
    count = lax.axis_size("ctx")
    return lax.ppermute(piece, "ctx", [(a, (a + step) % count) for a in range(count)])


def body(
    inputs, segments, block_reach,
    query_weight, query_bias, key_weight, value_weight, value_bias, output_weight, output_bias,
    first_gain, first_shift, expand_weight, expand_bias, contract_weight, contract_bias,
    second_gain, second_shift, output_grad,
):
    every = ("ctx", "fsdp")
    ctx = lax.axis_size("ctx")
    me = lax.axis_index("ctx")
    micro, _, rows, width = inputs.shape
    length = rows * ctx
    cols = width // ctx
    heads = cols // HD
    f32, bf16 = jnp.float32, jnp.bfloat16

    share = query_bias.shape[0]
    lines = 8 + expand_bias.shape[0] // share
    ext = -(-share // 8) * 8
    spare = -(-(3 * cols + lines) // 128) * 128 - 3 * cols
    small = jnp.concatenate([v.reshape(-1, share) for v in (
        query_bias, value_bias, output_bias, first_gain, first_shift, contract_bias, second_gain, second_shift, expand_bias)], axis=0)
    small = jnp.pad(small.T, ((0, 0), (0, spare - lines)))
    split = [jnp.stack([w[:, n * cols : (n + 1) * cols] for n in range(ctx)]) for w in (query_weight, key_weight, value_weight)]
    mine = jnp.concatenate(split + [jnp.broadcast_to(small, (ctx,) + small.shape)], axis=2)
    mine = jnp.pad(mine, ((0, 0), (0, ext - share), (0, 0)))

    wide = expand_weight.shape[1] // width
    packed = jnp.concatenate([output_weight, contract_weight] + [expand_weight[:, n * width : (n + 1) * width] for n in range(wide)], axis=0)
    packed = lax.all_gather(packed, every, axis=0, tiled=True)

    mine_all, tokens_first = collect(mine, inputs[0, 0])
    mine_all = mine_all.reshape(-1, ext, 3 * cols + spare)
    devices = mine_all.shape[0]
    later, mine_all = lax.optimization_barrier((inputs[1:, 0], mine_all))
    tokens_all = [tokens_first.reshape(length, width)]
    for m in range(1, micro):
        tokens_all.append(jnp.concatenate([later[m - 1]] + [shift(later[m - 1], -s) for s in range(1, ctx)], axis=0))
    w_mine = mine_all[:, :share, : 3 * cols].reshape(width, 3 * cols)
    small_all = mine_all[:, :share, 3 * cols : 3 * cols + lines].astype(f32).reshape(width, lines).T
    b_query, b_value, b_output, g_first, s_first, b_contract, g_second, s_second = [small_all[n] for n in range(8)]
    b_expand = small_all[8:].reshape(-1, devices, share).transpose(1, 0, 2).reshape(-1)

    packed = packed.reshape(devices, -1, width)
    back = [lax.rem(me + ctx - s, ctx) for s in range(ctx)]
    by_owner = packed[:, :share].reshape(ctx, cols, width)
    w_output = jnp.concatenate([lax.dynamic_index_in_dim(by_owner, back[s], 0, keepdims=False) for s in range(ctx)], axis=0)
    w_contract = packed[:, share : share + share * wide].reshape(-1, width)
    w_expand = packed[:, share + share * wide :].reshape(devices, wide, share, width).transpose(0, 2, 1, 3).reshape(width, -1)

    own = lambda vec: lax.dynamic_slice_in_dim(vec, me * cols, cols, 0)
    b_mine = jnp.concatenate([own(b_query), jnp.zeros((cols,), f32), own(b_value)])
    seg = segments[:, 0]
    reach = block_reach[:, 0]
    lo, hi = bounds(seg, reach)
    at = [jnp.stack([reach[m], me]) for m in range(micro)]

    qkv, att, lse, attended = [], [], [], []
    for m in range(micro):
        flat = tokens_all[m]
        if m:
            flat, _ = lax.optimization_barrier((flat, lse[-1]))
        projected = jnp.einsum("wc,tw->ct", w_mine, flat, preferred_element_type=f32)
        qkv.append((projected + b_mine[:, None]).astype(bf16))
        *pieces, logs = attend(qkv[m], seg[m : m + 1], lo[m], hi[m], at[m], heads, ctx)
        att.append(pieces), lse.append(logs)
        attended.append(jnp.concatenate([pieces[0]] + [shift(pieces[s], s) for s in range(1, ctx)], axis=0))
    attended = jnp.concatenate(attended, axis=1)

    tokens = inputs[:, 0].reshape(micro * rows, width)
    branch = jnp.einsum("ct,cn->tn", attended, w_output, preferred_element_type=f32) + b_output
    hidden, normed_first, recip_first = layer_norm(tokens.astype(f32) + branch, g_first, s_first)
    hidden_low = hidden.astype(bf16)
    pre = dot(hidden_low, w_expand) + b_expand
    phi = 0.5 * (1.0 + lax.erf(pre * (1.0 / math.sqrt(2.0))))
    act_low = (pre * phi).astype(bf16)
    slope = (phi + pre * (jnp.exp(-0.5 * pre * pre) * (1.0 / math.sqrt(2.0 * math.pi)))).astype(bf16)
    act_low, slope = lax.optimization_barrier((act_low, slope))
    second_sum = hidden + dot(act_low, w_contract) + b_contract
    result, normed_second, recip_second = layer_norm(second_sum, g_second, s_second)
    layer_output = result.astype(bf16)
    upstream = output_grad[:, 0].reshape(micro * rows, width).astype(f32)
    d_res2, grad_g2, grad_s2 = norm_back(upstream, normed_second, recip_second, g_second)
    d_ffn = d_res2.astype(bf16)
    grad_b2 = column_sum(d_ffn)
    d_pre = (back_term(d_ffn, w_contract) * slope.astype(f32)).astype(bf16)
    grad_b1 = column_sum(d_pre)
    d_hidden = d_res2 + back_term(d_pre, w_expand)
    d_res1, grad_g1, grad_s1 = norm_back(d_hidden, normed_first, recip_first, g_first)
    d_branch = d_res1.astype(bf16)
    grad_bo = column_sum(d_branch)
    d_attended = [
        jnp.einsum("cn,tn->ct", w_output, d_branch[m * rows : (m + 1) * rows], preferred_element_type=f32).astype(bf16).reshape(ctx, cols, rows)
        for m in range(micro)]

    *d_attended, d_ffn, d_pre, d_branch = lax.optimization_barrier((*d_attended, d_ffn, d_pre, d_branch))
    d_att = [[d_attended[m][0]] + [shift(d_attended[m][s], -s) for s in range(1, ctx)] for m in range(micro)]
    grad_w2 = weight_term(act_low, d_ffn).astype(bf16).reshape(devices, -1, width)
    grad_w1 = [weight_term(hidden_low, d_pre[:, n * width : (n + 1) * width]).astype(bf16).reshape(devices, share, width) for n in range(wide)]
    grad_wo = dot(attended, d_branch).astype(bf16).reshape(ctx, cols, width)
    grad_wo = jnp.concatenate([lax.dynamic_index_in_dim(grad_wo, back[b], 0, keepdims=False) for b in range(ctx)], axis=0).reshape(devices, share, width)
    grads = jnp.concatenate([grad_wo, grad_w2] + grad_w1, axis=1).reshape(-1, width)
    grads = lax.psum_scatter(grads, every, scatter_dimension=0, tiled=True)

    token_grad, grad_qkv, grad_b = [], 0.0, 0.0
    part = None
    for m in range(micro):
        given = d_att[m]
        if m:
            *given, part = lax.optimization_barrier((*given, part))
            parts = [part[0]] + [shift(part[s], s) for s in range(1, ctx)]
            token_grad.append(sum((p.astype(f32) for p in parts), d_res1[(m - 1) * rows : m * rows]))
        d_qkv = attend_back(qkv[m], att[m], given, lse[m], seg[m : m + 1], lo[m], hi[m], at[m], heads, ctx)
        part = jnp.einsum("ct,nc->tn", d_qkv, w_mine, preferred_element_type=f32).astype(bf16).reshape(ctx, rows, width)
        grad_qkv = grad_qkv + jnp.einsum("tw,ct->wc", tokens_all[m], d_qkv, preferred_element_type=f32)
        grad_b = grad_b + jnp.sum(d_qkv.astype(f32), axis=1)

    place = lambda vec: lax.dynamic_update_slice_in_dim(jnp.zeros((width,), f32), vec, me * cols, 0)
    vectors = [place(grad_b[:cols]), place(grad_b[2 * cols :]), grad_bo, grad_g1, grad_s1, grad_b2, grad_g2, grad_s2]
    stacked = jnp.concatenate([v.reshape(1, width) for v in vectors] + [grad_b1.reshape(devices, -1, share).transpose(1, 0, 2).reshape(-1, width)], axis=0)
    stacked = jnp.pad(stacked.T, ((0, 0), (0, spare - lines)))
    by_head = jnp.concatenate([grad_qkv, stacked], axis=1).astype(bf16).reshape(devices, share, 3 * cols + spare)
    by_head = jnp.pad(by_head, ((0, 0), (0, ext - share), (0, 0)))
    by_head, summed = fold(by_head, part)
    token_grad.append(d_res1[(micro - 1) * rows :] + summed)
    gq, gk, gv = [by_head[:, :share, n * cols : (n + 1) * cols].transpose(1, 0, 2).reshape(share, width) for n in range(3)]
    both = jnp.sum(by_head[:, :share, 3 * cols : 3 * cols + lines], axis=0).T
    gbq, gbv, gbo, gg1, gs1, gb2, gg2, gs2 = [both[n] for n in range(8)]
    gb1 = both[8:].reshape(-1)
    grads = grads.astype(f32)
    gwo, gw2 = grads[:share], grads[share : share + share * wide]
    gw1 = jnp.concatenate([grads[share * (1 + wide + n) : share * (2 + wide + n)] for n in range(wide)], axis=1)
    four = (micro, 1, rows, width)
    return (
        layer_output.reshape(four), jnp.stack(token_grad).reshape(four), gq, gbq, gk, gv, gbv, gwo, gbo, gg1, gs1,
        gw1, gb1, gw2, gb2, gg2, gs2,
    )


def solution(mesh):
    rows = P(("ctx", "fsdp"), None)
    flat = P(("ctx", "fsdp"))
    tokens = P(None, "fsdp", "ctx", None)
    params = (rows, flat, rows, rows, flat, rows, flat, flat, flat, rows, flat, rows, flat, flat, flat)
    return jax.shard_map(
        body,
        mesh=mesh,
        in_specs=(tokens, P(None, "fsdp", None), P(None, "fsdp")) + params + (tokens,),
        out_specs=(tokens, tokens) + params,
        check_vma=False,
    )
```

```python
import functools
import math

import jax
import jax.numpy as jnp
from jax import lax
from jax.experimental import pallas as pl
from jax.experimental.pallas import tpu as pltpu
from jax.sharding import PartitionSpec as P

HD = 64
KEY_BLOCK = 128
TILE = 256
SEG_COUNT = 32
FAR = 1e30

def mask_rows(seg_row, reach, first_block):
    n = seg_row.shape[1]
    row = lax.broadcasted_iota(jnp.int32, (HD, n), 0)
    seg = jnp.broadcast_to(seg_row, (HD, n))
    block = lax.broadcasted_iota(jnp.int32, (HD, n), 1) // KEY_BLOCK + first_block
    is_seg = row < SEG_COUNT
    key_at = row - SEG_COUNT
    far = jnp.logical_not(is_seg) & (jnp.abs(key_at - block) >= reach)
    q_side = jnp.where((is_seg & (seg == row)) | far, -FAR, 0.0)
    k_side = jnp.where((is_seg & (seg != row)) | (key_at == block), 1.0, 0.0)
    return q_side.astype(jnp.bfloat16), k_side.astype(jnp.bfloat16)


def token_block(me, s, count, rows):
    return pl.ds(pl.multiple_of(lax.rem(me + s, count) * rows, rows), rows)


def fwd_kernel(heads, count, lo_ref, hi_ref, at_ref, seg_ref, qkv_ref, *refs):
    att_refs, lse_ref, (kaug, qaug, vtr, att, held_s, held_p) = refs[:count], refs[count], refs[count + 1 :]
    reach, me = at_ref[0], at_ref[1]
    length = qkv_ref.shape[1]
    rows, width = length // count, heads * HD

    def prepare(s, _):
        here = pl.ds(pl.multiple_of(s * rows, rows), rows)
        there = token_block(me, s, count, rows)
        q_side, k_side = mask_rows(seg_ref[:, there], reach, lax.rem(me + s, count) * (rows // KEY_BLOCK))
        for h in range(heads):
            q = qkv_ref[h * HD : (h + 1) * HD, here]
            k = qkv_ref[width + h * HD : width + (h + 1) * HD, here]
            qaug[h, 0:HD, there] = (q.astype(jnp.float32) * (1.0 / math.sqrt(HD))).astype(jnp.bfloat16)
            qaug[h, HD : 2 * HD, there] = q_side
            kaug[h, there, :] = jnp.transpose(jnp.concatenate([k, k_side], axis=0))
            vtr[h, :, there] = qkv_ref[2 * width + h * HD : 2 * width + (h + 1) * HD, here]
        return 0
    lax.fori_loop(0, count, prepare, 0)

    def tile(n):
        return pl.ds(pl.multiple_of(n * TILE, TILE), TILE)

    tiles = length // TILE
    for h in range(heads):
        held_s[h] = jnp.dot(kaug[h, tile(lo_ref[0]), :], qaug[h, :, tile(0)], preferred_element_type=jnp.float32)

    def q_step(i, _):
        qs = tile(i)
        first, end = lo_ref[i], hi_ref[i]
        later = jnp.minimum(i + 1, tiles - 1)

        def k_step(j, carry):
            ks, last = tile(j), j + 1 == end
            after, after_q = tile(jnp.where(last, lo_ref[later], j + 1)), tile(jnp.where(last, later, i))
            out, kept = [], None
            def values(h, peak, total, fade, acc, p):
                out.append((peak, total, fade, acc * fade + jnp.dot(vtr[h, :, ks], p, preferred_element_type=jnp.float32)))
            for h in range(heads):
                peak, total, _, acc = carry[h]
                s = held_s[h]
                new = jnp.maximum(peak, jnp.max(s, axis=0, keepdims=True))
                p = jnp.exp(s - new)
                fade = jnp.exp(peak - new)
                total = total * fade + jnp.sum(p, axis=0, keepdims=True)
                held_s[h] = jnp.dot(kaug[h, after, :], qaug[h, :, after_q], preferred_element_type=jnp.float32)
                if h:
                    values(*kept)
                kept = (h, new, total, fade, acc, p.astype(jnp.bfloat16))
            values(*kept)
            return tuple(out)
        row = lambda value: jnp.full((1, TILE), value, jnp.float32)
        start = tuple((row(-3e38), row(0.0), row(0.0), jnp.zeros((HD, TILE), jnp.float32)) for _ in range(heads))
        done = lax.fori_loop(first, end, k_step, start)
        for h in range(heads):
            peak, total, fade, acc = done[h]
            att[h * HD : (h + 1) * HD, qs] = (acc / total).astype(jnp.bfloat16)
            lse_ref[h : h + 1, qs] = peak + jnp.log(total)
        return 0
    lax.fori_loop(0, tiles, q_step, 0)
    for s in range(count):
        att_refs[s][...] = att[:, token_block(me, s, count, rows)]


def attend(qkv, seg, lo, hi, at, heads, count):
    cols, length = qkv.shape
    width, rows = heads * HD, length // count
    whole = lambda shape: pl.BlockSpec(shape, lambda n, *_: (0, 0))
    return pl.pallas_call(
        functools.partial(fwd_kernel, heads, count),
        out_shape=[jax.ShapeDtypeStruct((width, rows), jnp.bfloat16)] * count + [jax.ShapeDtypeStruct((8, length), jnp.float32)],
        grid_spec=pltpu.PrefetchScalarGridSpec(
            num_scalar_prefetch=3, grid=(1,),
            in_specs=[whole((1, length)), whole((cols, length))],
            out_specs=[whole((width, rows))] * count + [whole((8, length))],
            scratch_shapes=[pltpu.VMEM((heads, length, 2 * HD), jnp.bfloat16), pltpu.VMEM((heads, 2 * HD, length), jnp.bfloat16),
                            pltpu.VMEM((heads, HD, length), jnp.bfloat16), pltpu.VMEM((width, length), jnp.bfloat16),
                            pltpu.VMEM((heads, TILE, TILE), jnp.float32), pltpu.VMEM((heads, TILE, TILE), jnp.bfloat16)]),
        compiler_params=pltpu.CompilerParams(dimension_semantics=("arbitrary",), vmem_limit_bytes=40 << 20),
        cost_estimate=pl.CostEstimate(flops=30_000_000_000, bytes_accessed=4_000_000, transcendentals=0),
        name="attend",
    )(lo, hi, at, seg, qkv)


def bwd_kernel(heads, count, lo_ref, hi_ref, at_ref, seg_ref, qkv_ref, lse_ref, *refs):
    att_refs, datt_refs, dqkv_ref = refs[:count], refs[count : 2 * count], refs[2 * count]
    kaug, qaug, v_nat, dotr, ktr, delta, dqt, dkt, dvt, held_s = refs[2 * count + 1 :]
    reach, me = at_ref[0], at_ref[1]
    length = qkv_ref.shape[1]
    rows, width = length // count, heads * HD
    tiles = length // TILE
    scale = 1.0 / math.sqrt(HD)
    f32, bf16 = jnp.float32, jnp.bfloat16
    for s in range(count):
        there = token_block(me, s, count, rows)
        for h in range(heads):
            do, o = datt_refs[s][h * HD : (h + 1) * HD, :], att_refs[s][h * HD : (h + 1) * HD, :]
            dotr[h, :, there] = do
            delta[h, :, there] = jnp.sum(do.astype(f32) * o.astype(f32), axis=0, keepdims=True)

    def prepare(s, _):
        here = pl.ds(pl.multiple_of(s * rows, rows), rows)
        there = token_block(me, s, count, rows)
        q_side, k_side = mask_rows(seg_ref[:, there], reach, lax.rem(me + s, count) * (rows // KEY_BLOCK))
        for h in range(heads):
            q = qkv_ref[h * HD : (h + 1) * HD, here]
            k = qkv_ref[width + h * HD : width + (h + 1) * HD, here]
            qaug[h, 0:HD, there] = (q.astype(f32) * scale).astype(bf16)
            qaug[h, HD : 2 * HD, there] = q_side
            kaug[h, there, :] = jnp.transpose(jnp.concatenate([k, k_side], axis=0))
            ktr[h, :, there] = k
            v_nat[h, there, :] = jnp.transpose(qkv_ref[2 * width + h * HD : 2 * width + (h + 1) * HD, here])
            dqt[h, :, there] = jnp.zeros((HD, rows), f32)
        return 0
    lax.fori_loop(0, count, prepare, 0)

    def tile(n):
        return pl.ds(pl.multiple_of(n * TILE, TILE), TILE)

    def over_queries(left, right):
        return lax.dot_general(left, right, (((1,), (1,)), ((), ())), preferred_element_type=f32)

    for h in range(heads):
        held_s[h] = jnp.dot(kaug[h, tile(0), :], qaug[h, :, tile(lo_ref[0])], preferred_element_type=f32)

    def k_step(j, _):
        ks = tile(j)
        first, end = lo_ref[j], hi_ref[j]
        later = jnp.minimum(j + 1, tiles - 1)
        dkt[...] = jnp.zeros_like(dkt)
        dvt[...] = jnp.zeros_like(dvt)

        def q_step(i, _):
            qs, last = tile(i), i + 1 == end
            after, after_k = tile(jnp.where(last, lo_ref[later], i + 1)), tile(jnp.where(last, later, j))
            def terms(h, p, ds):
                dvt[h] += over_queries(dotr[h, :, qs], p)
                dkt[h] += over_queries(qaug[h, 0:HD, qs], ds)
                dqt[h, :, qs] += jnp.dot(ktr[h, :, ks], ds, preferred_element_type=f32)

            def to_probs(h):
                return jnp.dot(v_nat[h, ks, :], dotr[h, :, qs], preferred_element_type=f32)
            dp, kept = to_probs(0), None
            for h in range(heads):
                ahead = to_probs(h + 1) if h + 1 < heads else None
                p = jnp.exp(held_s[h] - lse_ref[h : h + 1, qs])
                ds = (p * (dp - delta[h, :, qs])).astype(bf16)
                held_s[h] = jnp.dot(kaug[h, after_k, :], qaug[h, :, after], preferred_element_type=f32)
                if h:
                    terms(h - 1, *kept)
                kept, dp = (p.astype(bf16), ds), ahead
            terms(heads - 1, *kept)
            return 0
        lax.fori_loop(first, end, q_step, 0)
        slot = lax.rem(j // (rows // TILE) + count - me, count)
        out = pl.ds(pl.multiple_of(slot * rows + lax.rem(j, rows // TILE) * TILE, TILE), TILE)
        for h in range(heads):
            dqkv_ref[width + h * HD : width + (h + 1) * HD, out] = dkt[h].astype(bf16)
            dqkv_ref[2 * width + h * HD : 2 * width + (h + 1) * HD, out] = dvt[h].astype(bf16)
        return 0
    lax.fori_loop(0, tiles, k_step, 0)

    def finish(s, _):
        here = pl.ds(pl.multiple_of(s * rows, rows), rows)
        there = token_block(me, s, count, rows)
        for h in range(heads):
            dqkv_ref[h * HD : (h + 1) * HD, here] = (dqt[h, :, there] * scale).astype(bf16)
        return 0
    lax.fori_loop(0, count, finish, 0)


def attend_back(qkv, att, datt, lse, seg, lo, hi, at, heads, count):
    cols, length = qkv.shape
    width, rows = heads * HD, length // count
    whole = lambda shape: pl.BlockSpec(shape, lambda n, *_: (0, 0))
    return pl.pallas_call(
        functools.partial(bwd_kernel, heads, count),
        out_shape=jax.ShapeDtypeStruct((cols, length), jnp.bfloat16),
        grid_spec=pltpu.PrefetchScalarGridSpec(
            num_scalar_prefetch=3, grid=(1,),
            in_specs=[whole((1, length)), whole((cols, length)), whole((8, length))] + [whole((width, rows))] * (2 * count),
            out_specs=whole((cols, length)),
            scratch_shapes=[
                pltpu.VMEM((heads, length, 2 * HD), jnp.bfloat16),
                pltpu.VMEM((heads, 2 * HD, length), jnp.bfloat16),
                pltpu.VMEM((heads, length, HD), jnp.bfloat16),
                pltpu.VMEM((heads, HD, length), jnp.bfloat16),
                pltpu.VMEM((heads, HD, length), jnp.bfloat16),
                pltpu.VMEM((heads, 1, length), jnp.float32),
                pltpu.VMEM((heads, HD, length), jnp.float32),
                pltpu.VMEM((heads, HD, TILE), jnp.float32),
                pltpu.VMEM((heads, HD, TILE), jnp.float32),
                pltpu.VMEM((heads, TILE, TILE), jnp.float32)]),
        compiler_params=pltpu.CompilerParams(dimension_semantics=("arbitrary",), vmem_limit_bytes=48 << 20),
        cost_estimate=pl.CostEstimate(flops=30_000_000_000, bytes_accessed=6_000_000, transcendentals=0),
        name="attend_back",
    )(lo, hi, at, seg, qkv, lse, *att, *datt)


def bounds(segments, reach):
    first = segments[:, ::TILE]
    last = segments[:, TILE - 1::TILE]
    n = first.shape[1]
    at = jnp.arange(n)
    per = TILE // KEY_BLOCK
    gap = per * jnp.abs(at[:, None] - at[None, :]) - (per - 1)
    near = gap[None] < reach[:, None, None]
    before = (at[None, :] < at[:, None])[None] & near & (first[:, :, None] == last[:, None, :])
    after = (at[None, :] > at[:, None])[None] & near & (last[:, :, None] == first[:, None, :])
    lo = at[None] - jnp.sum(before, axis=2, dtype=jnp.int32)
    hi = at[None] + 1 + jnp.sum(after, axis=2, dtype=jnp.int32)
    return lo.astype(jnp.int32), hi.astype(jnp.int32)


MESH = pl.DeviceIdType.MESH


def greet(peers):
    barrier = pltpu.get_barrier_semaphore()
    for peer in peers:
        pl.semaphore_signal(barrier, inc=1, device_id=peer, device_id_type=MESH)
    pl.semaphore_wait(barrier, len(peers))


def add_low(left, right):
    return (left.astype(jnp.float32) + right.astype(jnp.float32)).astype(jnp.bfloat16)


class Sends:
    def __init__(self, send_sem, recv_sem):
        self.send_sem, self.recv_sem, self.used, self.open = send_sem, recv_sem, 0, []

    def start(self, src, dst, peer):
        n = self.used
        self.used += 1
        copy = pltpu.make_async_remote_copy(
            src_ref=src, dst_ref=dst, send_sem=self.send_sem.at[n], recv_sem=self.recv_sem.at[n],
            device_id=peer, device_id_type=MESH)
        copy.start()
        self.open.append(copy)
        return copy

    def finish(self):
        for copy in self.open:
            copy.wait_send()


def fold_kernel(zs, micro, heads_in, *refs):
    tokens_in, heads_out, tokens_out = refs[:micro], refs[micro], refs[micro + 1 : 2 * micro + 1]
    h_own, h_y, h_z, h_c, t_own, t_c, t_x, send_sem, recv_sem, load_sem = refs[2 * micro + 1 :]
    c, f = lax.axis_index("ctx"), lax.axis_index("fsdp")
    x, core, z, y = c // 2, c % 2, f // 2, f % 2
    partner = {"ctx": x * 2 + (1 - core), "fsdp": f}
    beside = {"ctx": (1 - x) * 2 + core, "fsdp": f}
    above = {"ctx": c, "fsdp": z * 2 + (1 - y)}
    far = [{"ctx": c, "fsdp": lax.rem(z + s, zs) * 2 + y} for s in range(1, zs)]
    across = [{"ctx": lax.rem(c + s, 4), "fsdp": f} for s in range(1, 4)]
    sends = Sends(send_sem, recv_sem)
    greet([above] + far + across)

    near = 1 + 2 * core
    other = 3 - 2 * core
    loads = []
    def load(src, dst):
        loads.append(pltpu.make_async_copy(src, dst, load_sem.at[len(loads)]))
        loads[-1].start()
        return loads[-1]
    load_there, copy_there, load_here, copy_here = [], [], [], []
    for m in range(micro):
        copy_there.append(sends.start(tokens_in[m].at[other], t_c.at[m, 1], partner))
        load_there.append(load(tokens_in[m].at[2], t_own.at[m, 1]))
    copy_h = sends.start(heads_in.at[:, :, 1 - y], h_y, above)
    load_h = load(heads_in.at[:, :, y], h_own)
    for m in range(micro):
        copy_here.append(sends.start(tokens_in[m].at[near], t_c.at[m, 0], partner))
        load_here.append(load(tokens_in[m].at[0], t_own.at[m, 0]))

    chunks = t_own.shape[2] // 64
    def sum_t(m, place):
        def step(i, _):
            rows = pl.ds(pl.multiple_of(i * 64, 64), 64)
            t_c[m, place, rows, :] = add_low(t_own[m, place, rows, :], t_c[m, place, rows, :])
            return 0
        lax.fori_loop(0, chunks, step, 0)
    copy_tx = []
    for m in range(micro):
        load_there[m].wait(), copy_there[m].wait_recv()
        sum_t(m, 1)
        copy_tx.append(sends.start(t_c.at[m, 1], t_x.at[m], beside))

    load_h.wait(), copy_h.wait_recv()
    def sum_h(i, _):
        a, b = i // zs, lax.rem(i, zs)
        h_y[a, b] = add_low(h_own[a, b], h_y[a, b])
        return 0
    lax.fori_loop(0, 4 * zs, sum_h, 0)
    copy_hz = [sends.start(h_y.at[:, lax.rem(z + s, zs)], h_z.at[s - 1], far[s - 1]) for s in range(1, zs)]
    for m in range(micro):
        load_here[m].wait(), copy_here[m].wait_recv()
        sum_t(m, 0)
    for copy in copy_hz:
        copy.wait_recv()
    def total_h(a, _):
        total = h_y[a, z].astype(jnp.float32)
        for s in range(1, zs):
            total = total + h_z[s - 1, a].astype(jnp.float32)
        h_own[a, 0] = total.astype(jnp.bfloat16)
        return 0
    lax.fori_loop(0, 4, total_h, 0)
    copy_hc = [sends.start(h_own.at[lax.rem(c + s, 4), 0], h_c.at[s - 1], across[s - 1]) for s in range(1, 4)]
    for m in range(micro):
        copy_tx[m].wait_recv()
        def last_t(i, _, m=m):
            rows = pl.ds(pl.multiple_of(i * 64, 64), 64)
            tokens_out[m][rows, :] = t_c[m, 0, rows, :].astype(jnp.float32) + t_x[m, rows, :].astype(jnp.float32)
            return 0
        lax.fori_loop(0, chunks, last_t, 0)
    heads_out[c] = h_own[c, 0].astype(jnp.float32)
    for s in range(1, 4):
        copy_hc[s - 1].wait_recv()
        heads_out[lax.rem(c + 4 - s, 4)] = h_c[s - 1].astype(jnp.float32)
    sends.finish()


def fold(by_head, tokens):
    ctx, fsdp = lax.axis_size("ctx"), lax.axis_size("fsdp")
    zs = fsdp // 2
    assert ctx == 4 and fsdp % 2 == 0
    f32, bf16 = jnp.float32, jnp.bfloat16
    hr, hw = by_head.shape[1:]
    micro = len(tokens)
    _, tr, tw = tokens[0].shape
    copies = 3 * micro + 1 + (zs - 1) + 3
    anywhere, vmem = pl.BlockSpec(memory_space=pl.ANY), pl.BlockSpec(memory_space=pltpu.VMEM)
    return pl.pallas_call(
        functools.partial(fold_kernel, zs, micro),
        out_shape=[jax.ShapeDtypeStruct((4, hr, hw), f32)] + [jax.ShapeDtypeStruct((tr, tw), f32)] * micro,
        in_specs=[anywhere] * (1 + micro), out_specs=[vmem] * (1 + micro),
        scratch_shapes=[
            pltpu.VMEM((4, zs, hr, hw), bf16), pltpu.VMEM((4, zs, hr, hw), bf16), pltpu.VMEM((zs - 1, 4, hr, hw), bf16), pltpu.VMEM((3, hr, hw), bf16),
            pltpu.VMEM((micro, 2, tr, tw), bf16), pltpu.VMEM((micro, 2, tr, tw), bf16), pltpu.VMEM((micro, tr, tw), bf16),
            pltpu.SemaphoreType.DMA((copies,)), pltpu.SemaphoreType.DMA((copies,)), pltpu.SemaphoreType.DMA((1 + 2 * micro,))],
        compiler_params=pltpu.CompilerParams(collective_id=1, has_side_effects=True, vmem_limit_bytes=63 << 20),
        name="fold",
    )(by_head.reshape(4, zs, 2, hr, hw), *tokens)


def collect_kernel(zs, micro, mine, tokens, mine_out, *refs):
    tokens_out, (held_mine, held, send_sem, recv_sem, load_sem) = refs[:micro], refs[micro:]
    c, f = lax.axis_index("ctx"), lax.axis_index("fsdp")
    x, core, z, y = c // 2, c % 2, f // 2, f % 2
    partner = {"ctx": x * 2 + (1 - core), "fsdp": f}
    beside = {"ctx": (1 - x) * 2 + core, "fsdp": f}
    above = {"ctx": c, "fsdp": z * 2 + (1 - y)}
    far = [{"ctx": c, "fsdp": lax.rem(z + s, zs) * 2 + y} for s in range(1, zs)]
    across = [{"ctx": lax.rem(c + s, 4), "fsdp": f} for s in range(1, 4)]
    greet([above] + far + across)
    sends = Sends(send_sem, recv_sem)
    loads = [pltpu.make_async_copy(mine.at[c], held_mine, load_sem.at[0]), pltpu.make_async_copy(tokens, held, load_sem.at[1])]
    for copy in loads:
        copy.start()
    first = [sends.start(mine.at[lax.rem(c + s, 4)], mine_out.at[c, z, y], across[s - 1]) for s in range(1, 4)]
    over_x = [sends.start(tokens.at[m], tokens_out[m].at[2], beside) for m in range(micro)]
    over_core = [sends.start(tokens.at[m], tokens_out[m].at[3 - 2 * core], partner) for m in range(micro)]
    loads[0].wait()
    stores = [pltpu.make_async_copy(held_mine, mine_out.at[c, z, y], load_sem.at[2])]
    stores[0].start()
    loads[1].wait()
    for m in range(micro):
        stores.append(pltpu.make_async_copy(held.at[m], tokens_out[m].at[0], load_sem.at[3 + m]))
        stores[-1].start()
    for copy in first:
        copy.wait_recv()
    stores[0].wait()
    over_y = sends.start(mine_out.at[:, z, y], mine_out.at[:, z, y], above)
    own_far = [sends.start(mine_out.at[:, z, y], mine_out.at[:, z, y], peer) for peer in far]
    up_down = []
    for s in range(1, zs):
        own_far[s - 1].wait_recv()
        there = lax.rem(z + zs - s, zs)
        up_down.append(sends.start(mine_out.at[:, there, y], mine_out.at[:, there, y], above))
    relay = []
    for m in range(micro):
        over_x[m].wait_recv()
        relay.append(sends.start(tokens_out[m].at[2], tokens_out[m].at[1 + 2 * core], partner))
    for copy in [over_y] + over_core + up_down + relay:
        copy.wait_recv()
    for copy in stores[1:]:
        copy.wait()
    sends.finish()


def collect(mine, tokens):
    ctx, fsdp = lax.axis_size("ctx"), lax.axis_size("fsdp")
    zs = fsdp // 2
    assert ctx == 4 and fsdp % 2 == 0
    micro = tokens.shape[0]
    copies = 3 + 1 + 2 * (zs - 1) + 3 * micro
    anywhere = pl.BlockSpec(memory_space=pl.ANY)
    return pl.pallas_call(
        functools.partial(collect_kernel, zs, micro),
        out_shape=[jax.ShapeDtypeStruct((4, zs, 2) + mine.shape[1:], mine.dtype)] + [jax.ShapeDtypeStruct((4,) + tokens.shape[1:], tokens.dtype)] * micro,
        in_specs=[anywhere] * 2, out_specs=[anywhere] * (1 + micro),
        scratch_shapes=[pltpu.VMEM(mine.shape[1:], mine.dtype), pltpu.VMEM(tokens.shape, tokens.dtype), pltpu.SemaphoreType.DMA((copies,)), pltpu.SemaphoreType.DMA((copies,)), pltpu.SemaphoreType.DMA((3 + micro,))],
        compiler_params=pltpu.CompilerParams(collective_id=0, has_side_effects=True),
        name="collect",
    )(mine, tokens)


def layer_norm(summed, gain, shift):
    row_mean = jnp.mean(summed, axis=-1, keepdims=True)
    centered = summed - row_mean
    variance = jnp.mean(centered * centered, axis=-1, keepdims=True)
    recip = lax.rsqrt(variance + 1e-05)
    normed = centered * recip
    return (normed * gain + shift, normed, recip)


def norm_back(upstream, normed, recip, gain):
    scaled = upstream * gain
    first_mean = jnp.mean(scaled, axis=-1, keepdims=True)
    second_mean = jnp.mean(scaled * normed, axis=-1, keepdims=True)
    d_summed = recip * (scaled - first_mean - normed * second_mean)
    return (d_summed, jnp.sum(upstream * normed, axis=0), jnp.sum(upstream, axis=0))


def dot(left, right):
    return jnp.dot(left, right, preferred_element_type=jnp.float32)


def weight_term(left, right):
    return jnp.einsum("ta,tb->ab", left, right, preferred_element_type=jnp.float32)


def back_term(grad_low, weight):
    return jnp.einsum("tb,ab->ta", grad_low, weight, preferred_element_type=jnp.float32)


def column_sum(grad_low):
    return jnp.sum(grad_low.astype(jnp.float32), axis=0)


def shift(piece, step):
    count = lax.axis_size("ctx")
    return lax.ppermute(piece, "ctx", [(a, (a + step) % count) for a in range(count)])


def body(
    inputs, segments, block_reach,
    query_weight, query_bias, key_weight, value_weight, value_bias, output_weight, output_bias,
    first_gain, first_shift, expand_weight, expand_bias, contract_weight, contract_bias,
    second_gain, second_shift, output_grad,
):
    every = ("ctx", "fsdp")
    ctx = lax.axis_size("ctx")
    me = lax.axis_index("ctx")
    micro, _, rows, width = inputs.shape
    length = rows * ctx
    cols = width // ctx
    heads = cols // HD
    f32, bf16 = jnp.float32, jnp.bfloat16

    share = query_bias.shape[0]
    lines = 8 + expand_bias.shape[0] // share
    ext = -(-share // 8) * 8
    spare = -(-(3 * cols + lines) // 128) * 128 - 3 * cols
    small = jnp.concatenate([v.reshape(-1, share) for v in (
        query_bias, value_bias, output_bias, first_gain, first_shift, contract_bias, second_gain, second_shift, expand_bias)], axis=0)
    small = jnp.pad(small.T, ((0, 0), (0, spare - lines)))
    split = [jnp.stack([w[:, n * cols : (n + 1) * cols] for n in range(ctx)]) for w in (query_weight, key_weight, value_weight)]
    mine = jnp.concatenate(split + [jnp.broadcast_to(small, (ctx,) + small.shape)], axis=2)
    mine = jnp.pad(mine, ((0, 0), (0, ext - share), (0, 0)))

    wide = expand_weight.shape[1] // width
    packed = jnp.concatenate([output_weight, contract_weight] + [expand_weight[:, n * width : (n + 1) * width] for n in range(wide)], axis=0)
    packed = lax.all_gather(packed, every, axis=0, tiled=True)

    mine_all, *tokens_all = collect(mine, inputs[:, 0])
    tokens_all = [t.reshape(length, width) for t in tokens_all]
    mine_all = mine_all.reshape(-1, ext, 3 * cols + spare)
    devices = mine_all.shape[0]
    w_mine = mine_all[:, :share, : 3 * cols].reshape(width, 3 * cols)
    small_all = mine_all[:, :share, 3 * cols : 3 * cols + lines].astype(f32).reshape(width, lines).T
    b_query, b_value, b_output, g_first, s_first, b_contract, g_second, s_second = [small_all[n] for n in range(8)]
    b_expand = small_all[8:].reshape(-1, devices, share).transpose(1, 0, 2).reshape(-1)

    packed = packed.reshape(devices, -1, width)
    back = [lax.rem(me + ctx - s, ctx) for s in range(ctx)]
    by_owner = packed[:, :share].reshape(ctx, cols, width)
    w_output = jnp.concatenate([lax.dynamic_index_in_dim(by_owner, back[s], 0, keepdims=False) for s in range(ctx)], axis=0)
    w_contract = packed[:, share : share + share * wide].reshape(-1, width)
    w_expand = packed[:, share + share * wide :].reshape(devices, wide, share, width).transpose(0, 2, 1, 3).reshape(width, -1)

    own = lambda vec: lax.dynamic_slice_in_dim(vec, me * cols, cols, 0)
    b_mine = jnp.concatenate([own(b_query), jnp.zeros((cols,), f32), own(b_value)])
    seg = segments[:, 0]
    reach = block_reach[:, 0]
    lo, hi = bounds(seg, reach)
    at = [jnp.stack([reach[m], me]) for m in range(micro)]

    qkv, att, lse, attended = [], [], [], []
    for m in range(micro):
        flat = tokens_all[m]
        if m:
            flat, _ = lax.optimization_barrier((flat, lse[-1]))
        projected = jnp.einsum("wc,tw->ct", w_mine, flat, preferred_element_type=f32)
        qkv.append((projected + b_mine[:, None]).astype(bf16))
        *pieces, logs = attend(qkv[m], seg[m : m + 1], lo[m], hi[m], at[m], heads, ctx)
        att.append(pieces), lse.append(logs)
        attended.append(jnp.concatenate([pieces[0]] + [shift(pieces[s], s) for s in range(1, ctx)], axis=0))
    attended = jnp.concatenate(attended, axis=1)

    tokens = inputs[:, 0].reshape(micro * rows, width)
    branch = jnp.einsum("ct,cn->tn", attended, w_output, preferred_element_type=f32) + b_output
    hidden, normed_first, recip_first = layer_norm(tokens.astype(f32) + branch, g_first, s_first)
    hidden_low = hidden.astype(bf16)
    pre = dot(hidden_low, w_expand) + b_expand
    phi = 0.5 * (1.0 + lax.erf(pre * (1.0 / math.sqrt(2.0))))
    act_low = (pre * phi).astype(bf16)
    slope = (phi + pre * (jnp.exp(-0.5 * pre * pre) * (1.0 / math.sqrt(2.0 * math.pi)))).astype(bf16)
    act_low, slope = lax.optimization_barrier((act_low, slope))
    second_sum = hidden + dot(act_low, w_contract) + b_contract
    result, normed_second, recip_second = layer_norm(second_sum, g_second, s_second)
    layer_output = result.astype(bf16)
    upstream = output_grad[:, 0].reshape(micro * rows, width).astype(f32)
    d_res2, grad_g2, grad_s2 = norm_back(upstream, normed_second, recip_second, g_second)
    d_ffn = d_res2.astype(bf16)
    grad_b2 = column_sum(d_ffn)
    d_pre = (back_term(d_ffn, w_contract) * slope.astype(f32)).astype(bf16)
    grad_b1 = column_sum(d_pre)
    d_hidden = d_res2 + back_term(d_pre, w_expand)
    d_res1, grad_g1, grad_s1 = norm_back(d_hidden, normed_first, recip_first, g_first)
    d_branch = d_res1.astype(bf16)
    grad_bo = column_sum(d_branch)
    d_attended = [
        jnp.einsum("cn,tn->ct", w_output, d_branch[m * rows : (m + 1) * rows], preferred_element_type=f32).astype(bf16).reshape(ctx, cols, rows)
        for m in range(micro)]

    *d_attended, d_ffn, d_pre, d_branch = lax.optimization_barrier((*d_attended, d_ffn, d_pre, d_branch))
    d_att = [[d_attended[m][0]] + [shift(d_attended[m][s], -s) for s in range(1, ctx)] for m in range(micro)]
    grad_w2 = weight_term(act_low, d_ffn).astype(bf16).reshape(devices, -1, width)
    grad_w1 = [weight_term(hidden_low, d_pre[:, n * width : (n + 1) * width]).astype(bf16).reshape(devices, share, width) for n in range(wide)]
    grad_wo = dot(attended, d_branch).astype(bf16).reshape(ctx, cols, width)
    grad_wo = jnp.concatenate([lax.dynamic_index_in_dim(grad_wo, back[b], 0, keepdims=False) for b in range(ctx)], axis=0).reshape(devices, share, width)
    grads = jnp.concatenate([grad_wo, grad_w2] + grad_w1, axis=1).reshape(-1, width)
    grads = lax.psum_scatter(grads, every, scatter_dimension=0, tiled=True)

    parts, grad_qkv, grad_b = [], 0.0, 0.0
    for m in range(micro):
        d_qkv = attend_back(qkv[m], att[m], d_att[m], lse[m], seg[m : m + 1], lo[m], hi[m], at[m], heads, ctx)
        parts.append(jnp.einsum("ct,nc->tn", d_qkv, w_mine, preferred_element_type=f32).astype(bf16).reshape(ctx, rows, width))
        grad_qkv = grad_qkv + jnp.einsum("tw,ct->wc", tokens_all[m], d_qkv, preferred_element_type=f32)
        grad_b = grad_b + jnp.sum(d_qkv.astype(f32), axis=1)

    place = lambda vec: lax.dynamic_update_slice_in_dim(jnp.zeros((width,), f32), vec, me * cols, 0)
    vectors = [place(grad_b[:cols]), place(grad_b[2 * cols :]), grad_bo, grad_g1, grad_s1, grad_b2, grad_g2, grad_s2]
    stacked = jnp.concatenate([v.reshape(1, width) for v in vectors] + [grad_b1.reshape(devices, -1, share).transpose(1, 0, 2).reshape(-1, width)], axis=0)
    stacked = jnp.pad(stacked.T, ((0, 0), (0, spare - lines)))
    by_head = jnp.concatenate([grad_qkv, stacked], axis=1).astype(bf16).reshape(devices, share, 3 * cols + spare)
    by_head = jnp.pad(by_head, ((0, 0), (0, ext - share), (0, 0)))
    by_head, *summed = fold(by_head, parts)
    token_grad = [d_res1[m * rows : (m + 1) * rows] + summed[m] for m in range(micro)]
    gq, gk, gv = [by_head[:, :share, n * cols : (n + 1) * cols].transpose(1, 0, 2).reshape(share, width) for n in range(3)]
    both = jnp.sum(by_head[:, :share, 3 * cols : 3 * cols + lines], axis=0).T
    gbq, gbv, gbo, gg1, gs1, gb2, gg2, gs2 = [both[n] for n in range(8)]
    gb1 = both[8:].reshape(-1)
    grads = grads.astype(f32)
    gwo, gw2 = grads[:share], grads[share : share + share * wide]
    gw1 = jnp.concatenate([grads[share * (1 + wide + n) : share * (2 + wide + n)] for n in range(wide)], axis=1)
    four = (micro, 1, rows, width)
    return (
        layer_output.reshape(four), jnp.stack(token_grad).reshape(four), gq, gbq, gk, gv, gbv, gwo, gbo, gg1, gs1,
        gw1, gb1, gw2, gb2, gg2, gs2,
    )


def solution(mesh):
    rows = P(("ctx", "fsdp"), None)
    flat = P(("ctx", "fsdp"))
    tokens = P(None, "fsdp", "ctx", None)
    params = (rows, flat, rows, rows, flat, rows, flat, flat, flat, rows, flat, rows, flat, flat, flat)
    return jax.shard_map(
        body,
        mesh=mesh,
        in_specs=(tokens, P(None, "fsdp", None), P(None, "fsdp")) + params + (tokens,),
        out_specs=(tokens, tokens) + params,
        check_vma=False,
    )
```

```python
import functools
import math

import jax
import jax.numpy as jnp
from jax import lax
from jax.experimental import pallas as pl
from jax.experimental.pallas import tpu as pltpu
from jax.sharding import PartitionSpec as P

HD = 64
KEY_BLOCK = 128
TILE = 256
SEG_COUNT = 32
FAR = 1e30

def mask_rows(seg_row, reach, first_block):
    n = seg_row.shape[1]
    row = lax.broadcasted_iota(jnp.int32, (HD, n), 0)
    seg = jnp.broadcast_to(seg_row, (HD, n))
    block = lax.broadcasted_iota(jnp.int32, (HD, n), 1) // KEY_BLOCK + first_block
    is_seg = row < SEG_COUNT
    key_at = row - SEG_COUNT
    far = jnp.logical_not(is_seg) & (jnp.abs(key_at - block) >= reach)
    q_side = jnp.where((is_seg & (seg == row)) | far, -FAR, 0.0)
    k_side = jnp.where((is_seg & (seg != row)) | (key_at == block), 1.0, 0.0)
    return q_side.astype(jnp.bfloat16), k_side.astype(jnp.bfloat16)


def token_block(me, s, count, rows):
    return pl.ds(pl.multiple_of(lax.rem(me + s, count) * rows, rows), rows)


def fwd_kernel(heads, count, lo_ref, hi_ref, at_ref, seg_ref, qkv_ref, *refs):
    att_refs, lse_ref, (kaug, qaug, vtr, att, held_s, held_p) = refs[:count], refs[count], refs[count + 1 :]
    reach, me = at_ref[0], at_ref[1]
    length = qkv_ref.shape[1]
    rows, width = length // count, heads * HD

    def prepare(s, _):
        here = pl.ds(pl.multiple_of(s * rows, rows), rows)
        there = token_block(me, s, count, rows)
        q_side, k_side = mask_rows(seg_ref[:, there], reach, lax.rem(me + s, count) * (rows // KEY_BLOCK))
        for h in range(heads):
            q = qkv_ref[h * HD : (h + 1) * HD, here]
            k = qkv_ref[width + h * HD : width + (h + 1) * HD, here]
            qaug[h, 0:HD, there] = (q.astype(jnp.float32) * (1.0 / math.sqrt(HD))).astype(jnp.bfloat16)
            qaug[h, HD : 2 * HD, there] = q_side
            kaug[h, there, :] = jnp.transpose(jnp.concatenate([k, k_side], axis=0))
            vtr[h, :, there] = qkv_ref[2 * width + h * HD : 2 * width + (h + 1) * HD, here]
        return 0
    lax.fori_loop(0, count, prepare, 0)

    def tile(n):
        return pl.ds(pl.multiple_of(n * TILE, TILE), TILE)

    tiles = length // TILE
    for h in range(heads):
        held_s[h] = jnp.dot(kaug[h, tile(lo_ref[0]), :], qaug[h, :, tile(0)], preferred_element_type=jnp.float32)

    def q_step(i, _):
        qs = tile(i)
        first, end = lo_ref[i], hi_ref[i]
        later = jnp.minimum(i + 1, tiles - 1)

        def k_step(j, carry):
            ks, last = tile(j), j + 1 == end
            after, after_q = tile(jnp.where(last, lo_ref[later], j + 1)), tile(jnp.where(last, later, i))
            out, kept = [], None
            def values(h, peak, total, fade, acc, p):
                out.append((peak, total, fade, acc * fade + jnp.dot(vtr[h, :, ks], p, preferred_element_type=jnp.float32)))
            for h in range(heads):
                peak, total, _, acc = carry[h]
                s = held_s[h]
                new = jnp.maximum(peak, jnp.max(s, axis=0, keepdims=True))
                p = jnp.exp(s - new)
                fade = jnp.exp(peak - new)
                total = total * fade + jnp.sum(p, axis=0, keepdims=True)
                held_s[h] = jnp.dot(kaug[h, after, :], qaug[h, :, after_q], preferred_element_type=jnp.float32)
                if h:
                    values(*kept)
                kept = (h, new, total, fade, acc, p.astype(jnp.bfloat16))
            values(*kept)
            return tuple(out)
        row = lambda value: jnp.full((1, TILE), value, jnp.float32)
        start = tuple((row(-3e38), row(0.0), row(0.0), jnp.zeros((HD, TILE), jnp.float32)) for _ in range(heads))
        done = lax.fori_loop(first, end, k_step, start)
        for h in range(heads):
            peak, total, fade, acc = done[h]
            att[h * HD : (h + 1) * HD, qs] = (acc / total).astype(jnp.bfloat16)
            lse_ref[h : h + 1, qs] = peak + jnp.log(total)
        return 0
    lax.fori_loop(0, tiles, q_step, 0)
    for s in range(count):
        att_refs[s][...] = att[:, token_block(me, s, count, rows)]


def attend(qkv, seg, lo, hi, at, heads, count):
    cols, length = qkv.shape
    width, rows = heads * HD, length // count
    whole = lambda shape: pl.BlockSpec(shape, lambda n, *_: (0, 0))
    return pl.pallas_call(
        functools.partial(fwd_kernel, heads, count),
        out_shape=[jax.ShapeDtypeStruct((width, rows), jnp.bfloat16)] * count + [jax.ShapeDtypeStruct((8, length), jnp.float32)],
        grid_spec=pltpu.PrefetchScalarGridSpec(
            num_scalar_prefetch=3, grid=(1,),
            in_specs=[whole((1, length)), whole((cols, length))],
            out_specs=[whole((width, rows))] * count + [whole((8, length))],
            scratch_shapes=[pltpu.VMEM((heads, length, 2 * HD), jnp.bfloat16), pltpu.VMEM((heads, 2 * HD, length), jnp.bfloat16),
                            pltpu.VMEM((heads, HD, length), jnp.bfloat16), pltpu.VMEM((width, length), jnp.bfloat16),
                            pltpu.VMEM((heads, TILE, TILE), jnp.float32), pltpu.VMEM((heads, TILE, TILE), jnp.bfloat16)]),
        compiler_params=pltpu.CompilerParams(dimension_semantics=("arbitrary",), vmem_limit_bytes=40 << 20),
        cost_estimate=pl.CostEstimate(flops=30_000_000_000, bytes_accessed=4_000_000, transcendentals=0),
        name="attend",
    )(lo, hi, at, seg, qkv)


def bwd_kernel(heads, count, lo_ref, hi_ref, at_ref, seg_ref, qkv_ref, lse_ref, *refs):
    att_refs, datt_refs, dqkv_ref = refs[:count], refs[count : 2 * count], refs[2 * count]
    kaug, qaug, v_nat, dotr, ktr, delta, dqt, dkt, dvt, held_s = refs[2 * count + 1 :]
    reach, me = at_ref[0], at_ref[1]
    length = qkv_ref.shape[1]
    rows, width = length // count, heads * HD
    tiles = length // TILE
    scale = 1.0 / math.sqrt(HD)
    f32, bf16 = jnp.float32, jnp.bfloat16
    for s in range(count):
        there = token_block(me, s, count, rows)
        for h in range(heads):
            do, o = datt_refs[s][h * HD : (h + 1) * HD, :], att_refs[s][h * HD : (h + 1) * HD, :]
            dotr[h, :, there] = do
            delta[h, :, there] = jnp.sum(do.astype(f32) * o.astype(f32), axis=0, keepdims=True)

    def prepare(s, _):
        here = pl.ds(pl.multiple_of(s * rows, rows), rows)
        there = token_block(me, s, count, rows)
        q_side, k_side = mask_rows(seg_ref[:, there], reach, lax.rem(me + s, count) * (rows // KEY_BLOCK))
        for h in range(heads):
            q = qkv_ref[h * HD : (h + 1) * HD, here]
            k = qkv_ref[width + h * HD : width + (h + 1) * HD, here]
            qaug[h, 0:HD, there] = (q.astype(f32) * scale).astype(bf16)
            qaug[h, HD : 2 * HD, there] = q_side
            kaug[h, there, :] = jnp.transpose(jnp.concatenate([k, k_side], axis=0))
            ktr[h, :, there] = k
            v_nat[h, there, :] = jnp.transpose(qkv_ref[2 * width + h * HD : 2 * width + (h + 1) * HD, here])
            dqt[h, :, there] = jnp.zeros((HD, rows), f32)
        return 0
    lax.fori_loop(0, count, prepare, 0)

    def tile(n):
        return pl.ds(pl.multiple_of(n * TILE, TILE), TILE)

    def over_queries(left, right):
        return lax.dot_general(left, right, (((1,), (1,)), ((), ())), preferred_element_type=f32)

    for h in range(heads):
        held_s[h] = jnp.dot(kaug[h, tile(0), :], qaug[h, :, tile(lo_ref[0])], preferred_element_type=f32)

    def k_step(j, _):
        ks = tile(j)
        first, end = lo_ref[j], hi_ref[j]
        later = jnp.minimum(j + 1, tiles - 1)
        dkt[...] = jnp.zeros_like(dkt)
        dvt[...] = jnp.zeros_like(dvt)

        def q_step(i, _):
            qs, last = tile(i), i + 1 == end
            after, after_k = tile(jnp.where(last, lo_ref[later], i + 1)), tile(jnp.where(last, later, j))
            def terms(h, p, ds):
                dvt[h] += over_queries(dotr[h, :, qs], p)
                dkt[h] += over_queries(qaug[h, 0:HD, qs], ds)
                dqt[h, :, qs] += jnp.dot(ktr[h, :, ks], ds, preferred_element_type=f32)

            def to_probs(h):
                return jnp.dot(v_nat[h, ks, :], dotr[h, :, qs], preferred_element_type=f32)
            dp, kept = to_probs(0), None
            for h in range(heads):
                ahead = to_probs(h + 1) if h + 1 < heads else None
                p = jnp.exp(held_s[h] - lse_ref[h : h + 1, qs])
                ds = (p * (dp - delta[h, :, qs])).astype(bf16)
                held_s[h] = jnp.dot(kaug[h, after_k, :], qaug[h, :, after], preferred_element_type=f32)
                if h:
                    terms(h - 1, *kept)
                kept, dp = (p.astype(bf16), ds), ahead
            terms(heads - 1, *kept)
            return 0
        lax.fori_loop(first, end, q_step, 0)
        slot = lax.rem(j // (rows // TILE) + count - me, count)
        out = pl.ds(pl.multiple_of(slot * rows + lax.rem(j, rows // TILE) * TILE, TILE), TILE)
        for h in range(heads):
            dqkv_ref[width + h * HD : width + (h + 1) * HD, out] = dkt[h].astype(bf16)
            dqkv_ref[2 * width + h * HD : 2 * width + (h + 1) * HD, out] = dvt[h].astype(bf16)
        return 0
    lax.fori_loop(0, tiles, k_step, 0)

    def finish(s, _):
        here = pl.ds(pl.multiple_of(s * rows, rows), rows)
        there = token_block(me, s, count, rows)
        for h in range(heads):
            dqkv_ref[h * HD : (h + 1) * HD, here] = (dqt[h, :, there] * scale).astype(bf16)
        return 0
    lax.fori_loop(0, count, finish, 0)


def attend_back(qkv, att, datt, lse, seg, lo, hi, at, heads, count):
    cols, length = qkv.shape
    width, rows = heads * HD, length // count
    whole = lambda shape: pl.BlockSpec(shape, lambda n, *_: (0, 0))
    return pl.pallas_call(
        functools.partial(bwd_kernel, heads, count),
        out_shape=jax.ShapeDtypeStruct((cols, length), jnp.bfloat16),
        grid_spec=pltpu.PrefetchScalarGridSpec(
            num_scalar_prefetch=3, grid=(1,),
            in_specs=[whole((1, length)), whole((cols, length)), whole((8, length))] + [whole((width, rows))] * (2 * count),
            out_specs=whole((cols, length)),
            scratch_shapes=[
                pltpu.VMEM((heads, length, 2 * HD), jnp.bfloat16),
                pltpu.VMEM((heads, 2 * HD, length), jnp.bfloat16),
                pltpu.VMEM((heads, length, HD), jnp.bfloat16),
                pltpu.VMEM((heads, HD, length), jnp.bfloat16),
                pltpu.VMEM((heads, HD, length), jnp.bfloat16),
                pltpu.VMEM((heads, 1, length), jnp.float32),
                pltpu.VMEM((heads, HD, length), jnp.float32),
                pltpu.VMEM((heads, HD, TILE), jnp.float32),
                pltpu.VMEM((heads, HD, TILE), jnp.float32),
                pltpu.VMEM((heads, TILE, TILE), jnp.float32)]),
        compiler_params=pltpu.CompilerParams(dimension_semantics=("arbitrary",), vmem_limit_bytes=48 << 20),
        cost_estimate=pl.CostEstimate(flops=30_000_000_000, bytes_accessed=6_000_000, transcendentals=0),
        name="attend_back",
    )(lo, hi, at, seg, qkv, lse, *att, *datt)


def bounds(segments, reach):
    first = segments[:, ::TILE]
    last = segments[:, TILE - 1::TILE]
    n = first.shape[1]
    at = jnp.arange(n)
    per = TILE // KEY_BLOCK
    gap = per * jnp.abs(at[:, None] - at[None, :]) - (per - 1)
    near = gap[None] < reach[:, None, None]
    before = (at[None, :] < at[:, None])[None] & near & (first[:, :, None] == last[:, None, :])
    after = (at[None, :] > at[:, None])[None] & near & (last[:, :, None] == first[:, None, :])
    lo = at[None] - jnp.sum(before, axis=2, dtype=jnp.int32)
    hi = at[None] + 1 + jnp.sum(after, axis=2, dtype=jnp.int32)
    return lo.astype(jnp.int32), hi.astype(jnp.int32)


MESH = pl.DeviceIdType.MESH


def greet(peers):
    barrier = pltpu.get_barrier_semaphore()
    for peer in peers:
        pl.semaphore_signal(barrier, inc=1, device_id=peer, device_id_type=MESH)
    pl.semaphore_wait(barrier, len(peers))


def add_low(left, right):
    return (left.astype(jnp.float32) + right.astype(jnp.float32)).astype(jnp.bfloat16)


class Sends:
    def __init__(self, send_sem, recv_sem):
        self.send_sem, self.recv_sem, self.used, self.open = send_sem, recv_sem, 0, []

    def start(self, src, dst, peer):
        n = self.used
        self.used += 1
        copy = pltpu.make_async_remote_copy(
            src_ref=src, dst_ref=dst, send_sem=self.send_sem.at[n], recv_sem=self.recv_sem.at[n],
            device_id=peer, device_id_type=MESH)
        copy.start()
        self.open.append(copy)
        return copy

    def finish(self):
        for copy in self.open:
            copy.wait_send()


def fold_kernel(zs, micro, heads_in, *refs):
    tokens_in, heads_out, tokens_out = refs[:micro], refs[micro], refs[micro + 1 : 2 * micro + 1]
    h_own, h_y, h_z, h_c, t_own, t_c, t_x, send_sem, recv_sem, load_sem = refs[2 * micro + 1 :]
    c, f = lax.axis_index("ctx"), lax.axis_index("fsdp")
    x, core, z, y = c // 2, c % 2, f // 2, f % 2
    partner = {"ctx": x * 2 + (1 - core), "fsdp": f}
    beside = {"ctx": (1 - x) * 2 + core, "fsdp": f}
    above = {"ctx": c, "fsdp": z * 2 + (1 - y)}
    far = [{"ctx": c, "fsdp": lax.rem(z + s, zs) * 2 + y} for s in range(1, zs)]
    across = [{"ctx": lax.rem(c + s, 4), "fsdp": f} for s in range(1, 4)]
    sends = Sends(send_sem, recv_sem)
    greet([above] + far + across)

    near = 1 + 2 * core
    other = 3 - 2 * core
    loads = []
    def load(src, dst):
        loads.append(pltpu.make_async_copy(src, dst, load_sem.at[len(loads)]))
        loads[-1].start()
        return loads[-1]
    load_there, copy_there, load_here, copy_here = [], [], [], []
    for m in range(micro):
        copy_there.append(sends.start(tokens_in[m].at[other], t_c.at[m, 1], partner))
        load_there.append(load(tokens_in[m].at[2], t_own.at[m, 1]))
    copy_h = sends.start(heads_in.at[:, :, 1 - y], h_y, above)
    load_h = load(heads_in.at[:, :, y], h_own)
    for m in range(micro):
        copy_here.append(sends.start(tokens_in[m].at[near], t_c.at[m, 0], partner))
        load_here.append(load(tokens_in[m].at[0], t_own.at[m, 0]))

    chunks = t_own.shape[2] // 64
    def sum_t(m, place):
        def step(i, _):
            rows = pl.ds(pl.multiple_of(i * 64, 64), 64)
            t_c[m, place, rows, :] = add_low(t_own[m, place, rows, :], t_c[m, place, rows, :])
            return 0
        lax.fori_loop(0, chunks, step, 0)
    copy_tx = []
    for m in range(micro):
        load_there[m].wait(), copy_there[m].wait_recv()
        sum_t(m, 1)
        copy_tx.append(sends.start(t_c.at[m, 1], t_x.at[m], beside))

    load_h.wait(), copy_h.wait_recv()
    def sum_h(i, _):
        a, b = i // zs, lax.rem(i, zs)
        h_y[a, b] = add_low(h_own[a, b], h_y[a, b])
        return 0
    lax.fori_loop(0, 4 * zs, sum_h, 0)
    copy_hz = [sends.start(h_y.at[:, lax.rem(z + s, zs)], h_z.at[s - 1], far[s - 1]) for s in range(1, zs)]
    for m in range(micro):
        load_here[m].wait(), copy_here[m].wait_recv()
        sum_t(m, 0)
    for copy in copy_hz:
        copy.wait_recv()
    def total_h(a, _):
        total = h_y[a, z].astype(jnp.float32)
        for s in range(1, zs):
            total = total + h_z[s - 1, a].astype(jnp.float32)
        h_own[a, 0] = total.astype(jnp.bfloat16)
        return 0
    lax.fori_loop(0, 4, total_h, 0)
    copy_hc = [sends.start(h_own.at[lax.rem(c + s, 4), 0], h_c.at[s - 1], across[s - 1]) for s in range(1, 4)]
    for m in range(micro):
        copy_tx[m].wait_recv()
        def last_t(i, _, m=m):
            rows = pl.ds(pl.multiple_of(i * 64, 64), 64)
            tokens_out[m][rows, :] = t_c[m, 0, rows, :].astype(jnp.float32) + t_x[m, rows, :].astype(jnp.float32)
            return 0
        lax.fori_loop(0, chunks, last_t, 0)
    heads_out[c] = h_own[c, 0].astype(jnp.float32)
    for s in range(1, 4):
        copy_hc[s - 1].wait_recv()
        heads_out[lax.rem(c + 4 - s, 4)] = h_c[s - 1].astype(jnp.float32)
    sends.finish()


def fold(by_head, tokens):
    ctx, fsdp = lax.axis_size("ctx"), lax.axis_size("fsdp")
    zs = fsdp // 2
    assert ctx == 4 and fsdp % 2 == 0
    f32, bf16 = jnp.float32, jnp.bfloat16
    hr, hw = by_head.shape[1:]
    micro = len(tokens)
    _, tr, tw = tokens[0].shape
    copies = 3 * micro + 1 + (zs - 1) + 3
    anywhere, vmem = pl.BlockSpec(memory_space=pl.ANY), pl.BlockSpec(memory_space=pltpu.VMEM)
    return pl.pallas_call(
        functools.partial(fold_kernel, zs, micro),
        out_shape=[jax.ShapeDtypeStruct((4, hr, hw), f32)] + [jax.ShapeDtypeStruct((tr, tw), f32)] * micro,
        in_specs=[anywhere] * (1 + micro), out_specs=[vmem] * (1 + micro),
        scratch_shapes=[
            pltpu.VMEM((4, zs, hr, hw), bf16), pltpu.VMEM((4, zs, hr, hw), bf16), pltpu.VMEM((zs - 1, 4, hr, hw), bf16), pltpu.VMEM((3, hr, hw), bf16),
            pltpu.VMEM((micro, 2, tr, tw), bf16), pltpu.VMEM((micro, 2, tr, tw), bf16), pltpu.VMEM((micro, tr, tw), bf16),
            pltpu.SemaphoreType.DMA((copies,)), pltpu.SemaphoreType.DMA((copies,)), pltpu.SemaphoreType.DMA((1 + 2 * micro,))],
        compiler_params=pltpu.CompilerParams(collective_id=1, has_side_effects=True, vmem_limit_bytes=63 << 20),
        name="fold",
    )(by_head.reshape(4, zs, 2, hr, hw), *tokens)


def collect_kernel(zs, micro, mine, tokens, mine_out, *refs):
    tokens_out, (held_mine, held, send_sem, recv_sem, load_sem) = refs[:micro], refs[micro:]
    c, f = lax.axis_index("ctx"), lax.axis_index("fsdp")
    x, core, z, y = c // 2, c % 2, f // 2, f % 2
    partner = {"ctx": x * 2 + (1 - core), "fsdp": f}
    beside = {"ctx": (1 - x) * 2 + core, "fsdp": f}
    above = {"ctx": c, "fsdp": z * 2 + (1 - y)}
    far = [{"ctx": c, "fsdp": lax.rem(z + s, zs) * 2 + y} for s in range(1, zs)]
    across = [{"ctx": lax.rem(c + s, 4), "fsdp": f} for s in range(1, 4)]
    greet([above] + far + across)
    sends = Sends(send_sem, recv_sem)
    loads = [pltpu.make_async_copy(mine.at[c], held_mine, load_sem.at[0]), pltpu.make_async_copy(tokens, held, load_sem.at[1])]
    for copy in loads:
        copy.start()
    first = [sends.start(mine.at[lax.rem(c + s, 4)], mine_out.at[c, z, y], across[s - 1]) for s in range(1, 4)]
    over_x = [sends.start(tokens.at[m], tokens_out[m].at[2], beside) for m in range(micro)]
    over_core = [sends.start(tokens.at[m], tokens_out[m].at[3 - 2 * core], partner) for m in range(micro)]
    loads[0].wait()
    stores = [pltpu.make_async_copy(held_mine, mine_out.at[c, z, y], load_sem.at[2])]
    stores[0].start()
    loads[1].wait()
    for m in range(micro):
        stores.append(pltpu.make_async_copy(held.at[m], tokens_out[m].at[0], load_sem.at[3 + m]))
        stores[-1].start()
    for copy in first:
        copy.wait_recv()
    stores[0].wait()
    over_y = sends.start(mine_out.at[:, z, y], mine_out.at[:, z, y], above)
    own_far = [sends.start(mine_out.at[:, z, y], mine_out.at[:, z, y], peer) for peer in far]
    up_down = []
    for s in range(1, zs):
        own_far[s - 1].wait_recv()
        there = lax.rem(z + zs - s, zs)
        up_down.append(sends.start(mine_out.at[:, there, y], mine_out.at[:, there, y], above))
    relay = []
    for m in range(micro):
        over_x[m].wait_recv()
        relay.append(sends.start(tokens_out[m].at[2], tokens_out[m].at[1 + 2 * core], partner))
    for copy in [over_y] + over_core + up_down + relay:
        copy.wait_recv()
    for copy in stores[1:]:
        copy.wait()
    sends.finish()


def collect(mine, tokens):
    ctx, fsdp = lax.axis_size("ctx"), lax.axis_size("fsdp")
    zs = fsdp // 2
    assert ctx == 4 and fsdp % 2 == 0
    micro = tokens.shape[0]
    copies = 3 + 1 + 2 * (zs - 1) + 3 * micro
    anywhere = pl.BlockSpec(memory_space=pl.ANY)
    return pl.pallas_call(
        functools.partial(collect_kernel, zs, micro),
        out_shape=[jax.ShapeDtypeStruct((4, zs, 2) + mine.shape[1:], mine.dtype)] + [jax.ShapeDtypeStruct((4,) + tokens.shape[1:], tokens.dtype)] * micro,
        in_specs=[anywhere] * 2, out_specs=[anywhere] * (1 + micro),
        scratch_shapes=[pltpu.VMEM(mine.shape[1:], mine.dtype), pltpu.VMEM(tokens.shape, tokens.dtype), pltpu.SemaphoreType.DMA((copies,)), pltpu.SemaphoreType.DMA((copies,)), pltpu.SemaphoreType.DMA((3 + micro,))],
        compiler_params=pltpu.CompilerParams(collective_id=0, has_side_effects=True),
        name="collect",
    )(mine, tokens)


def layer_norm(summed, gain, shift):
    row_mean = jnp.mean(summed, axis=-1, keepdims=True)
    centered = summed - row_mean
    variance = jnp.mean(centered * centered, axis=-1, keepdims=True)
    recip = lax.rsqrt(variance + 1e-05)
    normed = centered * recip
    return (normed * gain + shift, normed, recip)


def norm_back(upstream, normed, recip, gain):
    scaled = upstream * gain
    first_mean = jnp.mean(scaled, axis=-1, keepdims=True)
    second_mean = jnp.mean(scaled * normed, axis=-1, keepdims=True)
    d_summed = recip * (scaled - first_mean - normed * second_mean)
    return (d_summed, jnp.sum(upstream * normed, axis=0), jnp.sum(upstream, axis=0))


def dot(left, right):
    return jnp.dot(left, right, preferred_element_type=jnp.float32)


def weight_term(left, right):
    return jnp.einsum("ta,tb->ab", left, right, preferred_element_type=jnp.float32)


def back_term(grad_low, weight):
    return jnp.einsum("tb,ab->ta", grad_low, weight, preferred_element_type=jnp.float32)


def column_sum(grad_low):
    return jnp.sum(grad_low.astype(jnp.float32), axis=0)


def shift(piece, step):
    count = lax.axis_size("ctx")
    return lax.ppermute(piece, "ctx", [(a, (a + step) % count) for a in range(count)])


def body(
    inputs, segments, block_reach,
    query_weight, query_bias, key_weight, value_weight, value_bias, output_weight, output_bias,
    first_gain, first_shift, expand_weight, expand_bias, contract_weight, contract_bias,
    second_gain, second_shift, output_grad,
):
    every = ("ctx", "fsdp")
    ctx = lax.axis_size("ctx")
    me = lax.axis_index("ctx")
    micro, _, rows, width = inputs.shape
    length = rows * ctx
    cols = width // ctx
    heads = cols // HD
    f32, bf16 = jnp.float32, jnp.bfloat16

    share = query_bias.shape[0]
    lines = 8 + expand_bias.shape[0] // share
    ext = -(-share // 8) * 8
    spare = -(-(3 * cols + lines) // 128) * 128 - 3 * cols
    small = jnp.concatenate([v.reshape(-1, share) for v in (
        query_bias, value_bias, output_bias, first_gain, first_shift, contract_bias, second_gain, second_shift, expand_bias)], axis=0)
    small = jnp.pad(small.T, ((0, 0), (0, spare - lines)))
    split = [jnp.stack([w[:, n * cols : (n + 1) * cols] for n in range(ctx)]) for w in (query_weight, key_weight, value_weight)]
    mine = jnp.concatenate(split + [jnp.broadcast_to(a, (ctx,) + a.shape) for a in (small, output_weight)], axis=2)
    mine = jnp.pad(mine, ((0, 0), (0, ext - share), (0, 0)))

    wide = expand_weight.shape[1] // width
    w_expand = lax.all_gather(expand_weight, every, axis=0, tiled=True)
    w_contract = lax.all_gather(contract_weight, every, axis=0, tiled=True)

    mine_all, *tokens_all = collect(mine, inputs[:, 0])
    tokens_all = [t.reshape(length, width) for t in tokens_all]
    mine_all = mine_all.reshape(-1, ext, 3 * cols + spare + width)
    devices = mine_all.shape[0]
    w_mine = mine_all[:, :share, : 3 * cols].reshape(width, 3 * cols)
    small_all = mine_all[:, :share, 3 * cols : 3 * cols + lines].astype(f32).reshape(width, lines).T
    b_query, b_value, b_output, g_first, s_first, b_contract, g_second, s_second = [small_all[n] for n in range(8)]
    b_expand = small_all[8:].reshape(-1, devices, share).transpose(1, 0, 2).reshape(-1)

    back = [lax.rem(me + ctx - s, ctx) for s in range(ctx)]
    by_owner = mine_all[:, :share, 3 * cols + spare :].reshape(ctx, cols, width)
    w_output = jnp.concatenate([lax.dynamic_index_in_dim(by_owner, back[s], 0, keepdims=False) for s in range(ctx)], axis=0)

    own = lambda vec: lax.dynamic_slice_in_dim(vec, me * cols, cols, 0)
    b_mine = jnp.concatenate([own(b_query), jnp.zeros((cols,), f32), own(b_value)])
    seg = segments[:, 0]
    reach = block_reach[:, 0]
    lo, hi = bounds(seg, reach)
    at = [jnp.stack([reach[m], me]) for m in range(micro)]

    qkv, att, lse, attended = [], [], [], []
    for m in range(micro):
        flat = tokens_all[m]
        if m:
            flat, _ = lax.optimization_barrier((flat, lse[-1]))
        projected = jnp.einsum("wc,tw->ct", w_mine, flat, preferred_element_type=f32)
        qkv.append((projected + b_mine[:, None]).astype(bf16))
        *pieces, logs = attend(qkv[m], seg[m : m + 1], lo[m], hi[m], at[m], heads, ctx)
        att.append(pieces), lse.append(logs)
        attended.append(jnp.concatenate([pieces[0]] + [shift(pieces[s], s) for s in range(1, ctx)], axis=0))
    attended = jnp.concatenate(attended, axis=1)

    tokens = inputs[:, 0].reshape(micro * rows, width)
    branch = jnp.einsum("ct,cn->tn", attended, w_output, preferred_element_type=f32) + b_output
    hidden, normed_first, recip_first = layer_norm(tokens.astype(f32) + branch, g_first, s_first)
    hidden_low = hidden.astype(bf16)
    pre = dot(hidden_low, w_expand) + b_expand
    phi = 0.5 * (1.0 + lax.erf(pre * (1.0 / math.sqrt(2.0))))
    act_low = (pre * phi).astype(bf16)
    slope = (phi + pre * (jnp.exp(-0.5 * pre * pre) * (1.0 / math.sqrt(2.0 * math.pi)))).astype(bf16)
    act_low, slope = lax.optimization_barrier((act_low, slope))
    second_sum = hidden + dot(act_low, w_contract) + b_contract
    result, normed_second, recip_second = layer_norm(second_sum, g_second, s_second)
    layer_output = result.astype(bf16)
    upstream = output_grad[:, 0].reshape(micro * rows, width).astype(f32)
    d_res2, grad_g2, grad_s2 = norm_back(upstream, normed_second, recip_second, g_second)
    d_ffn = d_res2.astype(bf16)
    grad_b2 = column_sum(d_ffn)
    d_pre = (back_term(d_ffn, w_contract) * slope.astype(f32)).astype(bf16)
    grad_b1 = column_sum(d_pre)
    d_hidden = d_res2 + back_term(d_pre, w_expand)
    d_res1, grad_g1, grad_s1 = norm_back(d_hidden, normed_first, recip_first, g_first)
    d_branch = d_res1.astype(bf16)
    grad_bo = column_sum(d_branch)
    d_attended = [
        jnp.einsum("cn,tn->ct", w_output, d_branch[m * rows : (m + 1) * rows], preferred_element_type=f32).astype(bf16).reshape(ctx, cols, rows)
        for m in range(micro)]

    *d_attended, d_ffn, d_pre, d_branch = lax.optimization_barrier((*d_attended, d_ffn, d_pre, d_branch))
    d_att = [[d_attended[m][0]] + [shift(d_attended[m][s], -s) for s in range(1, ctx)] for m in range(micro)]
    grad_w2 = weight_term(act_low, d_ffn).astype(bf16).reshape(devices, -1, width)
    grad_w1 = [weight_term(hidden_low, d_pre[:, n * width : (n + 1) * width]).astype(bf16).reshape(devices, share, width) for n in range(wide)]
    grad_wo = dot(attended, d_branch).astype(bf16).reshape(ctx, cols, width)
    grad_wo = jnp.concatenate([lax.dynamic_index_in_dim(grad_wo, back[b], 0, keepdims=False) for b in range(ctx)], axis=0).reshape(devices, share, width)
    grads = jnp.concatenate([grad_wo, grad_w2] + grad_w1, axis=1).reshape(-1, width)
    grads = lax.psum_scatter(grads, every, scatter_dimension=0, tiled=True)

    parts, grad_qkv, grad_b = [], 0.0, 0.0
    for m in range(micro):
        d_qkv = attend_back(qkv[m], att[m], d_att[m], lse[m], seg[m : m + 1], lo[m], hi[m], at[m], heads, ctx)
        parts.append(jnp.einsum("ct,nc->tn", d_qkv, w_mine, preferred_element_type=f32).astype(bf16).reshape(ctx, rows, width))
        grad_qkv = grad_qkv + jnp.einsum("tw,ct->wc", tokens_all[m], d_qkv, preferred_element_type=f32)
        grad_b = grad_b + jnp.sum(d_qkv.astype(f32), axis=1)

    place = lambda vec: lax.dynamic_update_slice_in_dim(jnp.zeros((width,), f32), vec, me * cols, 0)
    vectors = [place(grad_b[:cols]), place(grad_b[2 * cols :]), grad_bo, grad_g1, grad_s1, grad_b2, grad_g2, grad_s2]
    stacked = jnp.concatenate([v.reshape(1, width) for v in vectors] + [grad_b1.reshape(devices, -1, share).transpose(1, 0, 2).reshape(-1, width)], axis=0)
    stacked = jnp.pad(stacked.T, ((0, 0), (0, spare - lines)))
    by_head = jnp.concatenate([grad_qkv, stacked], axis=1).astype(bf16).reshape(devices, share, 3 * cols + spare)
    by_head = jnp.pad(by_head, ((0, 0), (0, ext - share), (0, 0)))
    by_head, *summed = fold(by_head, parts)
    token_grad = [d_res1[m * rows : (m + 1) * rows] + summed[m] for m in range(micro)]
    gq, gk, gv = [by_head[:, :share, n * cols : (n + 1) * cols].transpose(1, 0, 2).reshape(share, width) for n in range(3)]
    both = jnp.sum(by_head[:, :share, 3 * cols : 3 * cols + lines], axis=0).T
    gbq, gbv, gbo, gg1, gs1, gb2, gg2, gs2 = [both[n] for n in range(8)]
    gb1 = both[8:].reshape(-1)
    grads = grads.astype(f32)
    gwo, gw2 = grads[:share], grads[share : share + share * wide]
    gw1 = jnp.concatenate([grads[share * (1 + wide + n) : share * (2 + wide + n)] for n in range(wide)], axis=1)
    four = (micro, 1, rows, width)
    return (
        layer_output.reshape(four), jnp.stack(token_grad).reshape(four), gq, gbq, gk, gv, gbv, gwo, gbo, gg1, gs1,
        gw1, gb1, gw2, gb2, gg2, gs2,
    )


def solution(mesh):
    rows = P(("ctx", "fsdp"), None)
    flat = P(("ctx", "fsdp"))
    tokens = P(None, "fsdp", "ctx", None)
    params = (rows, flat, rows, rows, flat, rows, flat, flat, flat, rows, flat, rows, flat, flat, flat)
    return jax.shard_map(
        body,
        mesh=mesh,
        in_specs=(tokens, P(None, "fsdp", None), P(None, "fsdp")) + params + (tokens,),
        out_specs=(tokens, tokens) + params,
        check_vma=False,
    )
```

```python
import functools
import math

import jax
import jax.numpy as jnp
from jax import lax
from jax.experimental import pallas as pl
from jax.experimental.pallas import tpu as pltpu
from jax.sharding import PartitionSpec as P

HD = 64
KEY_BLOCK = 128
TILE = 256
SEG_COUNT = 32
FAR = 1e30

def mask_rows(seg_row, reach, first_block):
    n = seg_row.shape[1]
    row = lax.broadcasted_iota(jnp.int32, (HD, n), 0)
    seg = jnp.broadcast_to(seg_row, (HD, n))
    block = lax.broadcasted_iota(jnp.int32, (HD, n), 1) // KEY_BLOCK + first_block
    is_seg = row < SEG_COUNT
    key_at = row - SEG_COUNT
    far = jnp.logical_not(is_seg) & (jnp.abs(key_at - block) >= reach)
    q_side = jnp.where((is_seg & (seg == row)) | far, -FAR, 0.0)
    k_side = jnp.where((is_seg & (seg != row)) | (key_at == block), 1.0, 0.0)
    return q_side.astype(jnp.bfloat16), k_side.astype(jnp.bfloat16)


def token_block(me, s, count, rows):
    return pl.ds(pl.multiple_of(lax.rem(me + s, count) * rows, rows), rows)


def fwd_kernel(heads, count, lo_ref, hi_ref, at_ref, seg_ref, qkv_ref, *refs):
    att_refs, lse_ref, (kaug, qaug, vtr, att, held_s, held_p) = refs[:count], refs[count], refs[count + 1 :]
    reach, me = at_ref[0], at_ref[1]
    length = qkv_ref.shape[1]
    rows, width = length // count, heads * HD

    def prepare(s, _):
        here = pl.ds(pl.multiple_of(s * rows, rows), rows)
        there = token_block(me, s, count, rows)
        q_side, k_side = mask_rows(seg_ref[:, there], reach, lax.rem(me + s, count) * (rows // KEY_BLOCK))
        for h in range(heads):
            q = qkv_ref[h * HD : (h + 1) * HD, here]
            k = qkv_ref[width + h * HD : width + (h + 1) * HD, here]
            qaug[h, 0:HD, there] = (q.astype(jnp.float32) * (1.0 / math.sqrt(HD))).astype(jnp.bfloat16)
            qaug[h, HD : 2 * HD, there] = q_side
            kaug[h, there, :] = jnp.transpose(jnp.concatenate([k, k_side], axis=0))
            vtr[h, :, there] = qkv_ref[2 * width + h * HD : 2 * width + (h + 1) * HD, here]
        return 0
    lax.fori_loop(0, count, prepare, 0)

    def tile(n):
        return pl.ds(pl.multiple_of(n * TILE, TILE), TILE)

    tiles = length // TILE
    for h in range(heads):
        held_s[h] = jnp.dot(kaug[h, tile(lo_ref[0]), :], qaug[h, :, tile(0)], preferred_element_type=jnp.float32)

    def q_step(i, _):
        qs = tile(i)
        first, end = lo_ref[i], hi_ref[i]
        later = jnp.minimum(i + 1, tiles - 1)

        def k_step(j, carry):
            ks, last = tile(j), j + 1 == end
            after, after_q = tile(jnp.where(last, lo_ref[later], j + 1)), tile(jnp.where(last, later, i))
            out, kept = [], None
            def values(h, peak, total, fade, acc, p):
                out.append((peak, total, fade, acc * fade + jnp.dot(vtr[h, :, ks], p, preferred_element_type=jnp.float32)))
            for h in range(heads):
                peak, total, _, acc = carry[h]
                s = held_s[h]
                new = jnp.maximum(peak, jnp.max(s, axis=0, keepdims=True))
                p = jnp.exp(s - new)
                fade = jnp.exp(peak - new)
                total = total * fade + jnp.sum(p, axis=0, keepdims=True)
                held_s[h] = jnp.dot(kaug[h, after, :], qaug[h, :, after_q], preferred_element_type=jnp.float32)
                if h:
                    values(*kept)
                kept = (h, new, total, fade, acc, p.astype(jnp.bfloat16))
            values(*kept)
            return tuple(out)
        row = lambda value: jnp.full((1, TILE), value, jnp.float32)
        start = tuple((row(-3e38), row(0.0), row(0.0), jnp.zeros((HD, TILE), jnp.float32)) for _ in range(heads))
        done = lax.fori_loop(first, end, k_step, start)
        for h in range(heads):
            peak, total, fade, acc = done[h]
            att[h * HD : (h + 1) * HD, qs] = (acc / total).astype(jnp.bfloat16)
            lse_ref[h : h + 1, qs] = peak + jnp.log(total)
        return 0
    lax.fori_loop(0, tiles, q_step, 0)
    for s in range(count):
        att_refs[s][...] = att[:, token_block(me, s, count, rows)]


def attend(qkv, seg, lo, hi, at, heads, count):
    cols, length = qkv.shape
    width, rows = heads * HD, length // count
    whole = lambda shape: pl.BlockSpec(shape, lambda n, *_: (0, 0))
    return pl.pallas_call(
        functools.partial(fwd_kernel, heads, count),
        out_shape=[jax.ShapeDtypeStruct((width, rows), jnp.bfloat16)] * count + [jax.ShapeDtypeStruct((8, length), jnp.float32)],
        grid_spec=pltpu.PrefetchScalarGridSpec(
            num_scalar_prefetch=3, grid=(1,),
            in_specs=[whole((1, length)), whole((cols, length))],
            out_specs=[whole((width, rows))] * count + [whole((8, length))],
            scratch_shapes=[pltpu.VMEM((heads, length, 2 * HD), jnp.bfloat16), pltpu.VMEM((heads, 2 * HD, length), jnp.bfloat16),
                            pltpu.VMEM((heads, HD, length), jnp.bfloat16), pltpu.VMEM((width, length), jnp.bfloat16),
                            pltpu.VMEM((heads, TILE, TILE), jnp.float32), pltpu.VMEM((heads, TILE, TILE), jnp.bfloat16)]),
        compiler_params=pltpu.CompilerParams(dimension_semantics=("arbitrary",), vmem_limit_bytes=40 << 20),
        cost_estimate=pl.CostEstimate(flops=30_000_000_000, bytes_accessed=4_000_000, transcendentals=0),
        name="attend",
    )(lo, hi, at, seg, qkv)


def bwd_kernel(heads, count, lo_ref, hi_ref, at_ref, seg_ref, qkv_ref, lse_ref, *refs):
    att_refs, datt_refs, dqkv_ref = refs[:count], refs[count : 2 * count], refs[2 * count]
    kaug, qaug, v_nat, dotr, ktr, delta, dqt, dkt, dvt, held_s = refs[2 * count + 1 :]
    reach, me = at_ref[0], at_ref[1]
    length = qkv_ref.shape[1]
    rows, width = length // count, heads * HD
    tiles = length // TILE
    scale = 1.0 / math.sqrt(HD)
    f32, bf16 = jnp.float32, jnp.bfloat16
    for s in range(count):
        there = token_block(me, s, count, rows)
        for h in range(heads):
            do, o = datt_refs[s][h * HD : (h + 1) * HD, :], att_refs[s][h * HD : (h + 1) * HD, :]
            dotr[h, :, there] = do
            delta[h, :, there] = jnp.sum(do.astype(f32) * o.astype(f32), axis=0, keepdims=True)

    def prepare(s, _):
        here = pl.ds(pl.multiple_of(s * rows, rows), rows)
        there = token_block(me, s, count, rows)
        q_side, k_side = mask_rows(seg_ref[:, there], reach, lax.rem(me + s, count) * (rows // KEY_BLOCK))
        for h in range(heads):
            q = qkv_ref[h * HD : (h + 1) * HD, here]
            k = qkv_ref[width + h * HD : width + (h + 1) * HD, here]
            qaug[h, 0:HD, there] = (q.astype(f32) * scale).astype(bf16)
            qaug[h, HD : 2 * HD, there] = q_side
            kaug[h, there, :] = jnp.transpose(jnp.concatenate([k, k_side], axis=0))
            ktr[h, :, there] = k
            v_nat[h, there, :] = jnp.transpose(qkv_ref[2 * width + h * HD : 2 * width + (h + 1) * HD, here])
            dqt[h, :, there] = jnp.zeros((HD, rows), f32)
        return 0
    lax.fori_loop(0, count, prepare, 0)

    def tile(n):
        return pl.ds(pl.multiple_of(n * TILE, TILE), TILE)

    def over_queries(left, right):
        return lax.dot_general(left, right, (((1,), (1,)), ((), ())), preferred_element_type=f32)

    for h in range(heads):
        held_s[h] = jnp.dot(kaug[h, tile(0), :], qaug[h, :, tile(lo_ref[0])], preferred_element_type=f32)

    def k_step(j, _):
        ks = tile(j)
        first, end = lo_ref[j], hi_ref[j]
        later = jnp.minimum(j + 1, tiles - 1)
        dkt[...] = jnp.zeros_like(dkt)
        dvt[...] = jnp.zeros_like(dvt)

        def q_step(i, _):
            qs, last = tile(i), i + 1 == end
            after, after_k = tile(jnp.where(last, lo_ref[later], i + 1)), tile(jnp.where(last, later, j))
            def terms(h, p, ds):
                dvt[h] += over_queries(dotr[h, :, qs], p)
                dkt[h] += over_queries(qaug[h, 0:HD, qs], ds)
                dqt[h, :, qs] += jnp.dot(ktr[h, :, ks], ds, preferred_element_type=f32)

            def to_probs(h):
                return jnp.dot(v_nat[h, ks, :], dotr[h, :, qs], preferred_element_type=f32)
            dp, kept = to_probs(0), None
            for h in range(heads):
                ahead = to_probs(h + 1) if h + 1 < heads else None
                p = jnp.exp(held_s[h] - lse_ref[h : h + 1, qs])
                ds = (p * (dp - delta[h, :, qs])).astype(bf16)
                held_s[h] = jnp.dot(kaug[h, after_k, :], qaug[h, :, after], preferred_element_type=f32)
                if h:
                    terms(h - 1, *kept)
                kept, dp = (p.astype(bf16), ds), ahead
            terms(heads - 1, *kept)
            return 0
        lax.fori_loop(first, end, q_step, 0)
        slot = lax.rem(j // (rows // TILE) + count - me, count)
        out = pl.ds(pl.multiple_of(slot * rows + lax.rem(j, rows // TILE) * TILE, TILE), TILE)
        for h in range(heads):
            dqkv_ref[width + h * HD : width + (h + 1) * HD, out] = dkt[h].astype(bf16)
            dqkv_ref[2 * width + h * HD : 2 * width + (h + 1) * HD, out] = dvt[h].astype(bf16)
        return 0
    lax.fori_loop(0, tiles, k_step, 0)

    def finish(s, _):
        here = pl.ds(pl.multiple_of(s * rows, rows), rows)
        there = token_block(me, s, count, rows)
        for h in range(heads):
            dqkv_ref[h * HD : (h + 1) * HD, here] = (dqt[h, :, there] * scale).astype(bf16)
        return 0
    lax.fori_loop(0, count, finish, 0)


def attend_back(qkv, att, datt, lse, seg, lo, hi, at, heads, count):
    cols, length = qkv.shape
    width, rows = heads * HD, length // count
    whole = lambda shape: pl.BlockSpec(shape, lambda n, *_: (0, 0))
    return pl.pallas_call(
        functools.partial(bwd_kernel, heads, count),
        out_shape=jax.ShapeDtypeStruct((cols, length), jnp.bfloat16),
        grid_spec=pltpu.PrefetchScalarGridSpec(
            num_scalar_prefetch=3, grid=(1,),
            in_specs=[whole((1, length)), whole((cols, length)), whole((8, length))] + [whole((width, rows))] * (2 * count),
            out_specs=whole((cols, length)),
            scratch_shapes=[
                pltpu.VMEM((heads, length, 2 * HD), jnp.bfloat16),
                pltpu.VMEM((heads, 2 * HD, length), jnp.bfloat16),
                pltpu.VMEM((heads, length, HD), jnp.bfloat16),
                pltpu.VMEM((heads, HD, length), jnp.bfloat16),
                pltpu.VMEM((heads, HD, length), jnp.bfloat16),
                pltpu.VMEM((heads, 1, length), jnp.float32),
                pltpu.VMEM((heads, HD, length), jnp.float32),
                pltpu.VMEM((heads, HD, TILE), jnp.float32),
                pltpu.VMEM((heads, HD, TILE), jnp.float32),
                pltpu.VMEM((heads, TILE, TILE), jnp.float32)]),
        compiler_params=pltpu.CompilerParams(dimension_semantics=("arbitrary",), vmem_limit_bytes=48 << 20),
        cost_estimate=pl.CostEstimate(flops=30_000_000_000, bytes_accessed=6_000_000, transcendentals=0),
        name="attend_back",
    )(lo, hi, at, seg, qkv, lse, *att, *datt)


def bounds(segments, reach):
    first = segments[:, ::TILE]
    last = segments[:, TILE - 1::TILE]
    n = first.shape[1]
    at = jnp.arange(n)
    per = TILE // KEY_BLOCK
    gap = per * jnp.abs(at[:, None] - at[None, :]) - (per - 1)
    near = gap[None] < reach[:, None, None]
    before = (at[None, :] < at[:, None])[None] & near & (first[:, :, None] == last[:, None, :])
    after = (at[None, :] > at[:, None])[None] & near & (last[:, :, None] == first[:, None, :])
    lo = at[None] - jnp.sum(before, axis=2, dtype=jnp.int32)
    hi = at[None] + 1 + jnp.sum(after, axis=2, dtype=jnp.int32)
    return lo.astype(jnp.int32), hi.astype(jnp.int32)


MESH = pl.DeviceIdType.MESH


def greet(peers):
    barrier = pltpu.get_barrier_semaphore()
    for peer in peers:
        pl.semaphore_signal(barrier, inc=1, device_id=peer, device_id_type=MESH)
    pl.semaphore_wait(barrier, len(peers))


def add_low(left, right):
    return (left.astype(jnp.float32) + right.astype(jnp.float32)).astype(jnp.bfloat16)


class Sends:
    def __init__(self, send_sem, recv_sem):
        self.send_sem, self.recv_sem, self.used, self.open = send_sem, recv_sem, 0, []

    def start(self, src, dst, peer):
        n = self.used
        self.used += 1
        copy = pltpu.make_async_remote_copy(
            src_ref=src, dst_ref=dst, send_sem=self.send_sem.at[n], recv_sem=self.recv_sem.at[n],
            device_id=peer, device_id_type=MESH)
        copy.start()
        self.open.append(copy)
        return copy

    def finish(self):
        for copy in self.open:
            copy.wait_send()


def fold_kernel(zs, micro, heads_in, *refs):
    tokens_in, heads_out, tokens_out = refs[:micro], refs[micro], refs[micro + 1 : 2 * micro + 1]
    h_own, h_y, h_z, h_c, t_own, t_c, t_x, send_sem, recv_sem, load_sem = refs[2 * micro + 1 :]
    c, f = lax.axis_index("ctx"), lax.axis_index("fsdp")
    x, core, z, y = c // 2, c % 2, f // 2, f % 2
    partner = {"ctx": x * 2 + (1 - core), "fsdp": f}
    beside = {"ctx": (1 - x) * 2 + core, "fsdp": f}
    above = {"ctx": c, "fsdp": z * 2 + (1 - y)}
    far = [{"ctx": c, "fsdp": lax.rem(z + s, zs) * 2 + y} for s in range(1, zs)]
    across = [{"ctx": lax.rem(c + s, 4), "fsdp": f} for s in range(1, 4)]
    sends = Sends(send_sem, recv_sem)
    greet([above] + far + across)

    near = 1 + 2 * core
    other = 3 - 2 * core
    loads = []
    def load(src, dst):
        loads.append(pltpu.make_async_copy(src, dst, load_sem.at[len(loads)]))
        loads[-1].start()
        return loads[-1]
    load_there, copy_there, load_here, copy_here = [], [], [], []
    for m in range(micro):
        copy_there.append(sends.start(tokens_in[m].at[other], t_c.at[m, 1], partner))
        load_there.append(load(tokens_in[m].at[2], t_own.at[m, 1]))
    copy_h = sends.start(heads_in.at[:, :, 1 - y], h_y, above)
    load_h = load(heads_in.at[:, :, y], h_own)
    for m in range(micro):
        copy_here.append(sends.start(tokens_in[m].at[near], t_c.at[m, 0], partner))
        load_here.append(load(tokens_in[m].at[0], t_own.at[m, 0]))

    chunks = t_own.shape[2] // 64
    def sum_t(m, place):
        def step(i, _):
            rows = pl.ds(pl.multiple_of(i * 64, 64), 64)
            t_c[m, place, rows, :] = add_low(t_own[m, place, rows, :], t_c[m, place, rows, :])
            return 0
        lax.fori_loop(0, chunks, step, 0)
    copy_tx = []
    for m in range(micro):
        load_there[m].wait(), copy_there[m].wait_recv()
        sum_t(m, 1)
        copy_tx.append(sends.start(t_c.at[m, 1], t_x.at[m], beside))

    load_h.wait(), copy_h.wait_recv()
    def sum_h(i, _):
        a, b = i // zs, lax.rem(i, zs)
        h_y[a, b] = add_low(h_own[a, b], h_y[a, b])
        return 0
    lax.fori_loop(0, 4 * zs, sum_h, 0)
    copy_hz = [sends.start(h_y.at[:, lax.rem(z + s, zs)], h_z.at[s - 1], far[s - 1]) for s in range(1, zs)]
    for m in range(micro):
        load_here[m].wait(), copy_here[m].wait_recv()
        sum_t(m, 0)
    for copy in copy_hz:
        copy.wait_recv()
    def total_h(a, _):
        total = h_y[a, z].astype(jnp.float32)
        for s in range(1, zs):
            total = total + h_z[s - 1, a].astype(jnp.float32)
        h_own[a, 0] = total.astype(jnp.bfloat16)
        return 0
    lax.fori_loop(0, 4, total_h, 0)
    copy_hc = [sends.start(h_own.at[lax.rem(c + s, 4), 0], h_c.at[s - 1], across[s - 1]) for s in range(1, 4)]
    for m in range(micro):
        copy_tx[m].wait_recv()
        def last_t(i, _, m=m):
            rows = pl.ds(pl.multiple_of(i * 64, 64), 64)
            tokens_out[m][rows, :] = t_c[m, 0, rows, :].astype(jnp.float32) + t_x[m, rows, :].astype(jnp.float32)
            return 0
        lax.fori_loop(0, chunks, last_t, 0)
    heads_out[c] = h_own[c, 0].astype(jnp.float32)
    for s in range(1, 4):
        copy_hc[s - 1].wait_recv()
        heads_out[lax.rem(c + 4 - s, 4)] = h_c[s - 1].astype(jnp.float32)
    sends.finish()


def fold(by_head, tokens):
    ctx, fsdp = lax.axis_size("ctx"), lax.axis_size("fsdp")
    zs = fsdp // 2
    assert ctx == 4 and fsdp % 2 == 0
    f32, bf16 = jnp.float32, jnp.bfloat16
    hr, hw = by_head.shape[1:]
    micro = len(tokens)
    _, tr, tw = tokens[0].shape
    copies = 3 * micro + 1 + (zs - 1) + 3
    anywhere, vmem = pl.BlockSpec(memory_space=pl.ANY), pl.BlockSpec(memory_space=pltpu.VMEM)
    return pl.pallas_call(
        functools.partial(fold_kernel, zs, micro),
        out_shape=[jax.ShapeDtypeStruct((4, hr, hw), f32)] + [jax.ShapeDtypeStruct((tr, tw), f32)] * micro,
        in_specs=[anywhere] * (1 + micro), out_specs=[vmem] * (1 + micro),
        scratch_shapes=[
            pltpu.VMEM((4, zs, hr, hw), bf16), pltpu.VMEM((4, zs, hr, hw), bf16), pltpu.VMEM((zs - 1, 4, hr, hw), bf16), pltpu.VMEM((3, hr, hw), bf16),
            pltpu.VMEM((micro, 2, tr, tw), bf16), pltpu.VMEM((micro, 2, tr, tw), bf16), pltpu.VMEM((micro, tr, tw), bf16),
            pltpu.SemaphoreType.DMA((copies,)), pltpu.SemaphoreType.DMA((copies,)), pltpu.SemaphoreType.DMA((1 + 2 * micro,))],
        compiler_params=pltpu.CompilerParams(collective_id=1, has_side_effects=True, vmem_limit_bytes=63 << 20),
        name="fold",
    )(by_head.reshape(4, zs, 2, hr, hw), *tokens)


def collect_kernel(zs, micro, shared, mine, tokens, *refs):
    given, mine_out, refs = refs[:shared], refs[shared], refs[shared + 1 :]
    tokens_out, shared_out, refs = refs[:micro], refs[micro : micro + shared], refs[micro + shared :]
    held_mine, held, held_shared, (send_sem, recv_sem, load_sem) = refs[0], refs[1], refs[2 : 2 + shared], refs[2 + shared :]
    c, f = lax.axis_index("ctx"), lax.axis_index("fsdp")
    x, core, z, y = c // 2, c % 2, f // 2, f % 2
    partner = {"ctx": x * 2 + (1 - core), "fsdp": f}
    beside = {"ctx": (1 - x) * 2 + core, "fsdp": f}
    above = {"ctx": c, "fsdp": z * 2 + (1 - y)}
    far = [{"ctx": c, "fsdp": lax.rem(z + s, zs) * 2 + y} for s in range(1, zs)]
    across = [{"ctx": lax.rem(c + s, 4), "fsdp": f} for s in range(1, 4)]
    greet([above] + far + across)
    sends = Sends(send_sem, recv_sem)
    used = []
    def local(src, dst):
        used.append(pltpu.make_async_copy(src, dst, load_sem.at[len(used)]))
        used[-1].start()
        return used[-1]

    load_mine = local(mine.at[c], held_mine)
    load_shared = [local(given[g], held_shared[g]) for g in range(shared)]
    load_tokens = local(tokens, held)
    first = [sends.start(mine.at[lax.rem(c + s, 4)], mine_out.at[c, z, y], across[s - 1]) for s in range(1, 4)]
    over = [sends.start(given[g], shared_out[g].at[x, core, z, y], beside) for g in range(shared)]
    over_x = [sends.start(tokens.at[m], tokens_out[m].at[2], beside) for m in range(micro)]
    over_core = [sends.start(tokens.at[m], tokens_out[m].at[3 - 2 * core], partner) for m in range(micro)]
    load_mine.wait()
    stores = [local(held_mine, mine_out.at[c, z, y])]
    for g in range(shared):
        load_shared[g].wait()
        stores.append(local(held_shared[g], shared_out[g].at[x, core, z, y]))
    load_tokens.wait()
    later = [local(held.at[m], tokens_out[m].at[0]) for m in range(micro)]
    for copy in first:
        copy.wait_recv()
    stores[0].wait()
    def spread(block, peer):
        return sends.start(block, block, peer)
    over_y = spread(mine_out.at[:, z, y], above)
    own_far = [spread(mine_out.at[:, z, y], peer) for peer in far]
    both = lambda g, there, side: shared_out[g].at[:, core, there, side]
    up, away, aside = [], [], []
    for g in range(shared):
        over[g].wait_recv()
        stores[1 + g].wait()
        away.append([spread(both(g, z, y), peer) for peer in far])
        up.append([spread(both(g, z, y), above)])
        aside.append(spread(both(g, z, y), partner))
    relay = []
    for s in range(1, zs):
        there = lax.rem(z + zs - s, zs)
        own_far[s - 1].wait_recv()
        relay.append(spread(mine_out.at[:, there, y], above))
        for g in range(shared):
            away[g][s - 1].wait_recv()
            up[g].append(spread(both(g, there, y), above))
            aside.append(spread(both(g, there, y), partner))
    for m in range(micro):
        over_x[m].wait_recv()
        relay.append(sends.start(tokens_out[m].at[2], tokens_out[m].at[1 + 2 * core], partner))
    for s in range(zs):
        for g in range(shared):
            up[g][s].wait_recv()
            aside.append(spread(both(g, lax.rem(z + zs - s, zs), 1 - y), partner))
    for copy in [over_y] + over_core + relay + aside:
        copy.wait_recv()
    for copy in later:
        copy.wait()
    sends.finish()


def collect(mine, tokens, shared):
    ctx, fsdp = lax.axis_size("ctx"), lax.axis_size("fsdp")
    zs = fsdp // 2
    assert ctx == 4 and fsdp % 2 == 0
    micro = tokens.shape[0]
    copies = 3 + 1 + 2 * (zs - 1) + 3 * micro + len(shared) * (4 * zs)
    anywhere = pl.BlockSpec(memory_space=pl.ANY)
    vmem = lambda a: pltpu.VMEM(a.shape, a.dtype)
    return pl.pallas_call(
        functools.partial(collect_kernel, zs, micro, len(shared)),
        out_shape=[jax.ShapeDtypeStruct((4, zs, 2) + mine.shape[1:], mine.dtype)] + [jax.ShapeDtypeStruct((4,) + tokens.shape[1:], tokens.dtype)] * micro
        + [jax.ShapeDtypeStruct((2, 2, zs, 2) + a.shape, a.dtype) for a in shared],
        in_specs=[anywhere] * (2 + len(shared)), out_specs=[anywhere] * (1 + micro + len(shared)),
        scratch_shapes=[pltpu.VMEM(mine.shape[1:], mine.dtype), vmem(tokens)] + [vmem(a) for a in shared]
        + [pltpu.SemaphoreType.DMA((copies,)), pltpu.SemaphoreType.DMA((copies,)), pltpu.SemaphoreType.DMA((3 + micro + 2 * len(shared),))],
        compiler_params=pltpu.CompilerParams(collective_id=0, has_side_effects=True),
        name="collect",
    )(mine, tokens, *shared)


def layer_norm(summed, gain, shift):
    row_mean = jnp.mean(summed, axis=-1, keepdims=True)
    centered = summed - row_mean
    variance = jnp.mean(centered * centered, axis=-1, keepdims=True)
    recip = lax.rsqrt(variance + 1e-05)
    normed = centered * recip
    return (normed * gain + shift, normed, recip)


def norm_back(upstream, normed, recip, gain):
    scaled = upstream * gain
    first_mean = jnp.mean(scaled, axis=-1, keepdims=True)
    second_mean = jnp.mean(scaled * normed, axis=-1, keepdims=True)
    d_summed = recip * (scaled - first_mean - normed * second_mean)
    return (d_summed, jnp.sum(upstream * normed, axis=0), jnp.sum(upstream, axis=0))


def dot(left, right):
    return jnp.dot(left, right, preferred_element_type=jnp.float32)


def weight_term(left, right):
    return jnp.einsum("ta,tb->ab", left, right, preferred_element_type=jnp.float32)


def back_term(grad_low, weight):
    return jnp.einsum("tb,ab->ta", grad_low, weight, preferred_element_type=jnp.float32)


def column_sum(grad_low):
    return jnp.sum(grad_low.astype(jnp.float32), axis=0)


def shift(piece, step):
    count = lax.axis_size("ctx")
    return lax.ppermute(piece, "ctx", [(a, (a + step) % count) for a in range(count)])


def body(
    inputs, segments, block_reach,
    query_weight, query_bias, key_weight, value_weight, value_bias, output_weight, output_bias,
    first_gain, first_shift, expand_weight, expand_bias, contract_weight, contract_bias,
    second_gain, second_shift, output_grad,
):
    every = ("ctx", "fsdp")
    ctx = lax.axis_size("ctx")
    me = lax.axis_index("ctx")
    micro, _, rows, width = inputs.shape
    length = rows * ctx
    cols = width // ctx
    heads = cols // HD
    f32, bf16 = jnp.float32, jnp.bfloat16

    share = query_bias.shape[0]
    lines = 8 + expand_bias.shape[0] // share
    ext = -(-share // 8) * 8
    spare = -(-(3 * cols + lines) // 128) * 128 - 3 * cols
    small = jnp.concatenate([v.reshape(-1, share) for v in (
        query_bias, value_bias, output_bias, first_gain, first_shift, contract_bias, second_gain, second_shift, expand_bias)], axis=0)
    small = jnp.pad(small.T, ((0, 0), (0, spare - lines)))
    split = [jnp.stack([w[:, n * cols : (n + 1) * cols] for n in range(ctx)]) for w in (query_weight, key_weight, value_weight)]
    mine = jnp.concatenate(split + [jnp.broadcast_to(small, (ctx,) + small.shape)], axis=2)
    mine = jnp.pad(mine, ((0, 0), (0, ext - share), (0, 0)))

    wide = expand_weight.shape[1] // width
    w_contract = lax.all_gather(contract_weight, every, axis=0, tiled=True)

    rows_up = lambda w: jnp.pad(w, ((0, ext - share), (0, 0)))
    mine_all, *got = collect(mine, inputs[:, 0], [rows_up(expand_weight), rows_up(output_weight)])
    tokens_all, (w_expand, by_owner) = got[:micro], got[micro:]
    tokens_all = [t.reshape(length, width) for t in tokens_all]
    mine_all = mine_all.reshape(-1, ext, 3 * cols + spare)
    devices = mine_all.shape[0]
    w_mine = mine_all[:, :share, : 3 * cols].reshape(width, 3 * cols)
    small_all = mine_all[:, :share, 3 * cols : 3 * cols + lines].astype(f32).reshape(width, lines).T
    b_query, b_value, b_output, g_first, s_first, b_contract, g_second, s_second = [small_all[n] for n in range(8)]
    b_expand = small_all[8:].reshape(-1, devices, share).transpose(1, 0, 2).reshape(-1)

    w_expand = w_expand.reshape(devices, ext, -1)[:, :share].reshape(width, -1)
    by_owner = by_owner.reshape(devices, ext, width)[:, :share].reshape(ctx, cols, width)
    back = [lax.rem(me + ctx - s, ctx) for s in range(ctx)]
    w_output = jnp.concatenate([lax.dynamic_index_in_dim(by_owner, back[s], 0, keepdims=False) for s in range(ctx)], axis=0)

    own = lambda vec: lax.dynamic_slice_in_dim(vec, me * cols, cols, 0)
    b_mine = jnp.concatenate([own(b_query), jnp.zeros((cols,), f32), own(b_value)])
    seg = segments[:, 0]
    reach = block_reach[:, 0]
    lo, hi = bounds(seg, reach)
    at = [jnp.stack([reach[m], me]) for m in range(micro)]

    qkv, att, lse, attended = [], [], [], []
    for m in range(micro):
        flat = tokens_all[m]
        if m:
            flat, _ = lax.optimization_barrier((flat, lse[-1]))
        projected = jnp.einsum("wc,tw->ct", w_mine, flat, preferred_element_type=f32)
        qkv.append((projected + b_mine[:, None]).astype(bf16))
        *pieces, logs = attend(qkv[m], seg[m : m + 1], lo[m], hi[m], at[m], heads, ctx)
        att.append(pieces), lse.append(logs)
        attended.append(jnp.concatenate([pieces[0]] + [shift(pieces[s], s) for s in range(1, ctx)], axis=0))
    attended = jnp.concatenate(attended, axis=1)

    tokens = inputs[:, 0].reshape(micro * rows, width)
    branch = jnp.einsum("ct,cn->tn", attended, w_output, preferred_element_type=f32) + b_output
    hidden, normed_first, recip_first = layer_norm(tokens.astype(f32) + branch, g_first, s_first)
    hidden_low = hidden.astype(bf16)
    pre = dot(hidden_low, w_expand) + b_expand
    phi = 0.5 * (1.0 + lax.erf(pre * (1.0 / math.sqrt(2.0))))
    act_low = (pre * phi).astype(bf16)
    slope = (phi + pre * (jnp.exp(-0.5 * pre * pre) * (1.0 / math.sqrt(2.0 * math.pi)))).astype(bf16)
    act_low, slope = lax.optimization_barrier((act_low, slope))
    second_sum = hidden + dot(act_low, w_contract) + b_contract
    result, normed_second, recip_second = layer_norm(second_sum, g_second, s_second)
    layer_output = result.astype(bf16)
    upstream = output_grad[:, 0].reshape(micro * rows, width).astype(f32)
    d_res2, grad_g2, grad_s2 = norm_back(upstream, normed_second, recip_second, g_second)
    d_ffn = d_res2.astype(bf16)
    grad_b2 = column_sum(d_ffn)
    d_pre = (back_term(d_ffn, w_contract) * slope.astype(f32)).astype(bf16)
    grad_b1 = column_sum(d_pre)
    d_hidden = d_res2 + back_term(d_pre, w_expand)
    d_res1, grad_g1, grad_s1 = norm_back(d_hidden, normed_first, recip_first, g_first)
    d_branch = d_res1.astype(bf16)
    grad_bo = column_sum(d_branch)
    d_attended = [
        jnp.einsum("cn,tn->ct", w_output, d_branch[m * rows : (m + 1) * rows], preferred_element_type=f32).astype(bf16).reshape(ctx, cols, rows)
        for m in range(micro)]

    *d_attended, d_ffn, d_pre, d_branch = lax.optimization_barrier((*d_attended, d_ffn, d_pre, d_branch))
    d_att = [[d_attended[m][0]] + [shift(d_attended[m][s], -s) for s in range(1, ctx)] for m in range(micro)]
    grad_w2 = weight_term(act_low, d_ffn).astype(bf16).reshape(devices, -1, width)
    grad_w1 = [weight_term(hidden_low, d_pre[:, n * width : (n + 1) * width]).astype(bf16).reshape(devices, share, width) for n in range(wide)]
    grad_wo = dot(attended, d_branch).astype(bf16).reshape(ctx, cols, width)
    grad_wo = jnp.concatenate([lax.dynamic_index_in_dim(grad_wo, back[b], 0, keepdims=False) for b in range(ctx)], axis=0).reshape(devices, share, width)
    grads = jnp.concatenate([grad_wo, grad_w2] + grad_w1, axis=1).reshape(-1, width)
    grads = lax.psum_scatter(grads, every, scatter_dimension=0, tiled=True)

    parts, grad_qkv, grad_b = [], 0.0, 0.0
    for m in range(micro):
        d_qkv = attend_back(qkv[m], att[m], d_att[m], lse[m], seg[m : m + 1], lo[m], hi[m], at[m], heads, ctx)
        parts.append(jnp.einsum("ct,nc->tn", d_qkv, w_mine, preferred_element_type=f32).astype(bf16).reshape(ctx, rows, width))
        grad_qkv = grad_qkv + jnp.einsum("tw,ct->wc", tokens_all[m], d_qkv, preferred_element_type=f32)
        grad_b = grad_b + jnp.sum(d_qkv.astype(f32), axis=1)

    place = lambda vec: lax.dynamic_update_slice_in_dim(jnp.zeros((width,), f32), vec, me * cols, 0)
    vectors = [place(grad_b[:cols]), place(grad_b[2 * cols :]), grad_bo, grad_g1, grad_s1, grad_b2, grad_g2, grad_s2]
    stacked = jnp.concatenate([v.reshape(1, width) for v in vectors] + [grad_b1.reshape(devices, -1, share).transpose(1, 0, 2).reshape(-1, width)], axis=0)
    stacked = jnp.pad(stacked.T, ((0, 0), (0, spare - lines)))
    by_head = jnp.concatenate([grad_qkv, stacked], axis=1).astype(bf16).reshape(devices, share, 3 * cols + spare)
    by_head = jnp.pad(by_head, ((0, 0), (0, ext - share), (0, 0)))
    by_head, *summed = fold(by_head, parts)
    token_grad = [d_res1[m * rows : (m + 1) * rows] + summed[m] for m in range(micro)]
    gq, gk, gv = [by_head[:, :share, n * cols : (n + 1) * cols].transpose(1, 0, 2).reshape(share, width) for n in range(3)]
    both = jnp.sum(by_head[:, :share, 3 * cols : 3 * cols + lines], axis=0).T
    gbq, gbv, gbo, gg1, gs1, gb2, gg2, gs2 = [both[n] for n in range(8)]
    gb1 = both[8:].reshape(-1)
    grads = grads.astype(f32)
    gwo, gw2 = grads[:share], grads[share : share + share * wide]
    gw1 = jnp.concatenate([grads[share * (1 + wide + n) : share * (2 + wide + n)] for n in range(wide)], axis=1)
    four = (micro, 1, rows, width)
    return (
        layer_output.reshape(four), jnp.stack(token_grad).reshape(four), gq, gbq, gk, gv, gbv, gwo, gbo, gg1, gs1,
        gw1, gb1, gw2, gb2, gg2, gs2,
    )


def solution(mesh):
    rows = P(("ctx", "fsdp"), None)
    flat = P(("ctx", "fsdp"))
    tokens = P(None, "fsdp", "ctx", None)
    params = (rows, flat, rows, rows, flat, rows, flat, flat, flat, rows, flat, rows, flat, flat, flat)
    return jax.shard_map(
        body,
        mesh=mesh,
        in_specs=(tokens, P(None, "fsdp", None), P(None, "fsdp")) + params + (tokens,),
        out_specs=(tokens, tokens) + params,
        check_vma=False,
    )
```

```python
import functools
import math

import jax
import jax.numpy as jnp
from jax import lax
from jax.experimental import pallas as pl
from jax.experimental.pallas import tpu as pltpu
from jax.sharding import PartitionSpec as P

HD = 64
KEY_BLOCK = 128
TILE = 256
SEG_COUNT = 32
FAR = 1e30

def mask_rows(seg_row, reach, first_block):
    n = seg_row.shape[1]
    row = lax.broadcasted_iota(jnp.int32, (HD, n), 0)
    seg = jnp.broadcast_to(seg_row, (HD, n))
    block = lax.broadcasted_iota(jnp.int32, (HD, n), 1) // KEY_BLOCK + first_block
    is_seg = row < SEG_COUNT
    key_at = row - SEG_COUNT
    far = jnp.logical_not(is_seg) & (jnp.abs(key_at - block) >= reach)
    q_side = jnp.where((is_seg & (seg == row)) | far, -FAR, 0.0)
    k_side = jnp.where((is_seg & (seg != row)) | (key_at == block), 1.0, 0.0)
    return q_side.astype(jnp.bfloat16), k_side.astype(jnp.bfloat16)


def token_block(me, s, count, rows):
    return pl.ds(pl.multiple_of(lax.rem(me + s, count) * rows, rows), rows)


def fwd_kernel(heads, count, lo_ref, hi_ref, at_ref, seg_ref, qkv_ref, *refs):
    att_refs, lse_ref, (kaug, qaug, vtr, att, held_s, held_p) = refs[:count], refs[count], refs[count + 1 :]
    reach, me = at_ref[0], at_ref[1]
    length = qkv_ref.shape[1]
    rows, width = length // count, heads * HD

    def prepare(s, _):
        here = pl.ds(pl.multiple_of(s * rows, rows), rows)
        there = token_block(me, s, count, rows)
        q_side, k_side = mask_rows(seg_ref[:, there], reach, lax.rem(me + s, count) * (rows // KEY_BLOCK))
        for h in range(heads):
            q = qkv_ref[h * HD : (h + 1) * HD, here]
            k = qkv_ref[width + h * HD : width + (h + 1) * HD, here]
            qaug[h, 0:HD, there] = (q.astype(jnp.float32) * (1.0 / math.sqrt(HD))).astype(jnp.bfloat16)
            qaug[h, HD : 2 * HD, there] = q_side
            kaug[h, there, :] = jnp.transpose(jnp.concatenate([k, k_side], axis=0))
            vtr[h, :, there] = qkv_ref[2 * width + h * HD : 2 * width + (h + 1) * HD, here]
        return 0
    lax.fori_loop(0, count, prepare, 0)

    def tile(n):
        return pl.ds(pl.multiple_of(n * TILE, TILE), TILE)

    tiles = length // TILE
    for h in range(heads):
        held_s[h] = jnp.dot(kaug[h, tile(lo_ref[0]), :], qaug[h, :, tile(0)], preferred_element_type=jnp.float32)

    def q_step(i, _):
        qs = tile(i)
        first, end = lo_ref[i], hi_ref[i]
        later = jnp.minimum(i + 1, tiles - 1)

        def k_step(j, carry):
            ks, last = tile(j), j + 1 == end
            after, after_q = tile(jnp.where(last, lo_ref[later], j + 1)), tile(jnp.where(last, later, i))
            out, kept = [], None
            def values(h, peak, total, fade, acc, p):
                out.append((peak, total, fade, acc * fade + jnp.dot(vtr[h, :, ks], p, preferred_element_type=jnp.float32)))
            for h in range(heads):
                peak, total, _, acc = carry[h]
                s = held_s[h]
                new = jnp.maximum(peak, jnp.max(s, axis=0, keepdims=True))
                p = jnp.exp(s - new)
                fade = jnp.exp(peak - new)
                total = total * fade + jnp.sum(p, axis=0, keepdims=True)
                held_s[h] = jnp.dot(kaug[h, after, :], qaug[h, :, after_q], preferred_element_type=jnp.float32)
                if h:
                    values(*kept)
                kept = (h, new, total, fade, acc, p.astype(jnp.bfloat16))
            values(*kept)
            return tuple(out)
        row = lambda value: jnp.full((1, TILE), value, jnp.float32)
        start = tuple((row(-3e38), row(0.0), row(0.0), jnp.zeros((HD, TILE), jnp.float32)) for _ in range(heads))
        done = lax.fori_loop(first, end, k_step, start)
        for h in range(heads):
            peak, total, fade, acc = done[h]
            att[h * HD : (h + 1) * HD, qs] = (acc / total).astype(jnp.bfloat16)
            lse_ref[h : h + 1, qs] = peak + jnp.log(total)
        return 0
    lax.fori_loop(0, tiles, q_step, 0)
    for s in range(count):
        att_refs[s][...] = att[:, token_block(me, s, count, rows)]


def attend(qkv, seg, lo, hi, at, heads, count):
    cols, length = qkv.shape
    width, rows = heads * HD, length // count
    whole = lambda shape: pl.BlockSpec(shape, lambda n, *_: (0, 0))
    return pl.pallas_call(
        functools.partial(fwd_kernel, heads, count),
        out_shape=[jax.ShapeDtypeStruct((width, rows), jnp.bfloat16)] * count + [jax.ShapeDtypeStruct((8, length), jnp.float32)],
        grid_spec=pltpu.PrefetchScalarGridSpec(
            num_scalar_prefetch=3, grid=(1,),
            in_specs=[whole((1, length)), whole((cols, length))],
            out_specs=[whole((width, rows))] * count + [whole((8, length))],
            scratch_shapes=[pltpu.VMEM((heads, length, 2 * HD), jnp.bfloat16), pltpu.VMEM((heads, 2 * HD, length), jnp.bfloat16),
                            pltpu.VMEM((heads, HD, length), jnp.bfloat16), pltpu.VMEM((width, length), jnp.bfloat16),
                            pltpu.VMEM((heads, TILE, TILE), jnp.float32), pltpu.VMEM((heads, TILE, TILE), jnp.bfloat16)]),
        compiler_params=pltpu.CompilerParams(dimension_semantics=("arbitrary",), vmem_limit_bytes=40 << 20),
        cost_estimate=pl.CostEstimate(flops=30_000_000_000, bytes_accessed=4_000_000, transcendentals=0),
        name="attend",
    )(lo, hi, at, seg, qkv)


def bwd_kernel(heads, count, lo_ref, hi_ref, at_ref, seg_ref, qkv_ref, lse_ref, *refs):
    att_refs, datt_refs, dqkv_ref = refs[:count], refs[count : 2 * count], refs[2 * count]
    kaug, qaug, v_nat, dotr, ktr, delta, dqt, dkt, dvt, held_s = refs[2 * count + 1 :]
    reach, me = at_ref[0], at_ref[1]
    length = qkv_ref.shape[1]
    rows, width = length // count, heads * HD
    tiles = length // TILE
    scale = 1.0 / math.sqrt(HD)
    f32, bf16 = jnp.float32, jnp.bfloat16
    for s in range(count):
        there = token_block(me, s, count, rows)
        for h in range(heads):
            do, o = datt_refs[s][h * HD : (h + 1) * HD, :], att_refs[s][h * HD : (h + 1) * HD, :]
            dotr[h, :, there] = do
            delta[h, :, there] = jnp.sum(do.astype(f32) * o.astype(f32), axis=0, keepdims=True)

    def prepare(s, _):
        here = pl.ds(pl.multiple_of(s * rows, rows), rows)
        there = token_block(me, s, count, rows)
        q_side, k_side = mask_rows(seg_ref[:, there], reach, lax.rem(me + s, count) * (rows // KEY_BLOCK))
        for h in range(heads):
            q = qkv_ref[h * HD : (h + 1) * HD, here]
            k = qkv_ref[width + h * HD : width + (h + 1) * HD, here]
            qaug[h, 0:HD, there] = (q.astype(f32) * scale).astype(bf16)
            qaug[h, HD : 2 * HD, there] = q_side
            kaug[h, there, :] = jnp.transpose(jnp.concatenate([k, k_side], axis=0))
            ktr[h, :, there] = k
            v_nat[h, there, :] = jnp.transpose(qkv_ref[2 * width + h * HD : 2 * width + (h + 1) * HD, here])
            dqt[h, :, there] = jnp.zeros((HD, rows), f32)
        return 0
    lax.fori_loop(0, count, prepare, 0)

    def tile(n):
        return pl.ds(pl.multiple_of(n * TILE, TILE), TILE)

    def over_queries(left, right):
        return lax.dot_general(left, right, (((1,), (1,)), ((), ())), preferred_element_type=f32)

    for h in range(heads):
        held_s[h] = jnp.dot(kaug[h, tile(0), :], qaug[h, :, tile(lo_ref[0])], preferred_element_type=f32)

    def k_step(j, _):
        ks = tile(j)
        first, end = lo_ref[j], hi_ref[j]
        later = jnp.minimum(j + 1, tiles - 1)
        dkt[...] = jnp.zeros_like(dkt)
        dvt[...] = jnp.zeros_like(dvt)

        def q_step(i, _):
            qs, last = tile(i), i + 1 == end
            after, after_k = tile(jnp.where(last, lo_ref[later], i + 1)), tile(jnp.where(last, later, j))
            def terms(h, p, ds):
                dvt[h] += over_queries(dotr[h, :, qs], p)
                dkt[h] += over_queries(qaug[h, 0:HD, qs], ds)
                dqt[h, :, qs] += jnp.dot(ktr[h, :, ks], ds, preferred_element_type=f32)

            def to_probs(h):
                return jnp.dot(v_nat[h, ks, :], dotr[h, :, qs], preferred_element_type=f32)
            dp, kept = to_probs(0), None
            for h in range(heads):
                ahead = to_probs(h + 1) if h + 1 < heads else None
                p = jnp.exp(held_s[h] - lse_ref[h : h + 1, qs])
                ds = (p * (dp - delta[h, :, qs])).astype(bf16)
                held_s[h] = jnp.dot(kaug[h, after_k, :], qaug[h, :, after], preferred_element_type=f32)
                if h:
                    terms(h - 1, *kept)
                kept, dp = (p.astype(bf16), ds), ahead
            terms(heads - 1, *kept)
            return 0
        lax.fori_loop(first, end, q_step, 0)
        slot = lax.rem(j // (rows // TILE) + count - me, count)
        out = pl.ds(pl.multiple_of(slot * rows + lax.rem(j, rows // TILE) * TILE, TILE), TILE)
        for h in range(heads):
            dqkv_ref[width + h * HD : width + (h + 1) * HD, out] = dkt[h].astype(bf16)
            dqkv_ref[2 * width + h * HD : 2 * width + (h + 1) * HD, out] = dvt[h].astype(bf16)
        return 0
    lax.fori_loop(0, tiles, k_step, 0)

    def finish(s, _):
        here = pl.ds(pl.multiple_of(s * rows, rows), rows)
        there = token_block(me, s, count, rows)
        for h in range(heads):
            dqkv_ref[h * HD : (h + 1) * HD, here] = (dqt[h, :, there] * scale).astype(bf16)
        return 0
    lax.fori_loop(0, count, finish, 0)


def attend_back(qkv, att, datt, lse, seg, lo, hi, at, heads, count):
    cols, length = qkv.shape
    width, rows = heads * HD, length // count
    whole = lambda shape: pl.BlockSpec(shape, lambda n, *_: (0, 0))
    return pl.pallas_call(
        functools.partial(bwd_kernel, heads, count),
        out_shape=jax.ShapeDtypeStruct((cols, length), jnp.bfloat16),
        grid_spec=pltpu.PrefetchScalarGridSpec(
            num_scalar_prefetch=3, grid=(1,),
            in_specs=[whole((1, length)), whole((cols, length)), whole((8, length))] + [whole((width, rows))] * (2 * count),
            out_specs=whole((cols, length)),
            scratch_shapes=[
                pltpu.VMEM((heads, length, 2 * HD), jnp.bfloat16),
                pltpu.VMEM((heads, 2 * HD, length), jnp.bfloat16),
                pltpu.VMEM((heads, length, HD), jnp.bfloat16),
                pltpu.VMEM((heads, HD, length), jnp.bfloat16),
                pltpu.VMEM((heads, HD, length), jnp.bfloat16),
                pltpu.VMEM((heads, 1, length), jnp.float32),
                pltpu.VMEM((heads, HD, length), jnp.float32),
                pltpu.VMEM((heads, HD, TILE), jnp.float32),
                pltpu.VMEM((heads, HD, TILE), jnp.float32),
                pltpu.VMEM((heads, TILE, TILE), jnp.float32)]),
        compiler_params=pltpu.CompilerParams(dimension_semantics=("arbitrary",), vmem_limit_bytes=48 << 20),
        cost_estimate=pl.CostEstimate(flops=30_000_000_000, bytes_accessed=6_000_000, transcendentals=0),
        name="attend_back",
    )(lo, hi, at, seg, qkv, lse, *att, *datt)


def bounds(segments, reach):
    first = segments[:, ::TILE]
    last = segments[:, TILE - 1::TILE]
    n = first.shape[1]
    at = jnp.arange(n)
    per = TILE // KEY_BLOCK
    gap = per * jnp.abs(at[:, None] - at[None, :]) - (per - 1)
    near = gap[None] < reach[:, None, None]
    before = (at[None, :] < at[:, None])[None] & near & (first[:, :, None] == last[:, None, :])
    after = (at[None, :] > at[:, None])[None] & near & (last[:, :, None] == first[:, None, :])
    lo = at[None] - jnp.sum(before, axis=2, dtype=jnp.int32)
    hi = at[None] + 1 + jnp.sum(after, axis=2, dtype=jnp.int32)
    return lo.astype(jnp.int32), hi.astype(jnp.int32)


MESH = pl.DeviceIdType.MESH


def greet(peers):
    barrier = pltpu.get_barrier_semaphore()
    for peer in peers:
        pl.semaphore_signal(barrier, inc=1, device_id=peer, device_id_type=MESH)
    pl.semaphore_wait(barrier, len(peers))


def add_low(left, right):
    return (left.astype(jnp.float32) + right.astype(jnp.float32)).astype(jnp.bfloat16)


class Sends:
    def __init__(self, send_sem, recv_sem):
        self.send_sem, self.recv_sem, self.used, self.open = send_sem, recv_sem, 0, []

    def start(self, src, dst, peer):
        n = self.used
        self.used += 1
        copy = pltpu.make_async_remote_copy(
            src_ref=src, dst_ref=dst, send_sem=self.send_sem.at[n], recv_sem=self.recv_sem.at[n],
            device_id=peer, device_id_type=MESH)
        copy.start()
        self.open.append(copy)
        return copy

    def finish(self):
        for copy in self.open:
            copy.wait_send()


def fold_kernel(zs, micro, heads_in, *refs):
    tokens_in, groups_out, rest_out, tokens_out = refs[:micro], refs[micro : micro + 3], refs[micro + 3], refs[micro + 4]
    h_own, h_y, h_z, h_c, t_own, t_c, t_x, send_sem, recv_sem, load_sem = refs[micro + 5 :]
    c, f = lax.axis_index("ctx"), lax.axis_index("fsdp")
    x, core, z, y = c // 2, c % 2, f // 2, f % 2
    partner = {"ctx": x * 2 + (1 - core), "fsdp": f}
    beside = {"ctx": (1 - x) * 2 + core, "fsdp": f}
    above = {"ctx": c, "fsdp": z * 2 + (1 - y)}
    far = [{"ctx": c, "fsdp": lax.rem(z + s, zs) * 2 + y} for s in range(1, zs)]
    across = [{"ctx": lax.rem(c + s, 4), "fsdp": f} for s in range(1, 4)]
    sends = Sends(send_sem, recv_sem)
    greet([above] + far + across)

    near = 1 + 2 * core
    other = 3 - 2 * core
    loads = []
    def load(src, dst):
        loads.append(pltpu.make_async_copy(src, dst, load_sem.at[len(loads)]))
        loads[-1].start()
        return loads[-1]
    load_there, copy_there, load_here, copy_here = [], [], [], []
    for m in range(micro):
        copy_there.append(sends.start(tokens_in[m].at[other], t_c.at[m, 1], partner))
        load_there.append(load(tokens_in[m].at[2], t_own.at[m, 1]))
    copy_h = sends.start(heads_in.at[:, :, 1 - y], h_y, above)
    load_h = load(heads_in.at[:, :, y], h_own)
    for m in range(micro):
        copy_here.append(sends.start(tokens_in[m].at[near], t_c.at[m, 0], partner))
        load_here.append(load(tokens_in[m].at[0], t_own.at[m, 0]))

    chunks = t_own.shape[2] // 64
    def sum_t(m, place):
        def step(i, _):
            rows = pl.ds(pl.multiple_of(i * 64, 64), 64)
            t_c[m, place, rows, :] = add_low(t_own[m, place, rows, :], t_c[m, place, rows, :])
            return 0
        lax.fori_loop(0, chunks, step, 0)
    copy_tx = []
    for m in range(micro):
        load_there[m].wait(), copy_there[m].wait_recv()
        sum_t(m, 1)
        copy_tx.append(sends.start(t_c.at[m, 1], t_x.at[m], beside))

    load_h.wait(), copy_h.wait_recv()
    def sum_h(i, _):
        a, b = i // zs, lax.rem(i, zs)
        h_y[a, b] = add_low(h_own[a, b], h_y[a, b])
        return 0
    lax.fori_loop(0, 4 * zs, sum_h, 0)
    copy_hz = [sends.start(h_y.at[:, lax.rem(z + s, zs)], h_z.at[s - 1], far[s - 1]) for s in range(1, zs)]
    for m in range(micro):
        load_here[m].wait(), copy_here[m].wait_recv()
        sum_t(m, 0)
    for copy in copy_hz:
        copy.wait_recv()
    def total_h(a, _):
        total = h_y[a, z].astype(jnp.float32)
        for s in range(1, zs):
            total = total + h_z[s - 1, a].astype(jnp.float32)
        h_own[a, 0] = total.astype(jnp.bfloat16)
        return 0
    lax.fori_loop(0, 4, total_h, 0)
    copy_hc = [sends.start(h_own.at[lax.rem(c + s, 4), 0], h_c.at[c], across[s - 1]) for s in range(1, 4)]
    for m in range(micro):
        copy_tx[m].wait_recv()
        def last_t(i, _, m=m):
            rows = pl.ds(pl.multiple_of(i * 64, 64), 64)
            tokens_out[m, rows, :] = t_c[m, 0, rows, :].astype(jnp.float32) + t_x[m, rows, :].astype(jnp.float32)
            return 0
        lax.fori_loop(0, chunks, last_t, 0)
    h_c[c] = h_own[c, 0]
    for copy in copy_hc:
        copy.wait_recv()
    cols = groups_out[0].shape[1] // 4
    rest = 0.0
    for a in range(4):
        term = h_c[a].astype(jnp.float32)
        for n in range(3):
            groups_out[n][:, a * cols : (a + 1) * cols] = term[:, n * cols : (n + 1) * cols]
        rest = rest + term[:, 3 * cols :]
    rest_out[...] = rest
    sends.finish()


def fold(by_head, tokens, cols):
    ctx, fsdp = lax.axis_size("ctx"), lax.axis_size("fsdp")
    zs = fsdp // 2
    assert ctx == 4 and fsdp % 2 == 0
    f32, bf16 = jnp.float32, jnp.bfloat16
    hr, hw = by_head.shape[1:]
    micro = len(tokens)
    _, tr, tw = tokens[0].shape
    copies = 3 * micro + 1 + (zs - 1) + 3
    anywhere, vmem = pl.BlockSpec(memory_space=pl.ANY), pl.BlockSpec(memory_space=pltpu.VMEM)
    return pl.pallas_call(
        functools.partial(fold_kernel, zs, micro),
        out_shape=[jax.ShapeDtypeStruct((hr, 4 * cols), f32)] * 3 + [jax.ShapeDtypeStruct((hr, hw - 3 * cols), f32), jax.ShapeDtypeStruct((micro, tr, tw), f32)],
        in_specs=[anywhere] * (1 + micro), out_specs=[vmem] * 5,
        scratch_shapes=[
            pltpu.VMEM((4, zs, hr, hw), bf16), pltpu.VMEM((4, zs, hr, hw), bf16), pltpu.VMEM((zs - 1, 4, hr, hw), bf16), pltpu.VMEM((4, hr, hw), bf16),
            pltpu.VMEM((micro, 2, tr, tw), bf16), pltpu.VMEM((micro, 2, tr, tw), bf16), pltpu.VMEM((micro, tr, tw), bf16),
            pltpu.SemaphoreType.DMA((copies,)), pltpu.SemaphoreType.DMA((copies,)), pltpu.SemaphoreType.DMA((1 + 2 * micro,))],
        compiler_params=pltpu.CompilerParams(collective_id=1, has_side_effects=True, vmem_limit_bytes=63 << 20),
        name="fold",
    )(by_head.reshape(4, zs, 2, hr, hw), *tokens)


def collect_kernel(zs, micro, mine, tokens, mine_out, *refs):
    tokens_out, (held_mine, held, send_sem, recv_sem, load_sem) = refs[:micro], refs[micro:]
    c, f = lax.axis_index("ctx"), lax.axis_index("fsdp")
    x, core, z, y = c // 2, c % 2, f // 2, f % 2
    partner = {"ctx": x * 2 + (1 - core), "fsdp": f}
    beside = {"ctx": (1 - x) * 2 + core, "fsdp": f}
    above = {"ctx": c, "fsdp": z * 2 + (1 - y)}
    far = [{"ctx": c, "fsdp": lax.rem(z + s, zs) * 2 + y} for s in range(1, zs)]
    across = [{"ctx": lax.rem(c + s, 4), "fsdp": f} for s in range(1, 4)]
    greet([above] + far + across)
    sends = Sends(send_sem, recv_sem)
    loads = [pltpu.make_async_copy(mine.at[c], held_mine, load_sem.at[0]), pltpu.make_async_copy(tokens, held, load_sem.at[1])]
    for copy in loads:
        copy.start()
    first = [sends.start(mine.at[lax.rem(c + s, 4)], mine_out.at[c, z, y], across[s - 1]) for s in range(1, 4)]
    over_x = [sends.start(tokens.at[m], tokens_out[m].at[2], beside) for m in range(micro)]
    over_core = [sends.start(tokens.at[m], tokens_out[m].at[3 - 2 * core], partner) for m in range(micro)]
    loads[0].wait()
    stores = [pltpu.make_async_copy(held_mine, mine_out.at[c, z, y], load_sem.at[2])]
    stores[0].start()
    loads[1].wait()
    for m in range(micro):
        stores.append(pltpu.make_async_copy(held.at[m], tokens_out[m].at[0], load_sem.at[3 + m]))
        stores[-1].start()
    for copy in first:
        copy.wait_recv()
    stores[0].wait()
    over_y = sends.start(mine_out.at[:, z, y], mine_out.at[:, z, y], above)
    own_far = [sends.start(mine_out.at[:, z, y], mine_out.at[:, z, y], peer) for peer in far]
    up_down = []
    for s in range(1, zs):
        own_far[s - 1].wait_recv()
        there = lax.rem(z + zs - s, zs)
        up_down.append(sends.start(mine_out.at[:, there, y], mine_out.at[:, there, y], above))
    relay = []
    for m in range(micro):
        over_x[m].wait_recv()
        relay.append(sends.start(tokens_out[m].at[2], tokens_out[m].at[1 + 2 * core], partner))
    for copy in [over_y] + over_core + up_down + relay:
        copy.wait_recv()
    for copy in stores[1:]:
        copy.wait()
    sends.finish()


def collect(mine, tokens):
    ctx, fsdp = lax.axis_size("ctx"), lax.axis_size("fsdp")
    zs = fsdp // 2
    assert ctx == 4 and fsdp % 2 == 0
    micro = tokens.shape[0]
    copies = 3 + 1 + 2 * (zs - 1) + 3 * micro
    anywhere = pl.BlockSpec(memory_space=pl.ANY)
    return pl.pallas_call(
        functools.partial(collect_kernel, zs, micro),
        out_shape=[jax.ShapeDtypeStruct((4, zs, 2) + mine.shape[1:], mine.dtype)] + [jax.ShapeDtypeStruct((4,) + tokens.shape[1:], tokens.dtype)] * micro,
        in_specs=[anywhere] * 2, out_specs=[anywhere] * (1 + micro),
        scratch_shapes=[pltpu.VMEM(mine.shape[1:], mine.dtype), pltpu.VMEM(tokens.shape, tokens.dtype), pltpu.SemaphoreType.DMA((copies,)), pltpu.SemaphoreType.DMA((copies,)), pltpu.SemaphoreType.DMA((3 + micro,))],
        compiler_params=pltpu.CompilerParams(collective_id=0, has_side_effects=True),
        name="collect",
    )(mine, tokens)


def layer_norm(summed, gain, shift):
    row_mean = jnp.mean(summed, axis=-1, keepdims=True)
    centered = summed - row_mean
    variance = jnp.mean(centered * centered, axis=-1, keepdims=True)
    recip = lax.rsqrt(variance + 1e-05)
    normed = centered * recip
    return (normed * gain + shift, normed, recip)


def norm_back(upstream, normed, recip, gain):
    scaled = upstream * gain
    first_mean = jnp.mean(scaled, axis=-1, keepdims=True)
    second_mean = jnp.mean(scaled * normed, axis=-1, keepdims=True)
    d_summed = recip * (scaled - first_mean - normed * second_mean)
    return (d_summed, jnp.sum(upstream * normed, axis=0), jnp.sum(upstream, axis=0))


def dot(left, right):
    return jnp.dot(left, right, preferred_element_type=jnp.float32)


def weight_term(left, right):
    return jnp.einsum("ta,tb->ab", left, right, preferred_element_type=jnp.float32)


def back_term(grad_low, weight):
    return jnp.einsum("tb,ab->ta", grad_low, weight, preferred_element_type=jnp.float32)


def column_sum(grad_low):
    return jnp.sum(grad_low.astype(jnp.float32), axis=0)


def shift(piece, step):
    count = lax.axis_size("ctx")
    return lax.ppermute(piece, "ctx", [(a, (a + step) % count) for a in range(count)])


def body(
    inputs, segments, block_reach,
    query_weight, query_bias, key_weight, value_weight, value_bias, output_weight, output_bias,
    first_gain, first_shift, expand_weight, expand_bias, contract_weight, contract_bias,
    second_gain, second_shift, output_grad,
):
    every = ("ctx", "fsdp")
    ctx = lax.axis_size("ctx")
    me = lax.axis_index("ctx")
    micro, _, rows, width = inputs.shape
    length = rows * ctx
    cols = width // ctx
    heads = cols // HD
    f32, bf16 = jnp.float32, jnp.bfloat16

    share = query_bias.shape[0]
    lines = 8 + expand_bias.shape[0] // share
    ext = -(-share // 8) * 8
    spare = -(-(3 * cols + lines) // 128) * 128 - 3 * cols
    small = jnp.concatenate([v.reshape(-1, share) for v in (
        query_bias, value_bias, output_bias, first_gain, first_shift, contract_bias, second_gain, second_shift, expand_bias)], axis=0)
    small = jnp.pad(small.T, ((0, 0), (0, spare - lines)))
    split = [jnp.stack([w[:, n * cols : (n + 1) * cols] for n in range(ctx)]) for w in (query_weight, key_weight, value_weight)]
    mine = jnp.concatenate(split + [jnp.broadcast_to(a, (ctx,) + a.shape) for a in (small, output_weight)], axis=2)
    mine = jnp.pad(mine, ((0, 0), (0, ext - share), (0, 0)))

    wide = expand_weight.shape[1] // width
    packed = jnp.concatenate([contract_weight, expand_weight.reshape(share, wide, width).transpose(1, 0, 2).reshape(-1, width)], axis=0)
    packed = lax.all_gather(packed, every, axis=0, tiled=True)

    mine_all, *tokens_all = collect(mine, inputs[:, 0])
    tokens_all = [t.reshape(length, width) for t in tokens_all]
    mine_all = mine_all.reshape(-1, ext, 3 * cols + spare + width)
    devices = mine_all.shape[0]
    w_mine = mine_all[:, :share, : 3 * cols].reshape(width, 3 * cols)
    small_all = mine_all[:, :share, 3 * cols : 3 * cols + lines].astype(f32).reshape(width, lines).T
    b_query, b_value, b_output, g_first, s_first, b_contract, g_second, s_second = [small_all[n] for n in range(8)]
    b_expand = small_all[8:].reshape(-1, devices, share).transpose(1, 0, 2).reshape(-1)

    packed = packed.reshape(devices, -1, width)
    back = [lax.rem(me + ctx - s, ctx) for s in range(ctx)]
    by_owner = mine_all[:, :share, 3 * cols + spare :].reshape(ctx, cols, width)
    w_output = jnp.concatenate([lax.dynamic_index_in_dim(by_owner, back[s], 0, keepdims=False) for s in range(ctx)], axis=0)
    w_contract = packed[:, : share * wide].reshape(-1, width)
    w_expand = packed[:, share * wide :].reshape(devices, wide, share, width).transpose(0, 2, 1, 3).reshape(width, -1)

    own = lambda vec: lax.dynamic_slice_in_dim(vec, me * cols, cols, 0)
    b_mine = jnp.concatenate([own(b_query), jnp.zeros((cols,), f32), own(b_value)])
    seg = segments[:, 0]
    reach = block_reach[:, 0]
    lo, hi = bounds(seg, reach)
    at = [jnp.stack([reach[m], me]) for m in range(micro)]

    qkv, att, lse, attended = [], [], [], []
    for m in range(micro):
        flat = tokens_all[m]
        if m:
            flat, _ = lax.optimization_barrier((flat, lse[-1]))
        projected = jnp.einsum("wc,tw->ct", w_mine, flat, preferred_element_type=f32)
        qkv.append((projected + b_mine[:, None]).astype(bf16))
        *pieces, logs = attend(qkv[m], seg[m : m + 1], lo[m], hi[m], at[m], heads, ctx)
        att.append(pieces), lse.append(logs)
        attended.append(jnp.concatenate([pieces[0]] + [shift(pieces[s], s) for s in range(1, ctx)], axis=0))
    attended = jnp.concatenate(attended, axis=1)

    tokens = inputs[:, 0].reshape(micro * rows, width)
    branch = jnp.einsum("ct,cn->tn", attended, w_output, preferred_element_type=f32) + b_output
    hidden, normed_first, recip_first = layer_norm(tokens.astype(f32) + branch, g_first, s_first)
    hidden_low = hidden.astype(bf16)
    pre = dot(hidden_low, w_expand) + b_expand
    phi = 0.5 * (1.0 + lax.erf(pre * (1.0 / math.sqrt(2.0))))
    act_low = (pre * phi).astype(bf16)
    slope = (phi + pre * (jnp.exp(-0.5 * pre * pre) * (1.0 / math.sqrt(2.0 * math.pi)))).astype(bf16)
    act_low, slope = lax.optimization_barrier((act_low, slope))
    second_sum = hidden + dot(act_low, w_contract) + b_contract
    result, normed_second, recip_second = layer_norm(second_sum, g_second, s_second)
    layer_output = result.astype(bf16)
    upstream = output_grad[:, 0].reshape(micro * rows, width).astype(f32)
    d_res2, grad_g2, grad_s2 = norm_back(upstream, normed_second, recip_second, g_second)
    d_ffn = d_res2.astype(bf16)
    grad_b2 = column_sum(d_ffn)
    d_pre = (back_term(d_ffn, w_contract) * slope.astype(f32)).astype(bf16)
    grad_b1 = column_sum(d_pre)
    d_hidden = d_res2 + back_term(d_pre, w_expand)
    d_res1, grad_g1, grad_s1 = norm_back(d_hidden, normed_first, recip_first, g_first)
    d_branch = d_res1.astype(bf16)
    grad_bo = column_sum(d_branch)
    d_attended = [
        jnp.einsum("cn,tn->ct", w_output, d_branch[m * rows : (m + 1) * rows], preferred_element_type=f32).astype(bf16).reshape(ctx, cols, rows)
        for m in range(micro)]

    *d_attended, d_ffn, d_pre, d_branch = lax.optimization_barrier((*d_attended, d_ffn, d_pre, d_branch))
    d_att = [[d_attended[m][0]] + [shift(d_attended[m][s], -s) for s in range(1, ctx)] for m in range(micro)]
    grad_w2 = weight_term(act_low, d_ffn).astype(bf16).reshape(devices, -1, width)
    grad_w1 = [weight_term(hidden_low, d_pre[:, n * width : (n + 1) * width]).astype(bf16).reshape(devices, share, width) for n in range(wide)]
    grad_wo = dot(attended, d_branch).astype(bf16).reshape(ctx, cols, width)
    grad_wo = jnp.concatenate([lax.dynamic_index_in_dim(grad_wo, back[b], 0, keepdims=False) for b in range(ctx)], axis=0).reshape(devices, share, width)
    grads = jnp.concatenate([grad_wo, grad_w2] + grad_w1, axis=1).reshape(-1, width)
    grads = lax.psum_scatter(grads, every, scatter_dimension=0, tiled=True)

    parts, grad_qkv, grad_b = [], 0.0, 0.0
    for m in range(micro):
        d_qkv = attend_back(qkv[m], att[m], d_att[m], lse[m], seg[m : m + 1], lo[m], hi[m], at[m], heads, ctx)
        parts.append(jnp.einsum("ct,nc->tn", d_qkv, w_mine, preferred_element_type=f32).astype(bf16).reshape(ctx, rows, width))
        grad_qkv = grad_qkv + jnp.einsum("tw,ct->wc", tokens_all[m], d_qkv, preferred_element_type=f32)
        grad_b = grad_b + jnp.sum(d_qkv.astype(f32), axis=1)

    place = lambda vec: lax.dynamic_update_slice_in_dim(jnp.zeros((width,), f32), vec, me * cols, 0)
    vectors = [place(grad_b[:cols]), place(grad_b[2 * cols :]), grad_bo, grad_g1, grad_s1, grad_b2, grad_g2, grad_s2]
    stacked = jnp.concatenate([v.reshape(1, width) for v in vectors] + [grad_b1.reshape(devices, -1, share).transpose(1, 0, 2).reshape(-1, width)], axis=0)
    stacked = jnp.pad(stacked.T, ((0, 0), (0, spare - lines)))
    by_head = jnp.concatenate([grad_qkv, stacked], axis=1).astype(bf16).reshape(devices, share, 3 * cols + spare)
    by_head = jnp.pad(by_head, ((0, 0), (0, ext - share), (0, 0)))
    gq, gk, gv, both, summed = fold(by_head, parts, cols)
    token_grad = d_res1.reshape(summed.shape) + summed
    gq, gk, gv = gq[:share], gk[:share], gv[:share]
    both = both[:share, :lines].T
    gbq, gbv, gbo, gg1, gs1, gb2, gg2, gs2 = [both[n] for n in range(8)]
    gb1 = both[8:].reshape(-1)
    grads = grads.astype(f32)
    gwo, gw2 = grads[:share], grads[share : share + share * wide]
    gw1 = jnp.concatenate([grads[share * (1 + wide + n) : share * (2 + wide + n)] for n in range(wide)], axis=1)
    four = (micro, 1, rows, width)
    return (
        layer_output.reshape(four), token_grad.reshape(four), gq, gbq, gk, gv, gbv, gwo, gbo, gg1, gs1,
        gw1, gb1, gw2, gb2, gg2, gs2,
    )


def solution(mesh):
    rows = P(("ctx", "fsdp"), None)
    flat = P(("ctx", "fsdp"))
    tokens = P(None, "fsdp", "ctx", None)
    params = (rows, flat, rows, rows, flat, rows, flat, flat, flat, rows, flat, rows, flat, flat, flat)
    return jax.shard_map(
        body,
        mesh=mesh,
        in_specs=(tokens, P(None, "fsdp", None), P(None, "fsdp")) + params + (tokens,),
        out_specs=(tokens, tokens) + params,
        check_vma=False,
    )
```

```python
import functools
import math

import jax
import jax.numpy as jnp
from jax import lax
from jax.experimental import pallas as pl
from jax.experimental.pallas import tpu as pltpu
from jax.sharding import PartitionSpec as P

HD = 64
KEY_BLOCK = 128
TILE = 256
SEG_COUNT = 32
FAR = 1e30

def mask_rows(seg_row, reach, first_block):
    n = seg_row.shape[1]
    row = lax.broadcasted_iota(jnp.int32, (HD, n), 0)
    seg = jnp.broadcast_to(seg_row, (HD, n))
    block = lax.broadcasted_iota(jnp.int32, (HD, n), 1) // KEY_BLOCK + first_block
    is_seg = row < SEG_COUNT
    key_at = row - SEG_COUNT
    far = jnp.logical_not(is_seg) & (jnp.abs(key_at - block) >= reach)
    q_side = jnp.where((is_seg & (seg == row)) | far, -FAR, 0.0)
    k_side = jnp.where((is_seg & (seg != row)) | (key_at == block), 1.0, 0.0)
    return q_side.astype(jnp.bfloat16), k_side.astype(jnp.bfloat16)


def token_block(me, s, count, rows):
    return pl.ds(pl.multiple_of(lax.rem(me + s, count) * rows, rows), rows)


def fwd_kernel(heads, count, lo_ref, hi_ref, at_ref, seg_ref, qkv_ref, *refs):
    att_refs, lse_ref, (kaug, qaug, vtr, att, held_s, held_p) = refs[:count], refs[count], refs[count + 1 :]
    reach, me = at_ref[0], at_ref[1]
    length = qkv_ref.shape[1]
    rows, width = length // count, heads * HD

    def prepare(s, _):
        here = pl.ds(pl.multiple_of(s * rows, rows), rows)
        there = token_block(me, s, count, rows)
        q_side, k_side = mask_rows(seg_ref[:, there], reach, lax.rem(me + s, count) * (rows // KEY_BLOCK))
        for h in range(heads):
            q = qkv_ref[h * HD : (h + 1) * HD, here]
            k = qkv_ref[width + h * HD : width + (h + 1) * HD, here]
            qaug[h, 0:HD, there] = (q.astype(jnp.float32) * (1.0 / math.sqrt(HD))).astype(jnp.bfloat16)
            qaug[h, HD : 2 * HD, there] = q_side
            kaug[h, there, :] = jnp.transpose(jnp.concatenate([k, k_side], axis=0))
            vtr[h, :, there] = qkv_ref[2 * width + h * HD : 2 * width + (h + 1) * HD, here]
        return 0
    lax.fori_loop(0, count, prepare, 0)

    def tile(n):
        return pl.ds(pl.multiple_of(n * TILE, TILE), TILE)

    tiles = length // TILE
    for h in range(heads):
        held_s[h] = jnp.dot(kaug[h, tile(lo_ref[0]), :], qaug[h, :, tile(0)], preferred_element_type=jnp.float32)

    def q_step(i, _):
        qs = tile(i)
        first, end = lo_ref[i], hi_ref[i]
        later = jnp.minimum(i + 1, tiles - 1)

        def k_step(j, carry):
            ks, last = tile(j), j + 1 == end
            after, after_q = tile(jnp.where(last, lo_ref[later], j + 1)), tile(jnp.where(last, later, i))
            out, kept = [], None
            def values(h, peak, total, fade, acc, p):
                out.append((peak, total, fade, acc * fade + jnp.dot(vtr[h, :, ks], p, preferred_element_type=jnp.float32)))
            for h in range(heads):
                peak, total, _, acc = carry[h]
                s = held_s[h]
                new = jnp.maximum(peak, jnp.max(s, axis=0, keepdims=True))
                p = jnp.exp(s - new)
                fade = jnp.exp(peak - new)
                total = total * fade + jnp.sum(p, axis=0, keepdims=True)
                held_s[h] = jnp.dot(kaug[h, after, :], qaug[h, :, after_q], preferred_element_type=jnp.float32)
                if h:
                    values(*kept)
                kept = (h, new, total, fade, acc, p.astype(jnp.bfloat16))
            values(*kept)
            return tuple(out)
        row = lambda value: jnp.full((1, TILE), value, jnp.float32)
        start = tuple((row(-3e38), row(0.0), row(0.0), jnp.zeros((HD, TILE), jnp.float32)) for _ in range(heads))
        done = lax.fori_loop(first, end, k_step, start)
        for h in range(heads):
            peak, total, fade, acc = done[h]
            att[h * HD : (h + 1) * HD, qs] = (acc / total).astype(jnp.bfloat16)
            lse_ref[h : h + 1, qs] = peak + jnp.log(total)
        return 0
    lax.fori_loop(0, tiles, q_step, 0)
    for s in range(count):
        att_refs[s][...] = att[:, token_block(me, s, count, rows)]


def attend(qkv, seg, lo, hi, at, heads, count):
    cols, length = qkv.shape
    width, rows = heads * HD, length // count
    whole = lambda shape: pl.BlockSpec(shape, lambda n, *_: (0, 0))
    return pl.pallas_call(
        functools.partial(fwd_kernel, heads, count),
        out_shape=[jax.ShapeDtypeStruct((width, rows), jnp.bfloat16)] * count + [jax.ShapeDtypeStruct((8, length), jnp.float32)],
        grid_spec=pltpu.PrefetchScalarGridSpec(
            num_scalar_prefetch=3, grid=(1,),
            in_specs=[whole((1, length)), whole((cols, length))],
            out_specs=[whole((width, rows))] * count + [whole((8, length))],
            scratch_shapes=[pltpu.VMEM((heads, length, 2 * HD), jnp.bfloat16), pltpu.VMEM((heads, 2 * HD, length), jnp.bfloat16),
                            pltpu.VMEM((heads, HD, length), jnp.bfloat16), pltpu.VMEM((width, length), jnp.bfloat16),
                            pltpu.VMEM((heads, TILE, TILE), jnp.float32), pltpu.VMEM((heads, TILE, TILE), jnp.bfloat16)]),
        compiler_params=pltpu.CompilerParams(dimension_semantics=("arbitrary",), vmem_limit_bytes=40 << 20),
        cost_estimate=pl.CostEstimate(flops=30_000_000_000, bytes_accessed=4_000_000, transcendentals=0),
        name="attend",
    )(lo, hi, at, seg, qkv)


def bwd_kernel(heads, count, lo_ref, hi_ref, at_ref, seg_ref, qkv_ref, lse_ref, *refs):
    att_refs, datt_refs, dqkv_ref = refs[:count], refs[count : 2 * count], refs[2 * count]
    kaug, qaug, v_nat, dotr, ktr, delta, dqt, dkt, dvt, held_s = refs[2 * count + 1 :]
    reach, me = at_ref[0], at_ref[1]
    length = qkv_ref.shape[1]
    rows, width = length // count, heads * HD
    tiles = length // TILE
    scale = 1.0 / math.sqrt(HD)
    f32, bf16 = jnp.float32, jnp.bfloat16
    for s in range(count):
        there = token_block(me, s, count, rows)
        for h in range(heads):
            do, o = datt_refs[s][h * HD : (h + 1) * HD, :], att_refs[s][h * HD : (h + 1) * HD, :]
            dotr[h, :, there] = do
            delta[h, :, there] = jnp.sum(do.astype(f32) * o.astype(f32), axis=0, keepdims=True)

    def prepare(s, _):
        here = pl.ds(pl.multiple_of(s * rows, rows), rows)
        there = token_block(me, s, count, rows)
        q_side, k_side = mask_rows(seg_ref[:, there], reach, lax.rem(me + s, count) * (rows // KEY_BLOCK))
        for h in range(heads):
            q = qkv_ref[h * HD : (h + 1) * HD, here]
            k = qkv_ref[width + h * HD : width + (h + 1) * HD, here]
            qaug[h, 0:HD, there] = (q.astype(f32) * scale).astype(bf16)
            qaug[h, HD : 2 * HD, there] = q_side
            kaug[h, there, :] = jnp.transpose(jnp.concatenate([k, k_side], axis=0))
            ktr[h, :, there] = k
            v_nat[h, there, :] = jnp.transpose(qkv_ref[2 * width + h * HD : 2 * width + (h + 1) * HD, here])
            dqt[h, :, there] = jnp.zeros((HD, rows), f32)
        return 0
    lax.fori_loop(0, count, prepare, 0)

    def tile(n):
        return pl.ds(pl.multiple_of(n * TILE, TILE), TILE)

    def over_queries(left, right):
        return lax.dot_general(left, right, (((1,), (1,)), ((), ())), preferred_element_type=f32)

    for h in range(heads):
        held_s[h] = jnp.dot(kaug[h, tile(0), :], qaug[h, :, tile(lo_ref[0])], preferred_element_type=f32)

    def k_step(j, _):
        ks = tile(j)
        first, end = lo_ref[j], hi_ref[j]
        later = jnp.minimum(j + 1, tiles - 1)
        dkt[...] = jnp.zeros_like(dkt)
        dvt[...] = jnp.zeros_like(dvt)

        def q_step(i, _):
            qs, last = tile(i), i + 1 == end
            after, after_k = tile(jnp.where(last, lo_ref[later], i + 1)), tile(jnp.where(last, later, j))
            def terms(h, p, ds):
                dvt[h] += over_queries(dotr[h, :, qs], p)
                dkt[h] += over_queries(qaug[h, 0:HD, qs], ds)
                dqt[h, :, qs] += jnp.dot(ktr[h, :, ks], ds, preferred_element_type=f32)

            def to_probs(h):
                return jnp.dot(v_nat[h, ks, :], dotr[h, :, qs], preferred_element_type=f32)
            dp, kept = to_probs(0), None
            for h in range(heads):
                ahead = to_probs(h + 1) if h + 1 < heads else None
                p = jnp.exp(held_s[h] - lse_ref[h : h + 1, qs])
                ds = (p * (dp - delta[h, :, qs])).astype(bf16)
                held_s[h] = jnp.dot(kaug[h, after_k, :], qaug[h, :, after], preferred_element_type=f32)
                if h:
                    terms(h - 1, *kept)
                kept, dp = (p.astype(bf16), ds), ahead
            terms(heads - 1, *kept)
            return 0
        lax.fori_loop(first, end, q_step, 0)
        slot = lax.rem(j // (rows // TILE) + count - me, count)
        out = pl.ds(pl.multiple_of(slot * rows + lax.rem(j, rows // TILE) * TILE, TILE), TILE)
        for h in range(heads):
            dqkv_ref[width + h * HD : width + (h + 1) * HD, out] = dkt[h].astype(bf16)
            dqkv_ref[2 * width + h * HD : 2 * width + (h + 1) * HD, out] = dvt[h].astype(bf16)
        return 0
    lax.fori_loop(0, tiles, k_step, 0)

    def finish(s, _):
        here = pl.ds(pl.multiple_of(s * rows, rows), rows)
        there = token_block(me, s, count, rows)
        for h in range(heads):
            dqkv_ref[h * HD : (h + 1) * HD, here] = (dqt[h, :, there] * scale).astype(bf16)
        return 0
    lax.fori_loop(0, count, finish, 0)


def attend_back(qkv, att, datt, lse, seg, lo, hi, at, heads, count):
    cols, length = qkv.shape
    width, rows = heads * HD, length // count
    whole = lambda shape: pl.BlockSpec(shape, lambda n, *_: (0, 0))
    return pl.pallas_call(
        functools.partial(bwd_kernel, heads, count),
        out_shape=jax.ShapeDtypeStruct((cols, length), jnp.bfloat16),
        grid_spec=pltpu.PrefetchScalarGridSpec(
            num_scalar_prefetch=3, grid=(1,),
            in_specs=[whole((1, length)), whole((cols, length)), whole((8, length))] + [whole((width, rows))] * (2 * count),
            out_specs=whole((cols, length)),
            scratch_shapes=[
                pltpu.VMEM((heads, length, 2 * HD), jnp.bfloat16),
                pltpu.VMEM((heads, 2 * HD, length), jnp.bfloat16),
                pltpu.VMEM((heads, length, HD), jnp.bfloat16),
                pltpu.VMEM((heads, HD, length), jnp.bfloat16),
                pltpu.VMEM((heads, HD, length), jnp.bfloat16),
                pltpu.VMEM((heads, 1, length), jnp.float32),
                pltpu.VMEM((heads, HD, length), jnp.float32),
                pltpu.VMEM((heads, HD, TILE), jnp.float32),
                pltpu.VMEM((heads, HD, TILE), jnp.float32),
                pltpu.VMEM((heads, TILE, TILE), jnp.float32)]),
        compiler_params=pltpu.CompilerParams(dimension_semantics=("arbitrary",), vmem_limit_bytes=48 << 20),
        cost_estimate=pl.CostEstimate(flops=30_000_000_000, bytes_accessed=6_000_000, transcendentals=0),
        name="attend_back",
    )(lo, hi, at, seg, qkv, lse, *att, *datt)


def bounds(segments, reach):
    first = segments[:, ::TILE]
    last = segments[:, TILE - 1::TILE]
    n = first.shape[1]
    at = jnp.arange(n)
    per = TILE // KEY_BLOCK
    gap = per * jnp.abs(at[:, None] - at[None, :]) - (per - 1)
    near = gap[None] < reach[:, None, None]
    before = (at[None, :] < at[:, None])[None] & near & (first[:, :, None] == last[:, None, :])
    after = (at[None, :] > at[:, None])[None] & near & (last[:, :, None] == first[:, None, :])
    lo = at[None] - jnp.sum(before, axis=2, dtype=jnp.int32)
    hi = at[None] + 1 + jnp.sum(after, axis=2, dtype=jnp.int32)
    return lo.astype(jnp.int32), hi.astype(jnp.int32)


MESH = pl.DeviceIdType.MESH


def greet(peers):
    barrier = pltpu.get_barrier_semaphore()
    for peer in peers:
        pl.semaphore_signal(barrier, inc=1, device_id=peer, device_id_type=MESH)
    pl.semaphore_wait(barrier, len(peers))


def add_low(left, right):
    return (left.astype(jnp.float32) + right.astype(jnp.float32)).astype(jnp.bfloat16)


class Sends:
    def __init__(self, send_sem, recv_sem):
        self.send_sem, self.recv_sem, self.used, self.open = send_sem, recv_sem, 0, []

    def start(self, src, dst, peer):
        n = self.used
        self.used += 1
        copy = pltpu.make_async_remote_copy(
            src_ref=src, dst_ref=dst, send_sem=self.send_sem.at[n], recv_sem=self.recv_sem.at[n],
            device_id=peer, device_id_type=MESH)
        copy.start()
        self.open.append(copy)
        return copy

    def finish(self):
        for copy in self.open:
            copy.wait_send()


def fold_kernel(zs, micro, heads_in, *refs):
    tokens_in, groups_out, rest_out, tokens_out = refs[:micro], refs[micro : micro + 3], refs[micro + 3], refs[micro + 4]
    h_own, h_y, h_z, h_c, t_own, t_c, t_x, send_sem, recv_sem, load_sem = refs[micro + 5 :]
    c, f = lax.axis_index("ctx"), lax.axis_index("fsdp")
    x, core, z, y = c // 2, c % 2, f // 2, f % 2
    partner = {"ctx": x * 2 + (1 - core), "fsdp": f}
    beside = {"ctx": (1 - x) * 2 + core, "fsdp": f}
    above = {"ctx": c, "fsdp": z * 2 + (1 - y)}
    far = [{"ctx": c, "fsdp": lax.rem(z + s, zs) * 2 + y} for s in range(1, zs)]
    across = [{"ctx": lax.rem(c + s, 4), "fsdp": f} for s in range(1, 4)]
    sends = Sends(send_sem, recv_sem)
    greet([above] + far + across)

    near = 1 + 2 * core
    other = 3 - 2 * core
    loads = []
    def load(src, dst):
        loads.append(pltpu.make_async_copy(src, dst, load_sem.at[len(loads)]))
        loads[-1].start()
        return loads[-1]
    load_there, copy_there, load_here, copy_here = [], [], [], []
    for m in range(micro):
        copy_there.append(sends.start(tokens_in[m].at[other], t_c.at[m, 1], partner))
        load_there.append(load(tokens_in[m].at[2], t_own.at[m, 1]))
    copy_h = sends.start(heads_in.at[:, :, 1 - y], h_y, above)
    load_h = load(heads_in.at[:, :, y], h_own)
    for m in range(micro):
        copy_here.append(sends.start(tokens_in[m].at[near], t_c.at[m, 0], partner))
        load_here.append(load(tokens_in[m].at[0], t_own.at[m, 0]))

    chunks = t_own.shape[2] // 64
    def sum_t(m, place):
        def step(i, _):
            rows = pl.ds(pl.multiple_of(i * 64, 64), 64)
            t_c[m, place, rows, :] = add_low(t_own[m, place, rows, :], t_c[m, place, rows, :])
            return 0
        lax.fori_loop(0, chunks, step, 0)
    copy_tx = []
    for m in range(micro):
        load_there[m].wait(), copy_there[m].wait_recv()
        sum_t(m, 1)
        copy_tx.append(sends.start(t_c.at[m, 1], t_x.at[m], beside))

    load_h.wait(), copy_h.wait_recv()
    def sum_h(i, _):
        a, b = i // zs, lax.rem(i, zs)
        h_y[a, b] = add_low(h_own[a, b], h_y[a, b])
        return 0
    lax.fori_loop(0, 4 * zs, sum_h, 0)
    copy_hz = [sends.start(h_y.at[:, lax.rem(z + s, zs)], h_z.at[s - 1], far[s - 1]) for s in range(1, zs)]
    for m in range(micro):
        load_here[m].wait(), copy_here[m].wait_recv()
        sum_t(m, 0)
    for copy in copy_hz:
        copy.wait_recv()
    def total_h(a, _):
        total = h_y[a, z].astype(jnp.float32)
        for s in range(1, zs):
            total = total + h_z[s - 1, a].astype(jnp.float32)
        h_own[a, 0] = total.astype(jnp.bfloat16)
        return 0
    lax.fori_loop(0, 4, total_h, 0)
    copy_hc = [sends.start(h_own.at[lax.rem(c + s, 4), 0], h_c.at[c], across[s - 1]) for s in range(1, 4)]
    for m in range(micro):
        copy_tx[m].wait_recv()
        def last_t(i, _, m=m):
            rows = pl.ds(pl.multiple_of(i * 64, 64), 64)
            tokens_out[m, rows, :] = t_c[m, 0, rows, :].astype(jnp.float32) + t_x[m, rows, :].astype(jnp.float32)
            return 0
        lax.fori_loop(0, chunks, last_t, 0)
    h_c[c] = h_own[c, 0]
    for copy in copy_hc:
        copy.wait_recv()
    cols = groups_out[0].shape[1] // 4
    rest = 0.0
    for a in range(4):
        term = h_c[a].astype(jnp.float32)
        for n in range(3):
            groups_out[n][:, a * cols : (a + 1) * cols] = term[:, n * cols : (n + 1) * cols]
        rest = rest + term[:, 3 * cols :]
    rest_out[...] = rest
    sends.finish()


def fold(by_head, tokens, cols):
    ctx, fsdp = lax.axis_size("ctx"), lax.axis_size("fsdp")
    zs = fsdp // 2
    assert ctx == 4 and fsdp % 2 == 0
    f32, bf16 = jnp.float32, jnp.bfloat16
    hr, hw = by_head.shape[1:]
    micro = len(tokens)
    _, tr, tw = tokens[0].shape
    copies = 3 * micro + 1 + (zs - 1) + 3
    anywhere, vmem = pl.BlockSpec(memory_space=pl.ANY), pl.BlockSpec(memory_space=pltpu.VMEM)
    return pl.pallas_call(
        functools.partial(fold_kernel, zs, micro),
        out_shape=[jax.ShapeDtypeStruct((hr, 4 * cols), f32)] * 3 + [jax.ShapeDtypeStruct((hr, hw - 3 * cols), f32), jax.ShapeDtypeStruct((micro, tr, tw), f32)],
        in_specs=[anywhere] * (1 + micro), out_specs=[vmem] * 5,
        scratch_shapes=[
            pltpu.VMEM((4, zs, hr, hw), bf16), pltpu.VMEM((4, zs, hr, hw), bf16), pltpu.VMEM((zs - 1, 4, hr, hw), bf16), pltpu.VMEM((4, hr, hw), bf16),
            pltpu.VMEM((micro, 2, tr, tw), bf16), pltpu.VMEM((micro, 2, tr, tw), bf16), pltpu.VMEM((micro, tr, tw), bf16),
            pltpu.SemaphoreType.DMA((copies,)), pltpu.SemaphoreType.DMA((copies,)), pltpu.SemaphoreType.DMA((1 + 2 * micro,))],
        compiler_params=pltpu.CompilerParams(collective_id=1, has_side_effects=True, vmem_limit_bytes=63 << 20),
        name="fold",
    )(by_head.reshape(4, zs, 2, hr, hw), *tokens)


def collect_kernel(zs, micro, mine, tokens, mine_out, *refs):
    tokens_out, (held_mine, held, send_sem, recv_sem, load_sem) = refs[:micro], refs[micro:]
    c, f = lax.axis_index("ctx"), lax.axis_index("fsdp")
    x, core, z, y = c // 2, c % 2, f // 2, f % 2
    partner = {"ctx": x * 2 + (1 - core), "fsdp": f}
    beside = {"ctx": (1 - x) * 2 + core, "fsdp": f}
    above = {"ctx": c, "fsdp": z * 2 + (1 - y)}
    far = [{"ctx": c, "fsdp": lax.rem(z + s, zs) * 2 + y} for s in range(1, zs)]
    across = [{"ctx": lax.rem(c + s, 4), "fsdp": f} for s in range(1, 4)]
    greet([above] + far + across)
    sends = Sends(send_sem, recv_sem)
    loads = [pltpu.make_async_copy(mine.at[c], held_mine, load_sem.at[0]), pltpu.make_async_copy(tokens, held, load_sem.at[1])]
    for copy in loads:
        copy.start()
    first = [sends.start(mine.at[lax.rem(c + s, 4)], mine_out.at[c, z, y], across[s - 1]) for s in range(1, 4)]
    over_x = [sends.start(tokens.at[m], tokens_out[m].at[2], beside) for m in range(micro)]
    over_core = [sends.start(tokens.at[m], tokens_out[m].at[3 - 2 * core], partner) for m in range(micro)]
    loads[0].wait()
    stores = [pltpu.make_async_copy(held_mine, mine_out.at[c, z, y], load_sem.at[2])]
    stores[0].start()
    loads[1].wait()
    for m in range(micro):
        stores.append(pltpu.make_async_copy(held.at[m], tokens_out[m].at[0], load_sem.at[3 + m]))
        stores[-1].start()
    for copy in first:
        copy.wait_recv()
    stores[0].wait()
    over_y = sends.start(mine_out.at[:, z, y], mine_out.at[:, z, y], above)
    own_far = [sends.start(mine_out.at[:, z, y], mine_out.at[:, z, y], peer) for peer in far]
    up_down = []
    for s in range(1, zs):
        own_far[s - 1].wait_recv()
        there = lax.rem(z + zs - s, zs)
        up_down.append(sends.start(mine_out.at[:, there, y], mine_out.at[:, there, y], above))
    relay = []
    for m in range(micro):
        over_x[m].wait_recv()
        relay.append(sends.start(tokens_out[m].at[2], tokens_out[m].at[1 + 2 * core], partner))
    for copy in [over_y] + over_core + up_down + relay:
        copy.wait_recv()
    for copy in stores[1:]:
        copy.wait()
    sends.finish()


def collect(mine, tokens):
    ctx, fsdp = lax.axis_size("ctx"), lax.axis_size("fsdp")
    zs = fsdp // 2
    assert ctx == 4 and fsdp % 2 == 0
    micro = tokens.shape[0]
    copies = 3 + 1 + 2 * (zs - 1) + 3 * micro
    anywhere = pl.BlockSpec(memory_space=pl.ANY)
    return pl.pallas_call(
        functools.partial(collect_kernel, zs, micro),
        out_shape=[jax.ShapeDtypeStruct((4, zs, 2) + mine.shape[1:], mine.dtype)] + [jax.ShapeDtypeStruct((4,) + tokens.shape[1:], tokens.dtype)] * micro,
        in_specs=[anywhere] * 2, out_specs=[anywhere] * (1 + micro),
        scratch_shapes=[pltpu.VMEM(mine.shape[1:], mine.dtype), pltpu.VMEM(tokens.shape, tokens.dtype), pltpu.SemaphoreType.DMA((copies,)), pltpu.SemaphoreType.DMA((copies,)), pltpu.SemaphoreType.DMA((3 + micro,))],
        compiler_params=pltpu.CompilerParams(collective_id=0, has_side_effects=True),
        name="collect",
    )(mine, tokens)


def layer_norm(summed, gain, shift):
    row_mean = jnp.mean(summed, axis=-1, keepdims=True)
    centered = summed - row_mean
    variance = jnp.mean(centered * centered, axis=-1, keepdims=True)
    recip = lax.rsqrt(variance + 1e-05)
    normed = centered * recip
    return (normed * gain + shift, normed, recip)


def norm_back(upstream, normed, recip, gain):
    scaled = upstream * gain
    first_mean = jnp.mean(scaled, axis=-1, keepdims=True)
    second_mean = jnp.mean(scaled * normed, axis=-1, keepdims=True)
    d_summed = recip * (scaled - first_mean - normed * second_mean)
    return (d_summed, jnp.sum(upstream * normed, axis=0), jnp.sum(upstream, axis=0))


def dot(left, right):
    return jnp.dot(left, right, preferred_element_type=jnp.float32)


def weight_term(left, right):
    return jnp.einsum("ta,tb->ab", left, right, preferred_element_type=jnp.float32)


def back_term(grad_low, weight):
    return jnp.einsum("tb,ab->ta", grad_low, weight, preferred_element_type=jnp.float32)


def column_sum(grad_low):
    return jnp.sum(grad_low.astype(jnp.float32), axis=0)


def shift(piece, step):
    count = lax.axis_size("ctx")
    return lax.ppermute(piece, "ctx", [(a, (a + step) % count) for a in range(count)])


def body(
    inputs, segments, block_reach,
    query_weight, query_bias, key_weight, value_weight, value_bias, output_weight, output_bias,
    first_gain, first_shift, expand_weight, expand_bias, contract_weight, contract_bias,
    second_gain, second_shift, output_grad,
):
    every = ("ctx", "fsdp")
    ctx = lax.axis_size("ctx")
    me = lax.axis_index("ctx")
    micro, _, rows, width = inputs.shape
    length = rows * ctx
    cols = width // ctx
    heads = cols // HD
    f32, bf16 = jnp.float32, jnp.bfloat16

    share = query_bias.shape[0]
    lines = 8 + expand_bias.shape[0] // share
    ext = -(-share // 8) * 8
    spare = -(-(3 * cols + lines) // 128) * 128 - 3 * cols
    small = jnp.concatenate([v.reshape(-1, share) for v in (
        query_bias, value_bias, output_bias, first_gain, first_shift, contract_bias, second_gain, second_shift, expand_bias)], axis=0)
    small = jnp.pad(small.T, ((0, 0), (0, spare - lines)))
    split = [jnp.stack([w[:, n * cols : (n + 1) * cols] for n in range(ctx)]) for w in (query_weight, key_weight, value_weight)]
    mine = jnp.concatenate(split + [jnp.broadcast_to(small, (ctx,) + small.shape)], axis=2)
    mine = jnp.pad(mine, ((0, 0), (0, ext - share), (0, 0)))

    wide = expand_weight.shape[1] // width
    packed = jnp.concatenate([output_weight, contract_weight, expand_weight.reshape(share, wide, width).transpose(1, 0, 2).reshape(-1, width)], axis=0)
    packed = lax.all_gather(packed, every, axis=0, tiled=True)

    mine_all, *tokens_all = collect(mine, inputs[:, 0])
    tokens_all = [t.reshape(length, width) for t in tokens_all]
    mine_all = mine_all.reshape(-1, ext, 3 * cols + spare)
    devices = mine_all.shape[0]
    w_mine = mine_all[:, :share, : 3 * cols].reshape(width, 3 * cols)
    small_all = mine_all[:, :share, 3 * cols : 3 * cols + lines].astype(f32).reshape(width, lines).T
    b_query, b_value, b_output, g_first, s_first, b_contract, g_second, s_second = [small_all[n] for n in range(8)]
    b_expand = small_all[8:].reshape(-1, devices, share).transpose(1, 0, 2).reshape(-1)

    packed = packed.reshape(devices, -1, width)
    back = [lax.rem(me + ctx - s, ctx) for s in range(ctx)]
    by_owner = packed[:, :share].reshape(ctx, cols, width)
    w_output = jnp.concatenate([lax.dynamic_index_in_dim(by_owner, back[s], 0, keepdims=False) for s in range(ctx)], axis=0)
    w_contract = packed[:, share : share + share * wide].reshape(-1, width)
    w_expand = packed[:, share + share * wide :].reshape(devices, wide, share, width).transpose(0, 2, 1, 3).reshape(width, -1)

    own = lambda vec: lax.dynamic_slice_in_dim(vec, me * cols, cols, 0)
    b_mine = jnp.concatenate([own(b_query), jnp.zeros((cols,), f32), own(b_value)])
    seg = segments[:, 0]
    reach = block_reach[:, 0]
    lo, hi = bounds(seg, reach)
    at = [jnp.stack([reach[m], me]) for m in range(micro)]

    qkv, att, lse, attended = [], [], [], []
    for m in range(micro):
        flat = tokens_all[m]
        if m:
            flat, _ = lax.optimization_barrier((flat, lse[-1]))
        projected = jnp.einsum("wc,tw->ct", w_mine, flat, preferred_element_type=f32)
        qkv.append((projected + b_mine[:, None]).astype(bf16))
        *pieces, logs = attend(qkv[m], seg[m : m + 1], lo[m], hi[m], at[m], heads, ctx)
        att.append(pieces), lse.append(logs)
        attended.append(jnp.concatenate([pieces[0]] + [shift(pieces[s], s) for s in range(1, ctx)], axis=0))
    attended = jnp.concatenate(attended, axis=1)

    tokens = inputs[:, 0].reshape(micro * rows, width)
    branch = jnp.einsum("ct,cn->tn", attended, w_output, preferred_element_type=f32) + b_output
    hidden, normed_first, recip_first = layer_norm(tokens.astype(f32) + branch, g_first, s_first)
    hidden_low = hidden.astype(bf16)
    pre = dot(hidden_low, w_expand) + b_expand
    phi = 0.5 * (1.0 + lax.erf(pre * (1.0 / math.sqrt(2.0))))
    act_low = (pre * phi).astype(bf16)
    slope = (phi + pre * (jnp.exp(-0.5 * pre * pre) * (1.0 / math.sqrt(2.0 * math.pi)))).astype(bf16)
    act_low, slope = lax.optimization_barrier((act_low, slope))
    second_sum = hidden + dot(act_low, w_contract) + b_contract
    result, normed_second, recip_second = layer_norm(second_sum, g_second, s_second)
    layer_output = result.astype(bf16)
    upstream = output_grad[:, 0].reshape(micro * rows, width).astype(f32)
    d_res2, grad_g2, grad_s2 = norm_back(upstream, normed_second, recip_second, g_second)
    d_ffn = d_res2.astype(bf16)
    grad_b2 = column_sum(d_ffn)
    d_pre = (back_term(d_ffn, w_contract) * slope.astype(f32)).astype(bf16)
    grad_b1 = column_sum(d_pre)
    d_hidden = d_res2 + back_term(d_pre, w_expand)
    d_res1, grad_g1, grad_s1 = norm_back(d_hidden, normed_first, recip_first, g_first)
    d_branch = d_res1.astype(bf16)
    grad_bo = column_sum(d_branch)
    d_attended = [
        jnp.einsum("cn,tn->ct", w_output, d_branch[m * rows : (m + 1) * rows], preferred_element_type=f32).astype(bf16).reshape(ctx, cols, rows)
        for m in range(micro)]

    *d_attended, d_ffn, d_pre, d_branch = lax.optimization_barrier((*d_attended, d_ffn, d_pre, d_branch))
    d_att = [[d_attended[m][0]] + [shift(d_attended[m][s], -s) for s in range(1, ctx)] for m in range(micro)]
    grad_w2 = weight_term(act_low, d_ffn).astype(bf16).reshape(devices, -1, width)
    grad_w1 = [weight_term(hidden_low, d_pre[:, n * width : (n + 1) * width]).astype(bf16).reshape(devices, share, width) for n in range(wide)]
    grad_wo = dot(attended, d_branch).astype(bf16).reshape(ctx, cols, width)
    grad_wo = jnp.concatenate([lax.dynamic_index_in_dim(grad_wo, back[b], 0, keepdims=False) for b in range(ctx)], axis=0).reshape(devices, share, width)
    grads = jnp.concatenate([grad_wo, grad_w2] + grad_w1, axis=1).reshape(-1, width)
    grads = lax.psum_scatter(grads, every, scatter_dimension=0, tiled=True)

    parts, grad_qkv, grad_b = [], 0.0, 0.0
    for m in range(micro):
        d_qkv = attend_back(qkv[m], att[m], d_att[m], lse[m], seg[m : m + 1], lo[m], hi[m], at[m], heads, ctx)
        parts.append(jnp.einsum("ct,nc->tn", d_qkv, w_mine, preferred_element_type=f32).astype(bf16).reshape(ctx, rows, width))
        grad_qkv = grad_qkv + jnp.einsum("tw,ct->wc", tokens_all[m], d_qkv, preferred_element_type=f32)
        grad_b = grad_b + jnp.sum(d_qkv.astype(f32), axis=1)

    place = lambda vec: lax.dynamic_update_slice_in_dim(jnp.zeros((width,), f32), vec, me * cols, 0)
    vectors = [place(grad_b[:cols]), place(grad_b[2 * cols :]), grad_bo, grad_g1, grad_s1, grad_b2, grad_g2, grad_s2]
    stacked = jnp.concatenate([v.reshape(1, width) for v in vectors] + [grad_b1.reshape(devices, -1, share).transpose(1, 0, 2).reshape(-1, width)], axis=0)
    stacked = jnp.pad(stacked.T, ((0, 0), (0, spare - lines)))
    by_head = jnp.concatenate([grad_qkv, stacked], axis=1).astype(bf16).reshape(devices, share, 3 * cols + spare)
    by_head = jnp.pad(by_head, ((0, 0), (0, ext - share), (0, 0)))
    gq, gk, gv, both, summed = fold(by_head, parts, cols)
    token_grad = d_res1.reshape(summed.shape) + summed
    gq, gk, gv = gq[:share], gk[:share], gv[:share]
    both = both[:share, :lines].T
    gbq, gbv, gbo, gg1, gs1, gb2, gg2, gs2 = [both[n] for n in range(8)]
    gb1 = both[8:].reshape(-1)
    grads = grads.astype(f32)
    gwo, gw2 = grads[:share], grads[share : share + share * wide]
    gw1 = jnp.concatenate([grads[share * (1 + wide + n) : share * (2 + wide + n)] for n in range(wide)], axis=1)
    four = (micro, 1, rows, width)
    return (
        layer_output.reshape(four), token_grad.reshape(four), gq, gbq, gk, gv, gbv, gwo, gbo, gg1, gs1,
        gw1, gb1, gw2, gb2, gg2, gs2,
    )


def solution(mesh):
    rows = P(("ctx", "fsdp"), None)
    flat = P(("ctx", "fsdp"))
    tokens = P(None, "fsdp", "ctx", None)
    params = (rows, flat, rows, rows, flat, rows, flat, flat, flat, rows, flat, rows, flat, flat, flat)
    return jax.shard_map(
        body,
        mesh=mesh,
        in_specs=(tokens, P(None, "fsdp", None), P(None, "fsdp")) + params + (tokens,),
        out_specs=(tokens, tokens) + params,
        check_vma=False,
    )
```

```python
import functools
import math

import jax
import jax.numpy as jnp
from jax import lax
from jax.experimental import pallas as pl
from jax.experimental.pallas import tpu as pltpu
from jax.sharding import PartitionSpec as P

HD = 64
KEY_BLOCK = 128
TILE = 256
SEG_COUNT = 32
FAR = 1e30

def mask_rows(seg_row, reach, first_block):
    n = seg_row.shape[1]
    row = lax.broadcasted_iota(jnp.int32, (HD, n), 0)
    seg = jnp.broadcast_to(seg_row, (HD, n))
    block = lax.broadcasted_iota(jnp.int32, (HD, n), 1) // KEY_BLOCK + first_block
    is_seg = row < SEG_COUNT
    key_at = row - SEG_COUNT
    far = jnp.logical_not(is_seg) & (jnp.abs(key_at - block) >= reach)
    q_side = jnp.where((is_seg & (seg == row)) | far, -FAR, 0.0)
    k_side = jnp.where((is_seg & (seg != row)) | (key_at == block), 1.0, 0.0)
    return q_side.astype(jnp.bfloat16), k_side.astype(jnp.bfloat16)


def token_block(me, s, count, rows):
    return pl.ds(pl.multiple_of(lax.rem(me + s, count) * rows, rows), rows)


def fwd_kernel(heads, count, lo_ref, hi_ref, at_ref, seg_ref, qkv_ref, *refs):
    att_refs, lse_ref, (kaug, qaug, vtr, att, held_s, held_p) = refs[:count], refs[count], refs[count + 1 :]
    reach, me = at_ref[0], at_ref[1]
    length = qkv_ref.shape[1]
    rows, width = length // count, heads * HD

    def prepare(s, _):
        here = pl.ds(pl.multiple_of(s * rows, rows), rows)
        there = token_block(me, s, count, rows)
        q_side, k_side = mask_rows(seg_ref[:, there], reach, lax.rem(me + s, count) * (rows // KEY_BLOCK))
        for h in range(heads):
            q = qkv_ref[h * HD : (h + 1) * HD, here]
            k = qkv_ref[width + h * HD : width + (h + 1) * HD, here]
            qaug[h, 0:HD, there] = (q.astype(jnp.float32) * (1.0 / math.sqrt(HD))).astype(jnp.bfloat16)
            qaug[h, HD : 2 * HD, there] = q_side
            kaug[h, there, :] = jnp.transpose(jnp.concatenate([k, k_side], axis=0))
            vtr[h, :, there] = qkv_ref[2 * width + h * HD : 2 * width + (h + 1) * HD, here]
        return 0
    lax.fori_loop(0, count, prepare, 0)

    def tile(n):
        return pl.ds(pl.multiple_of(n * TILE, TILE), TILE)

    tiles = length // TILE
    for h in range(heads):
        held_s[h] = jnp.dot(kaug[h, tile(lo_ref[0]), :], qaug[h, :, tile(0)], preferred_element_type=jnp.float32)

    def q_step(i, _):
        qs = tile(i)
        first, end = lo_ref[i], hi_ref[i]
        later = jnp.minimum(i + 1, tiles - 1)

        def k_step(j, carry):
            ks, last = tile(j), j + 1 == end
            after, after_q = tile(jnp.where(last, lo_ref[later], j + 1)), tile(jnp.where(last, later, i))
            out, kept = [], None
            def values(h, peak, total, fade, acc, p):
                out.append((peak, total, fade, acc * fade + jnp.dot(vtr[h, :, ks], p, preferred_element_type=jnp.float32)))
            for h in range(heads):
                peak, total, _, acc = carry[h]
                s = held_s[h]
                new = jnp.maximum(peak, jnp.max(s, axis=0, keepdims=True))
                p = jnp.exp(s - new)
                fade = jnp.exp(peak - new)
                total = total * fade + jnp.sum(p, axis=0, keepdims=True)
                held_s[h] = jnp.dot(kaug[h, after, :], qaug[h, :, after_q], preferred_element_type=jnp.float32)
                if h:
                    values(*kept)
                kept = (h, new, total, fade, acc, p.astype(jnp.bfloat16))
            values(*kept)
            return tuple(out)
        row = lambda value: jnp.full((1, TILE), value, jnp.float32)
        start = tuple((row(-3e38), row(0.0), row(0.0), jnp.zeros((HD, TILE), jnp.float32)) for _ in range(heads))
        done = lax.fori_loop(first, end, k_step, start)
        for h in range(heads):
            peak, total, fade, acc = done[h]
            att[h * HD : (h + 1) * HD, qs] = (acc / total).astype(jnp.bfloat16)
            lse_ref[h : h + 1, qs] = peak + jnp.log(total)
        return 0
    lax.fori_loop(0, tiles, q_step, 0)
    for s in range(count):
        att_refs[s][...] = att[:, token_block(me, s, count, rows)]


def attend(qkv, seg, lo, hi, at, heads, count):
    cols, length = qkv.shape
    width, rows = heads * HD, length // count
    whole = lambda shape: pl.BlockSpec(shape, lambda n, *_: (0, 0))
    return pl.pallas_call(
        functools.partial(fwd_kernel, heads, count),
        out_shape=[jax.ShapeDtypeStruct((width, rows), jnp.bfloat16)] * count + [jax.ShapeDtypeStruct((8, length), jnp.float32)],
        grid_spec=pltpu.PrefetchScalarGridSpec(
            num_scalar_prefetch=3, grid=(1,),
            in_specs=[whole((1, length)), whole((cols, length))],
            out_specs=[whole((width, rows))] * count + [whole((8, length))],
            scratch_shapes=[pltpu.VMEM((heads, length, 2 * HD), jnp.bfloat16), pltpu.VMEM((heads, 2 * HD, length), jnp.bfloat16),
                            pltpu.VMEM((heads, HD, length), jnp.bfloat16), pltpu.VMEM((width, length), jnp.bfloat16),
                            pltpu.VMEM((heads, TILE, TILE), jnp.float32), pltpu.VMEM((heads, TILE, TILE), jnp.bfloat16)]),
        compiler_params=pltpu.CompilerParams(dimension_semantics=("arbitrary",), vmem_limit_bytes=40 << 20),
        cost_estimate=pl.CostEstimate(flops=30_000_000_000, bytes_accessed=4_000_000, transcendentals=0),
        name="attend",
    )(lo, hi, at, seg, qkv)


def bwd_kernel(heads, count, lo_ref, hi_ref, at_ref, seg_ref, qkv_ref, lse_ref, *refs):
    att_refs, datt_refs, dqkv_ref = refs[:count], refs[count : 2 * count], refs[2 * count]
    kaug, qaug, v_nat, dotr, ktr, delta, dqt, dkt, dvt, held_s = refs[2 * count + 1 :]
    reach, me = at_ref[0], at_ref[1]
    length = qkv_ref.shape[1]
    rows, width = length // count, heads * HD
    tiles = length // TILE
    scale = 1.0 / math.sqrt(HD)
    f32, bf16 = jnp.float32, jnp.bfloat16
    for s in range(count):
        there = token_block(me, s, count, rows)
        for h in range(heads):
            do, o = datt_refs[s][h * HD : (h + 1) * HD, :], att_refs[s][h * HD : (h + 1) * HD, :]
            dotr[h, :, there] = do
            delta[h, :, there] = jnp.sum(do.astype(f32) * o.astype(f32), axis=0, keepdims=True)

    def prepare(s, _):
        here = pl.ds(pl.multiple_of(s * rows, rows), rows)
        there = token_block(me, s, count, rows)
        q_side, k_side = mask_rows(seg_ref[:, there], reach, lax.rem(me + s, count) * (rows // KEY_BLOCK))
        for h in range(heads):
            q = qkv_ref[h * HD : (h + 1) * HD, here]
            k = qkv_ref[width + h * HD : width + (h + 1) * HD, here]
            qaug[h, 0:HD, there] = (q.astype(f32) * scale).astype(bf16)
            qaug[h, HD : 2 * HD, there] = q_side
            kaug[h, there, :] = jnp.transpose(jnp.concatenate([k, k_side], axis=0))
            ktr[h, :, there] = k
            v_nat[h, there, :] = jnp.transpose(qkv_ref[2 * width + h * HD : 2 * width + (h + 1) * HD, here])
            dqt[h, :, there] = jnp.zeros((HD, rows), f32)
        return 0
    lax.fori_loop(0, count, prepare, 0)

    def tile(n):
        return pl.ds(pl.multiple_of(n * TILE, TILE), TILE)

    def over_queries(left, right):
        return lax.dot_general(left, right, (((1,), (1,)), ((), ())), preferred_element_type=f32)

    for h in range(heads):
        held_s[h] = jnp.dot(kaug[h, tile(0), :], qaug[h, :, tile(lo_ref[0])], preferred_element_type=f32)

    def k_step(j, _):
        ks = tile(j)
        first, end = lo_ref[j], hi_ref[j]
        later = jnp.minimum(j + 1, tiles - 1)
        dkt[...] = jnp.zeros_like(dkt)
        dvt[...] = jnp.zeros_like(dvt)

        def q_step(i, _):
            qs, last = tile(i), i + 1 == end
            after, after_k = tile(jnp.where(last, lo_ref[later], i + 1)), tile(jnp.where(last, later, j))
            def terms(h, p, ds):
                dvt[h] += over_queries(dotr[h, :, qs], p)
                dkt[h] += over_queries(qaug[h, 0:HD, qs], ds)
                dqt[h, :, qs] += jnp.dot(ktr[h, :, ks], ds, preferred_element_type=f32)

            def to_probs(h):
                return jnp.dot(v_nat[h, ks, :], dotr[h, :, qs], preferred_element_type=f32)
            dp, kept = to_probs(0), None
            for h in range(heads):
                ahead = to_probs(h + 1) if h + 1 < heads else None
                p = jnp.exp(held_s[h] - lse_ref[h : h + 1, qs])
                ds = (p * (dp - delta[h, :, qs])).astype(bf16)
                held_s[h] = jnp.dot(kaug[h, after_k, :], qaug[h, :, after], preferred_element_type=f32)
                if h:
                    terms(h - 1, *kept)
                kept, dp = (p.astype(bf16), ds), ahead
            terms(heads - 1, *kept)
            return 0
        lax.fori_loop(first, end, q_step, 0)
        slot = lax.rem(j // (rows // TILE) + count - me, count)
        out = pl.ds(pl.multiple_of(slot * rows + lax.rem(j, rows // TILE) * TILE, TILE), TILE)
        for h in range(heads):
            dqkv_ref[width + h * HD : width + (h + 1) * HD, out] = dkt[h].astype(bf16)
            dqkv_ref[2 * width + h * HD : 2 * width + (h + 1) * HD, out] = dvt[h].astype(bf16)
        return 0
    lax.fori_loop(0, tiles, k_step, 0)

    def finish(s, _):
        here = pl.ds(pl.multiple_of(s * rows, rows), rows)
        there = token_block(me, s, count, rows)
        for h in range(heads):
            dqkv_ref[h * HD : (h + 1) * HD, here] = (dqt[h, :, there] * scale).astype(bf16)
        return 0
    lax.fori_loop(0, count, finish, 0)


def attend_back(qkv, att, datt, lse, seg, lo, hi, at, heads, count):
    cols, length = qkv.shape
    width, rows = heads * HD, length // count
    whole = lambda shape: pl.BlockSpec(shape, lambda n, *_: (0, 0))
    return pl.pallas_call(
        functools.partial(bwd_kernel, heads, count),
        out_shape=jax.ShapeDtypeStruct((cols, length), jnp.bfloat16),
        grid_spec=pltpu.PrefetchScalarGridSpec(
            num_scalar_prefetch=3, grid=(1,),
            in_specs=[whole((1, length)), whole((cols, length)), whole((8, length))] + [whole((width, rows))] * (2 * count),
            out_specs=whole((cols, length)),
            scratch_shapes=[
                pltpu.VMEM((heads, length, 2 * HD), jnp.bfloat16),
                pltpu.VMEM((heads, 2 * HD, length), jnp.bfloat16),
                pltpu.VMEM((heads, length, HD), jnp.bfloat16),
                pltpu.VMEM((heads, HD, length), jnp.bfloat16),
                pltpu.VMEM((heads, HD, length), jnp.bfloat16),
                pltpu.VMEM((heads, 1, length), jnp.float32),
                pltpu.VMEM((heads, HD, length), jnp.float32),
                pltpu.VMEM((heads, HD, TILE), jnp.float32),
                pltpu.VMEM((heads, HD, TILE), jnp.float32),
                pltpu.VMEM((heads, TILE, TILE), jnp.float32)]),
        compiler_params=pltpu.CompilerParams(dimension_semantics=("arbitrary",), vmem_limit_bytes=48 << 20),
        cost_estimate=pl.CostEstimate(flops=30_000_000_000, bytes_accessed=6_000_000, transcendentals=0),
        name="attend_back",
    )(lo, hi, at, seg, qkv, lse, *att, *datt)


def bounds(segments, reach):
    first = segments[:, ::TILE]
    last = segments[:, TILE - 1::TILE]
    n = first.shape[1]
    at = jnp.arange(n)
    per = TILE // KEY_BLOCK
    gap = per * jnp.abs(at[:, None] - at[None, :]) - (per - 1)
    near = gap[None] < reach[:, None, None]
    before = (at[None, :] < at[:, None])[None] & near & (first[:, :, None] == last[:, None, :])
    after = (at[None, :] > at[:, None])[None] & near & (last[:, :, None] == first[:, None, :])
    lo = at[None] - jnp.sum(before, axis=2, dtype=jnp.int32)
    hi = at[None] + 1 + jnp.sum(after, axis=2, dtype=jnp.int32)
    return lo.astype(jnp.int32), hi.astype(jnp.int32)


MESH = pl.DeviceIdType.MESH


def greet(peers):
    barrier = pltpu.get_barrier_semaphore()
    for peer in peers:
        pl.semaphore_signal(barrier, inc=1, device_id=peer, device_id_type=MESH)
    pl.semaphore_wait(barrier, len(peers))


def add_low(left, right):
    return (left.astype(jnp.float32) + right.astype(jnp.float32)).astype(jnp.bfloat16)


class Sends:
    def __init__(self, send_sem, recv_sem):
        self.send_sem, self.recv_sem, self.used, self.open = send_sem, recv_sem, 0, []

    def start(self, src, dst, peer):
        n = self.used
        self.used += 1
        copy = pltpu.make_async_remote_copy(
            src_ref=src, dst_ref=dst, send_sem=self.send_sem.at[n], recv_sem=self.recv_sem.at[n],
            device_id=peer, device_id_type=MESH)
        copy.start()
        self.open.append(copy)
        return copy

    def finish(self):
        for copy in self.open:
            copy.wait_send()


def fold_kernel(zs, micro, heads_in, *refs):
    tokens_in, groups_out, rest_out, tokens_out = refs[:micro], refs[micro : micro + 3], refs[micro + 3], refs[micro + 4]
    h_own, h_y, h_z, h_c, t_own, t_c, t_x, send_sem, recv_sem, load_sem = refs[micro + 5 :]
    c, f = lax.axis_index("ctx"), lax.axis_index("fsdp")
    x, core, z, y = c // 2, c % 2, f // 2, f % 2
    partner = {"ctx": x * 2 + (1 - core), "fsdp": f}
    beside = {"ctx": (1 - x) * 2 + core, "fsdp": f}
    above = {"ctx": c, "fsdp": z * 2 + (1 - y)}
    far = [{"ctx": c, "fsdp": lax.rem(z + s, zs) * 2 + y} for s in range(1, zs)]
    across = [{"ctx": lax.rem(c + s, 4), "fsdp": f} for s in range(1, 4)]
    sends = Sends(send_sem, recv_sem)
    greet([above] + far + across)

    near = 1 + 2 * core
    other = 3 - 2 * core
    loads = []
    def load(src, dst):
        loads.append(pltpu.make_async_copy(src, dst, load_sem.at[len(loads)]))
        loads[-1].start()
        return loads[-1]
    load_there, copy_there, load_here, copy_here = [], [], [], []
    for m in range(micro):
        copy_there.append(sends.start(tokens_in[m].at[other], t_c.at[m, 1], partner))
        load_there.append(load(tokens_in[m].at[2], t_own.at[m, 1]))
    copy_h = sends.start(heads_in.at[:, :, 1 - y], h_y, above)
    load_h = load(heads_in.at[:, :, y], h_own)
    for m in range(micro):
        copy_here.append(sends.start(tokens_in[m].at[near], t_c.at[m, 0], partner))
        load_here.append(load(tokens_in[m].at[0], t_own.at[m, 0]))

    chunks = t_own.shape[2] // 64
    def sum_t(m, place):
        def step(i, _):
            rows = pl.ds(pl.multiple_of(i * 64, 64), 64)
            t_c[m, place, rows, :] = add_low(t_own[m, place, rows, :], t_c[m, place, rows, :])
            return 0
        lax.fori_loop(0, chunks, step, 0)
    copy_tx = []
    for m in range(micro):
        load_there[m].wait(), copy_there[m].wait_recv()
        sum_t(m, 1)
        copy_tx.append(sends.start(t_c.at[m, 1], t_x.at[m], beside))

    load_h.wait(), copy_h.wait_recv()
    def sum_h(i, _):
        a, b = i // zs, lax.rem(i, zs)
        h_y[a, b] = add_low(h_own[a, b], h_y[a, b])
        return 0
    lax.fori_loop(0, 4 * zs, sum_h, 0)
    copy_hz = [sends.start(h_y.at[:, lax.rem(z + s, zs)], h_z.at[s - 1], far[s - 1]) for s in range(1, zs)]
    for m in range(micro):
        load_here[m].wait(), copy_here[m].wait_recv()
        sum_t(m, 0)
    for copy in copy_hz:
        copy.wait_recv()
    def total_h(a, _):
        total = h_y[a, z].astype(jnp.float32)
        for s in range(1, zs):
            total = total + h_z[s - 1, a].astype(jnp.float32)
        h_own[a, 0] = total.astype(jnp.bfloat16)
        return 0
    lax.fori_loop(0, 4, total_h, 0)
    copy_hc = [sends.start(h_own.at[lax.rem(c + s, 4), 0], h_c.at[c], across[s - 1]) for s in range(1, 4)]
    for m in range(micro):
        copy_tx[m].wait_recv()
        def last_t(i, _, m=m):
            rows = pl.ds(pl.multiple_of(i * 64, 64), 64)
            tokens_out[m, rows, :] = t_c[m, 0, rows, :].astype(jnp.float32) + t_x[m, rows, :].astype(jnp.float32)
            return 0
        lax.fori_loop(0, chunks, last_t, 0)
    h_c[c] = h_own[c, 0]
    for copy in copy_hc:
        copy.wait_recv()
    cols = groups_out[0].shape[1] // 4
    rest = 0.0
    for a in range(4):
        term = h_c[a].astype(jnp.float32)
        for n in range(3):
            groups_out[n][:, a * cols : (a + 1) * cols] = term[:, n * cols : (n + 1) * cols]
        rest = rest + term[:, 3 * cols :]
    rest_out[...] = rest
    sends.finish()


def fold(by_head, tokens, cols):
    ctx, fsdp = lax.axis_size("ctx"), lax.axis_size("fsdp")
    zs = fsdp // 2
    assert ctx == 4 and fsdp % 2 == 0
    f32, bf16 = jnp.float32, jnp.bfloat16
    hr, hw = by_head.shape[1:]
    micro = len(tokens)
    _, tr, tw = tokens[0].shape
    copies = 3 * micro + 1 + (zs - 1) + 3
    anywhere, vmem = pl.BlockSpec(memory_space=pl.ANY), pl.BlockSpec(memory_space=pltpu.VMEM)
    return pl.pallas_call(
        functools.partial(fold_kernel, zs, micro),
        out_shape=[jax.ShapeDtypeStruct((hr, 4 * cols), f32)] * 3 + [jax.ShapeDtypeStruct((hr, hw - 3 * cols), f32), jax.ShapeDtypeStruct((micro, tr, tw), f32)],
        in_specs=[anywhere] * (1 + micro), out_specs=[vmem] * 5,
        scratch_shapes=[
            pltpu.VMEM((4, zs, hr, hw), bf16), pltpu.VMEM((4, zs, hr, hw), bf16), pltpu.VMEM((zs - 1, 4, hr, hw), bf16), pltpu.VMEM((4, hr, hw), bf16),
            pltpu.VMEM((micro, 2, tr, tw), bf16), pltpu.VMEM((micro, 2, tr, tw), bf16), pltpu.VMEM((micro, tr, tw), bf16),
            pltpu.SemaphoreType.DMA((copies,)), pltpu.SemaphoreType.DMA((copies,)), pltpu.SemaphoreType.DMA((1 + 2 * micro,))],
        compiler_params=pltpu.CompilerParams(collective_id=1, has_side_effects=True, vmem_limit_bytes=63 << 20),
        name="fold",
    )(by_head.reshape(4, zs, 2, hr, hw), *tokens)


def collect_kernel(zs, micro, mine, tokens, mine_out, *refs):
    tokens_out, (held_mine, held, send_sem, recv_sem, load_sem) = refs[:micro], refs[micro:]
    c, f = lax.axis_index("ctx"), lax.axis_index("fsdp")
    x, core, z, y = c // 2, c % 2, f // 2, f % 2
    partner = {"ctx": x * 2 + (1 - core), "fsdp": f}
    beside = {"ctx": (1 - x) * 2 + core, "fsdp": f}
    above = {"ctx": c, "fsdp": z * 2 + (1 - y)}
    far = [{"ctx": c, "fsdp": lax.rem(z + s, zs) * 2 + y} for s in range(1, zs)]
    across = [{"ctx": lax.rem(c + s, 4), "fsdp": f} for s in range(1, 4)]
    greet([above] + far + across)
    sends = Sends(send_sem, recv_sem)
    loads = [pltpu.make_async_copy(mine.at[c], held_mine, load_sem.at[0]), pltpu.make_async_copy(tokens, held, load_sem.at[1])]
    for copy in loads:
        copy.start()
    first = [sends.start(mine.at[lax.rem(c + s, 4)], mine_out.at[c, z, y], across[s - 1]) for s in range(1, 4)]
    over_x = [sends.start(tokens.at[m], tokens_out[m].at[2], beside) for m in range(micro)]
    over_core = [sends.start(tokens.at[m], tokens_out[m].at[3 - 2 * core], partner) for m in range(micro)]
    loads[0].wait()
    stores = [pltpu.make_async_copy(held_mine, mine_out.at[c, z, y], load_sem.at[2])]
    stores[0].start()
    loads[1].wait()
    for m in range(micro):
        stores.append(pltpu.make_async_copy(held.at[m], tokens_out[m].at[0], load_sem.at[3 + m]))
        stores[-1].start()
    for copy in first:
        copy.wait_recv()
    stores[0].wait()
    over_y = sends.start(mine_out.at[:, z, y], mine_out.at[:, z, y], above)
    own_far = [sends.start(mine_out.at[:, z, y], mine_out.at[:, z, y], peer) for peer in far]
    up_down = []
    for s in range(1, zs):
        own_far[s - 1].wait_recv()
        there = lax.rem(z + zs - s, zs)
        up_down.append(sends.start(mine_out.at[:, there, y], mine_out.at[:, there, y], above))
    relay = []
    for m in range(micro):
        over_x[m].wait_recv()
        relay.append(sends.start(tokens_out[m].at[2], tokens_out[m].at[1 + 2 * core], partner))
    for copy in [over_y] + over_core + up_down + relay:
        copy.wait_recv()
    for copy in stores[1:]:
        copy.wait()
    sends.finish()


def collect(mine, tokens):
    ctx, fsdp = lax.axis_size("ctx"), lax.axis_size("fsdp")
    zs = fsdp // 2
    assert ctx == 4 and fsdp % 2 == 0
    micro = tokens.shape[0]
    copies = 3 + 1 + 2 * (zs - 1) + 3 * micro
    anywhere = pl.BlockSpec(memory_space=pl.ANY)
    return pl.pallas_call(
        functools.partial(collect_kernel, zs, micro),
        out_shape=[jax.ShapeDtypeStruct((4, zs, 2) + mine.shape[1:], mine.dtype)] + [jax.ShapeDtypeStruct((4,) + tokens.shape[1:], tokens.dtype)] * micro,
        in_specs=[anywhere] * 2, out_specs=[anywhere] * (1 + micro),
        scratch_shapes=[pltpu.VMEM(mine.shape[1:], mine.dtype), pltpu.VMEM(tokens.shape, tokens.dtype), pltpu.SemaphoreType.DMA((copies,)), pltpu.SemaphoreType.DMA((copies,)), pltpu.SemaphoreType.DMA((3 + micro,))],
        compiler_params=pltpu.CompilerParams(collective_id=0, has_side_effects=True),
        name="collect",
    )(mine, tokens)


def layer_norm(summed, gain, shift):
    row_mean = jnp.mean(summed, axis=-1, keepdims=True)
    centered = summed - row_mean
    variance = jnp.mean(centered * centered, axis=-1, keepdims=True)
    recip = lax.rsqrt(variance + 1e-05)
    normed = centered * recip
    return (normed * gain + shift, normed, recip)


def norm_back(upstream, normed, recip, gain):
    scaled = upstream * gain
    first_mean = jnp.mean(scaled, axis=-1, keepdims=True)
    second_mean = jnp.mean(scaled * normed, axis=-1, keepdims=True)
    d_summed = recip * (scaled - first_mean - normed * second_mean)
    return (d_summed, jnp.sum(upstream * normed, axis=0), jnp.sum(upstream, axis=0))


def dot(left, right):
    return jnp.dot(left, right, preferred_element_type=jnp.float32)


def weight_term(left, right):
    return jnp.einsum("ta,tb->ab", left, right, preferred_element_type=jnp.float32)


def back_term(grad_low, weight):
    return jnp.einsum("tb,ab->ta", grad_low, weight, preferred_element_type=jnp.float32)


def column_sum(grad_low):
    return jnp.sum(grad_low.astype(jnp.float32), axis=0)


def shift(piece, step):
    count = lax.axis_size("ctx")
    return lax.ppermute(piece, "ctx", [(a, (a + step) % count) for a in range(count)])


def body(
    inputs, segments, block_reach,
    query_weight, query_bias, key_weight, value_weight, value_bias, output_weight, output_bias,
    first_gain, first_shift, expand_weight, expand_bias, contract_weight, contract_bias,
    second_gain, second_shift, output_grad,
):
    every = ("ctx", "fsdp")
    ctx = lax.axis_size("ctx")
    me = lax.axis_index("ctx")
    micro, _, rows, width = inputs.shape
    length = rows * ctx
    cols = width // ctx
    heads = cols // HD
    f32, bf16 = jnp.float32, jnp.bfloat16

    share = query_bias.shape[0]
    lines = 8 + expand_bias.shape[0] // share
    ext = -(-share // 8) * 8
    spare = -(-(3 * cols + lines) // 128) * 128 - 3 * cols
    small = jnp.concatenate([v.reshape(-1, share) for v in (
        query_bias, value_bias, output_bias, first_gain, first_shift, contract_bias, second_gain, second_shift, expand_bias)], axis=0)
    small = jnp.pad(small.T, ((0, 0), (0, spare - lines)))
    split = [jnp.stack([w[:, n * cols : (n + 1) * cols] for n in range(ctx)]) for w in (query_weight, key_weight, value_weight)]
    mine = jnp.concatenate(split + [jnp.broadcast_to(small, (ctx,) + small.shape)], axis=2)
    mine = jnp.pad(mine, ((0, 0), (0, ext - share), (0, 0)))

    wide = expand_weight.shape[1] // width
    packed = jnp.concatenate([output_weight, contract_weight, expand_weight.reshape(share, wide, width).transpose(1, 0, 2).reshape(-1, width)], axis=0)
    packed = lax.all_gather(packed, every, axis=0, tiled=True)

    mine_all, *tokens_all = collect(mine, inputs[:, 0])
    tokens_all = [t.reshape(length, width) for t in tokens_all]
    mine_all = mine_all.reshape(-1, ext, 3 * cols + spare)
    devices = mine_all.shape[0]
    w_mine = mine_all[:, :share, : 3 * cols].reshape(width, 3 * cols)
    small_all = mine_all[:, :share, 3 * cols : 3 * cols + lines].astype(f32).reshape(width, lines).T
    b_query, b_value, b_output, g_first, s_first, b_contract, g_second, s_second = [small_all[n] for n in range(8)]
    b_expand = small_all[8:].reshape(-1, devices, share).transpose(1, 0, 2).reshape(-1)

    packed = packed.reshape(devices, -1, width)
    back = [lax.rem(me + ctx - s, ctx) for s in range(ctx)]
    by_owner = packed[:, :share].reshape(ctx, cols, width)
    w_output = jnp.concatenate([lax.dynamic_index_in_dim(by_owner, back[s], 0, keepdims=False) for s in range(ctx)], axis=0)
    w_contract = packed[:, share : share + share * wide].reshape(-1, width)
    w_expand = packed[:, share + share * wide :].reshape(devices, wide, share, width).transpose(0, 2, 1, 3).reshape(width, -1)

    own = lambda vec: lax.dynamic_slice_in_dim(vec, me * cols, cols, 0)
    b_mine = jnp.concatenate([own(b_query), jnp.zeros((cols,), f32), own(b_value)])
    seg = segments[:, 0]
    reach = block_reach[:, 0]
    lo, hi = bounds(seg, reach)
    at = [jnp.stack([reach[m], me]) for m in range(micro)]

    qkv, att, lse, attended = [], [], [], []
    for m in range(micro):
        flat = tokens_all[m]
        if m:
            flat, _ = lax.optimization_barrier((flat, lse[-1]))
        projected = jnp.einsum("wc,tw->ct", w_mine, flat, preferred_element_type=f32)
        qkv.append((projected + b_mine[:, None]).astype(bf16))
        *pieces, logs = attend(qkv[m], seg[m : m + 1], lo[m], hi[m], at[m], heads, ctx)
        att.append(pieces), lse.append(logs)
        attended.append(jnp.concatenate([pieces[0]] + [shift(pieces[s], s) for s in range(1, ctx)], axis=0))
    attended = jnp.concatenate(attended, axis=1)

    tokens = inputs[:, 0].reshape(micro * rows, width)
    branch = jnp.einsum("ct,cn->tn", attended, w_output, preferred_element_type=f32) + b_output
    hidden, normed_first, recip_first = layer_norm(tokens.astype(f32) + branch, g_first, s_first)
    hidden_low = hidden.astype(bf16)
    pre = dot(hidden_low, w_expand) + b_expand
    phi = 0.5 * (1.0 + lax.erf(pre * (1.0 / math.sqrt(2.0))))
    act_low = (pre * phi).astype(bf16)
    slope = (phi + pre * (jnp.exp(-0.5 * pre * pre) * (1.0 / math.sqrt(2.0 * math.pi)))).astype(bf16)
    act_low, slope = lax.optimization_barrier((act_low, slope))
    second_sum = hidden + dot(act_low, w_contract) + b_contract
    result, normed_second, recip_second = layer_norm(second_sum, g_second, s_second)
    layer_output = result.astype(bf16)
    upstream = output_grad[:, 0].reshape(micro * rows, width).astype(f32)
    d_res2, grad_g2, grad_s2 = norm_back(upstream, normed_second, recip_second, g_second)
    d_ffn = d_res2.astype(bf16)
    grad_b2 = column_sum(d_ffn)
    d_pre = (back_term(d_ffn, w_contract) * slope.astype(f32)).astype(bf16)
    grad_b1 = column_sum(d_pre)
    d_hidden = d_res2 + back_term(d_pre, w_expand)
    d_res1, grad_g1, grad_s1 = norm_back(d_hidden, normed_first, recip_first, g_first)
    d_branch = d_res1.astype(bf16)
    grad_bo = column_sum(d_branch)
    d_attended = [
        jnp.einsum("cn,tn->ct", w_output, d_branch[m * rows : (m + 1) * rows], preferred_element_type=f32).astype(bf16).reshape(ctx, cols, rows)
        for m in range(micro)]

    d_att = [[d_attended[m][0]] + [shift(d_attended[m][s], -s) for s in range(1, ctx)] for m in range(micro)]
    grad_w2 = weight_term(act_low, d_ffn).astype(bf16).reshape(devices, -1, width)
    grad_w1 = [weight_term(hidden_low, d_pre[:, n * width : (n + 1) * width]).astype(bf16).reshape(devices, share, width) for n in range(wide)]
    grad_wo = dot(attended, d_branch).astype(bf16).reshape(ctx, cols, width)
    grad_wo = jnp.concatenate([lax.dynamic_index_in_dim(grad_wo, back[b], 0, keepdims=False) for b in range(ctx)], axis=0).reshape(devices, share, width)
    grads = jnp.concatenate([grad_wo, grad_w2] + grad_w1, axis=1).reshape(-1, width)
    grads = lax.psum_scatter(grads, every, scatter_dimension=0, tiled=True)

    parts, grad_qkv, grad_b = [], 0.0, 0.0
    for m in range(micro):
        d_qkv = attend_back(qkv[m], att[m], d_att[m], lse[m], seg[m : m + 1], lo[m], hi[m], at[m], heads, ctx)
        parts.append(jnp.einsum("ct,nc->tn", d_qkv, w_mine, preferred_element_type=f32).astype(bf16).reshape(ctx, rows, width))
        grad_qkv = grad_qkv + jnp.einsum("tw,ct->wc", tokens_all[m], d_qkv, preferred_element_type=f32)
        grad_b = grad_b + jnp.sum(d_qkv.astype(f32), axis=1)

    place = lambda vec: lax.dynamic_update_slice_in_dim(jnp.zeros((width,), f32), vec, me * cols, 0)
    vectors = [place(grad_b[:cols]), place(grad_b[2 * cols :]), grad_bo, grad_g1, grad_s1, grad_b2, grad_g2, grad_s2]
    stacked = jnp.concatenate([v.reshape(1, width) for v in vectors] + [grad_b1.reshape(devices, -1, share).transpose(1, 0, 2).reshape(-1, width)], axis=0)
    stacked = jnp.pad(stacked.T, ((0, 0), (0, spare - lines)))
    by_head = jnp.concatenate([grad_qkv, stacked], axis=1).astype(bf16).reshape(devices, share, 3 * cols + spare)
    by_head = jnp.pad(by_head, ((0, 0), (0, ext - share), (0, 0)))
    gq, gk, gv, both, summed = fold(by_head, parts, cols)
    token_grad = d_res1.reshape(summed.shape) + summed
    gq, gk, gv = gq[:share], gk[:share], gv[:share]
    both = both[:share, :lines].T
    gbq, gbv, gbo, gg1, gs1, gb2, gg2, gs2 = [both[n] for n in range(8)]
    gb1 = both[8:].reshape(-1)
    grads = grads.astype(f32)
    gwo, gw2 = grads[:share], grads[share : share + share * wide]
    gw1 = jnp.concatenate([grads[share * (1 + wide + n) : share * (2 + wide + n)] for n in range(wide)], axis=1)
    four = (micro, 1, rows, width)
    return (
        layer_output.reshape(four), token_grad.reshape(four), gq, gbq, gk, gv, gbv, gwo, gbo, gg1, gs1,
        gw1, gb1, gw2, gb2, gg2, gs2,
    )


def solution(mesh):
    rows = P(("ctx", "fsdp"), None)
    flat = P(("ctx", "fsdp"))
    tokens = P(None, "fsdp", "ctx", None)
    params = (rows, flat, rows, rows, flat, rows, flat, flat, flat, rows, flat, rows, flat, flat, flat)
    return jax.shard_map(
        body,
        mesh=mesh,
        in_specs=(tokens, P(None, "fsdp", None), P(None, "fsdp")) + params + (tokens,),
        out_specs=(tokens, tokens) + params,
        check_vma=False,
    )
```
